32 devices in a mesh: groups: 2 (over y), ctx: 8 (over z, x), head: 2 (over core).
Axes of the slice: x: 2, y: 2, z: 4, core: 2. Of those that a mesh axis runs over, the one named last changes fastest.
Arguments:
- tokens: bfloat16 [6144, 4096], P(('groups', 'ctx'), 'head'), parts along dimension 0, may hold values from -6 to 6
- w_query: bfloat16 [4096, 2048], P('ctx', 'head'), may hold values from -0.09375 to 0.09375
- w_key: bfloat16 [4096, 2048], P('ctx', 'head'), may hold values from -0.09375 to 0.09375
- w_value: bfloat16 [4096, 2048], P('ctx', 'head'), may hold values from -0.09375 to 0.09375
- w_out: bfloat16 [2048, 4096], P('head'), may hold values from -0.125 to 0.125
Outputs:
- layer_out: bfloat16 [6144, 4096], P(('groups', 'ctx'), 'head'), parts along dimension 0
The draws below stay inside these ranges and needn't reach their ends.
There are 2 independent parts, one for each index of `groups`. The reference program is written for one: setup_inputs(seed, part) draws one part's arguments, and reference() takes and returns one part's arrays. A program takes and returns all parts, laid end to end along the dimension named above; an argument that names none is the same for every part. Nothing has to cross between parts.
All inputs are finite; a program needn't handle non-finite values.
Results may differ from the reference program's by a relative error of at most 0.0067.
Values may be sent and summed in bfloat16 or wider, within the bound.
No kernel may reach another device: no remote copies, remote signals or barrier semaphores. Data moves between devices by JAX's collectives and lax.ppermute only.
A program may use at most 128 MiB of HBM per device.

```python
import jax
import jax.numpy as jnp
from jax import lax

D = 4096
HEADS = 16
HDIM = 128
TOK_DEV = 384
TOKENS = 3072
N_CTX = 8


def block_scale(stream_key, shape, split, least, high):
    level = 1.0
    for dim, parts in split:
        draws = jax.random.uniform(jax.random.fold_in(jax.random.fold_in(stream_key, 6), dim), (parts,), jnp.float32, least / len(split), high / len(split))
        level = level * jnp.repeat(jnp.exp(draws), shape[dim] // parts).reshape((-1,) + (1,) * (len(shape) - 1 - dim))
    return level


def normal_values(stream_key, shape, scale, reach, pieces=(), kind=jnp.bfloat16):
    array = jax.random.normal(stream_key, shape, jnp.float32) * scale
    if len(pieces) > 0:
        array = block_scale(stream_key, shape, pieces, -0.22, 0.18) * array
    return jnp.clip(array, min=-reach, max=reach).astype(kind)


def setup_inputs(seed: int = 0, part: int = 0) -> dict:
    seeds = jax.random.split(jax.random.key(seed), 6)
    part_keys = jax.random.split(jax.random.fold_in(seeds[5], part), 6)
    tokens = normal_values(part_keys[0], (TOKENS, D), 1.0, 6.0, ((0, 8), (1, 2)))
    w_query = normal_values(seeds[1], (D, HEADS * HDIM), D ** -0.5, 0.09375, ((0, 8), (1, 2)))
    w_key = normal_values(seeds[2], (D, HEADS * HDIM), D ** -0.5, 0.09375, ((0, 8), (1, 2)))
    w_value = normal_values(seeds[3], (D, HEADS * HDIM), D ** -0.5, 0.09375, ((0, 8), (1, 2)))
    w_out = normal_values(seeds[4], (HEADS * HDIM, D), (HEADS * HDIM) ** -0.5, 0.125, ((0, 2),))
    return dict(tokens=tokens, w_query=w_query, w_key=w_key, w_value=w_value, w_out=w_out)


def reference(tokens, w_query, w_key, w_value, w_out):
    blocks = tokens.reshape(N_CTX, TOK_DEV, D)
    position = lax.broadcasted_iota(jnp.int32, (TOK_DEV, TOK_DEV), 0)
    other = lax.broadcasted_iota(jnp.int32, (TOK_DEV, TOK_DEV), 1)
    causal = other <= position

    def advance(carried, segment):
        query = jax.nn.silu(jnp.dot(segment, w_query, preferred_element_type=jnp.float32)).astype(jnp.bfloat16)
        key_rows = jax.nn.silu(jnp.dot(segment, w_key, preferred_element_type=jnp.float32)).astype(jnp.bfloat16)
        value_rows = jnp.dot(segment, w_value, preferred_element_type=jnp.float32).astype(jnp.bfloat16)
        query = query.astype(jnp.float32).reshape(TOK_DEV, HEADS, HDIM)
        key_rows = key_rows.astype(jnp.float32).reshape(TOK_DEV, HEADS, HDIM)
        value_rows = value_rows.astype(jnp.float32).reshape(TOK_DEV, HEADS, HDIM)
        scores = jnp.einsum('thd,shd->hts', query, key_rows)
        weights = lax.optimization_barrier(jnp.where(causal[None], scores, 0.0).astype(jnp.bfloat16)).astype(jnp.float32)
        earlier_b = lax.optimization_barrier(carried.astype(jnp.bfloat16)).astype(jnp.float32)
        mixed = jnp.einsum('hts,she->the', weights, value_rows) + jnp.einsum('thd,hde->the', query, earlier_b)
        normed = mixed * lax.rsqrt(lax.optimization_barrier(jnp.mean(mixed * mixed, axis=-1, keepdims=True)) + 1e-06)
        normed = normed.astype(jnp.bfloat16).reshape(TOK_DEV, HEADS * HDIM)
        result = jnp.dot(normed, w_out, preferred_element_type=jnp.float32).astype(jnp.bfloat16)
        carried = carried + jnp.einsum('thd,the->hde', key_rows, value_rows)
        return (carried, result)
    _, results = lax.scan(advance, jnp.zeros((HEADS, HDIM, HDIM), jnp.float32), blocks)
    return results.reshape(N_CTX * TOK_DEV, D)
```

```python
import jax
import jax.numpy as jnp
from jax import lax
from jax.sharding import PartitionSpec as P

HDIM = 128
SUB = 4
F32 = jnp.float32
BF16 = jnp.bfloat16


def dot(a, b):
    return jnp.dot(a, b, preferred_element_type=F32)


def exclusive_prefix(value, groups):
    def shift(v, step):
        pairs = [(g * SUB + j, (g + step) * SUB + j) for g in range(groups - step) for j in range(SUB)]
        return lax.ppermute(v, "ctx", pairs)

    if groups == 1:
        return jnp.zeros_like(value)
    total = shift(value, 1)
    step = 1
    while step < groups - 1:
        total = total + shift(total, step)
        step *= 2
    return total


def local(tokens, w_query, w_key, w_value, w_out):
    n_ctx = lax.axis_size("ctx")
    groups = n_ctx // SUB
    rows = tokens.shape[0]
    depth = w_query.shape[0]
    width = 2 * tokens.shape[1]
    ctx = lax.axis_index("ctx")
    block = ctx % SUB
    part = lax.axis_index("groups")
    core = lax.axis_index("head")

    def xor(value, step):
        return lax.ppermute(value, "ctx", [(i, i ^ step) for i in range(n_ctx)])

    def other_part(value):
        return lax.ppermute(value, "groups", [(0, 1), (1, 0)])

    def other_core(value):
        return lax.ppermute(value, "head", [(0, 1), (1, 0)])

    def columns(weight):
        heads = weight.reshape(depth, SUB, 2, HDIM)
        mine = lax.dynamic_index_in_dim(heads, part, 2, keepdims=False)
        return mine.transpose(1, 0, 2)

    def spread(pieces):
        sent = jnp.concatenate([pieces] * groups, axis=0).reshape(n_ctx * depth, -1)
        return lax.all_to_all(sent, "ctx", 0, 0, tiled=True)

    beside = xor(tokens, 1)
    across = xor(tokens, 2)
    kv_mine = spread(jnp.concatenate([columns(w_key), columns(w_value)], axis=2))
    half = tokens.shape[1] // 2
    corner = jnp.concatenate([xor(across[:, :half], 1), xor(beside[:, half:], 2)], axis=1)
    kv_other = other_part(kv_mine)
    q_mine = spread(columns(w_query))
    q_other = other_part(q_mine)

    out_cols = w_out.shape[1] // 2
    out_mine = lax.dynamic_slice_in_dim(w_out, core * out_cols, out_cols, 1)
    out_other = other_core(lax.dynamic_slice_in_dim(w_out, (1 - core) * out_cols, out_cols, 1))

    stream = jnp.zeros((SUB * rows, width), BF16)
    for step, piece in enumerate((tokens, beside, across, corner)):
        whole = lax.all_gather(piece, "head", axis=1, tiled=True)
        stream = lax.dynamic_update_slice(stream, whole, ((block ^ step) * rows, 0))

    position = lax.broadcasted_iota(jnp.int32, (rows, rows), 0)
    other = lax.broadcasted_iota(jnp.int32, (rows, rows), 1)
    causal = other <= position

    def attend(kv, q):
        both = dot(stream, kv)
        key = jax.nn.silu(both[:, :HDIM]).astype(BF16).reshape(SUB, rows, HDIM)
        value = both[:, HDIM:].astype(BF16).reshape(SUB, rows, HDIM)
        own = jnp.einsum("bsd,bse->bde", key, value, preferred_element_type=F32)
        carried = exclusive_prefix(own.sum(0), groups)
        prefixes = [carried]
        for b in range(SUB - 1):
            prefixes.append(prefixes[-1] + own[b])
        earlier = jnp.stack(prefixes).astype(BF16)
        query = jax.nn.silu(dot(stream, q)).astype(BF16).reshape(SUB, rows, HDIM)
        scores = jnp.einsum("btd,bsd->bts", query, key, preferred_element_type=F32)
        weights = jnp.where(causal[None], scores, 0.0).astype(BF16)
        mixed = jnp.einsum("bts,bse->bte", weights, value, preferred_element_type=F32)
        mixed = mixed + jnp.einsum("btd,bde->bte", query, earlier, preferred_element_type=F32)
        return (mixed * lax.rsqrt(jnp.mean(mixed * mixed, axis=-1, keepdims=True) + 1e-06)).astype(BF16)

    mine = attend(kv_mine, q_mine)
    theirs = attend(kv_other, q_other)
    first = jnp.where(part == 0, mine, theirs)
    second = jnp.where(part == 0, theirs, mine)
    normed = jnp.concatenate([first, second], axis=2)

    def block_for(step):
        return lax.dynamic_index_in_dim(normed, block ^ step, 0, keepdims=False)

    full = jnp.zeros((rows, SUB * 2 * HDIM), BF16)
    for step in range(SUB):
        piece = block_for(step)
        if step:
            piece = xor(piece, step)
        full = lax.dynamic_update_slice(full, piece, (0, (block ^ step) * 2 * HDIM))
    return (dot(full, out_mine) + dot(other_core(full), out_other)).astype(BF16)


def solution(mesh):
    in_specs = (
        P(("groups", "ctx"), "head"),
        P("ctx", "head"),
        P("ctx", "head"),
        P("ctx", "head"),
        P("head", None),
    )
    out_specs = P(("groups", "ctx"), "head")
    return jax.shard_map(local, mesh=mesh, in_specs=in_specs, out_specs=out_specs, check_vma=False)
```

```python
import functools

import jax
import jax.numpy as jnp
from jax import lax
from jax.experimental import pallas as pl
from jax.experimental.pallas import tpu as pltpu
from jax.sharding import PartitionSpec as P

HDIM = 128
SUB = 4
F32 = jnp.float32
BF16 = jnp.bfloat16
ANY = pl.BlockSpec(memory_space=pl.ANY)
VMEM = pl.BlockSpec(memory_space=pltpu.VMEM)


def dot(a, b, contract=((1,), (0,))):
    return lax.dot_general(a, b, (contract, ((), ())), preferred_element_type=F32)


def cost(flops, moved):
    return pl.CostEstimate(flops=int(flops), bytes_accessed=int(moved), transcendentals=0)


def silu(u):
    return u / (1.0 + jnp.exp(-u))


def pack_columns(place, weights, count):
    depth = weights[0].shape[0]
    width = HDIM * len(weights)

    def kernel(place_ref, *refs):
        *ins, out = refs
        for i, ref in enumerate(ins):
            out[:, i * HDIM : (i + 1) * HDIM] = ref[...]

    return pl.pallas_call(
        kernel,
        out_shape=jax.ShapeDtypeStruct((count * depth, width), BF16),
        grid_spec=pltpu.PrefetchScalarGridSpec(
            num_scalar_prefetch=1,
            grid=(count,),
            in_specs=[pl.BlockSpec((depth, HDIM), lambda i, s: (0, 2 * lax.rem(i, SUB) + s[1]))] * len(weights),
            out_specs=pl.BlockSpec((depth, width), lambda i, s: (i, 0)),
        ),
        cost_estimate=cost(0, 2 * count * depth * width * 2),
        name="pack_columns",
    )(place, *weights)


def pack_rows(place, w_out):
    rows, width = w_out.shape
    half = width // 2

    def kernel(place_ref, keep_in, send_in, keep, send):
        keep[...] = keep_in[...]
        send[...] = send_in[...]

    def head(i, s):
        return 2 * jnp.bitwise_xor(s[0], lax.rem(i, SUB)) + jnp.bitwise_xor(s[1], i // SUB)

    return pl.pallas_call(
        kernel,
        out_shape=[jax.ShapeDtypeStruct((rows, half), BF16)] * 2,
        grid_spec=pltpu.PrefetchScalarGridSpec(
            num_scalar_prefetch=1,
            grid=(rows // HDIM,),
            in_specs=[
                pl.BlockSpec((HDIM, half), lambda i, s: (head(i, s), s[2])),
                pl.BlockSpec((HDIM, half), lambda i, s: (head(i, s), 1 - s[2])),
            ],
            out_specs=[pl.BlockSpec((HDIM, half), lambda i, s: (i, 0))] * 2,
        ),
        cost_estimate=cost(0, 2 * rows * width * 2),
        name="pack_rows",
    )(place, w_out, w_out)


class Stream:
    def __init__(self, pieces, rows, half):
        self.pieces, self.rows, self.half = pieces, rows, half

    def scratch(self, width):
        return [
            pltpu.VMEM((SUB, self.rows, 2 * self.half), BF16),
            pltpu.VMEM((2 * self.half, width), BF16),
            pltpu.SemaphoreType.DMA((len(self.pieces) + 2,)),
        ]

    def copies(self, place_ref, refs, w_ref, held, w_held, sems):
        core = place_ref[2]
        by_block = [[] for _ in range(SUB)]
        weight = []
        for i in range(2):
            start = (core if i == 0 else 1 - core) * self.half
            weight.append(
                pltpu.make_async_copy(
                    w_ref.at[pl.ds(start, self.half), :], w_held.at[pl.ds(i * self.half, self.half), :], sems.at[i]
                )
            )
        for i, ((array, block, column), ref) in enumerate(zip(self.pieces, refs)):
            target = held.at[block, :, pl.ds(column, array.shape[1])]
            by_block[block].append(pltpu.make_async_copy(ref, target, sems.at[i + 2]))
        for copy in weight:
            copy.start()
        for group in by_block:
            for copy in group:
                copy.start()
        return weight, by_block

    def arrays(self):
        return [array for array, _, _ in self.pieces]


SMEM = pl.BlockSpec(memory_space=pltpu.SMEM)


def project(place, stream, kv):
    rows, count = stream.rows, len(stream.pieces)

    def kernel(place_ref, *refs):
        ins, w_ref = refs[:count], refs[count]
        key_ref, value_ref, state_ref, held, w_held, sems = refs[count + 1 :]
        weight, by_block = stream.copies(place_ref, ins, w_ref, held, w_held, sems)
        for copy in weight:
            copy.wait()
        state = jnp.zeros((HDIM, HDIM), F32)
        for r in range(SUB):
            for copy in by_block[r]:
                copy.wait()
            both = dot(held[r], w_held[...])
            key = silu(both[:, :HDIM]).astype(BF16)
            value = both[:, HDIM:].astype(BF16)
            key_ref[r] = key
            value_ref[r] = value
            state = state + dot(key, value, ((0,), (0,)))
        state_ref[...] = state

    shape = jax.ShapeDtypeStruct((SUB, rows, HDIM), BF16)
    return pl.pallas_call(
        kernel,
        out_shape=[shape, shape, jax.ShapeDtypeStruct((HDIM, HDIM), F32)],
        in_specs=[SMEM] + [ANY] * (count + 1),
        out_specs=[VMEM] * 3,
        scratch_shapes=stream.scratch(2 * HDIM),
        cost_estimate=cost(2 * SUB * rows * 2 * stream.half * 2 * HDIM, SUB * rows * 2 * stream.half * 2),
        name="project",
    )(place, *stream.arrays(), kv)


def finish(place, stream, w_q, key, value, carried):
    rows, count = stream.rows, len(stream.pieces)

    def kernel(place_ref, *refs):
        ins, w_ref = refs[:count], refs[count]
        key_ref, value_ref, carried_ref, out_ref, held, w_held, sems = refs[count + 1 :]
        weight, by_block = stream.copies(place_ref, ins, w_ref, held, w_held, sems)
        block = place_ref[0]
        states = [dot(key_ref[r], value_ref[r], ((0,), (0,))) for r in range(SUB)]
        causal = lax.broadcasted_iota(jnp.int32, (rows, rows), 1) <= lax.broadcasted_iota(
            jnp.int32, (rows, rows), 0
        )
        for copy in weight:
            copy.wait()
        for r in range(SUB):
            earlier = carried_ref[...]
            for other in range(SUB):
                if other != r:
                    before = jnp.bitwise_xor(block, other) < jnp.bitwise_xor(block, r)
                    earlier = earlier + jnp.where(before, states[other], 0.0)
            for copy in by_block[r]:
                copy.wait()
            query = silu(dot(held[r], w_held[...])).astype(BF16)
            scores = dot(query, key_ref[r], ((1,), (1,)))
            weights = jnp.where(causal, scores, 0.0).astype(BF16)
            mixed = dot(weights, value_ref[r]) + dot(query, earlier.astype(BF16))
            scale = lax.rsqrt(jnp.mean(mixed * mixed, axis=-1, keepdims=True) + 1e-06)
            out_ref[r] = (mixed * scale).astype(BF16)

    return pl.pallas_call(
        kernel,
        out_shape=jax.ShapeDtypeStruct((SUB, rows, HDIM), BF16),
        in_specs=[SMEM] + [ANY] * (count + 1) + [VMEM] * 3,
        out_specs=VMEM,
        scratch_shapes=stream.scratch(HDIM),
        cost_estimate=cost(2 * SUB * rows * 2 * stream.half * HDIM, SUB * rows * 2 * stream.half * 2),
        name="finish",
    )(place, *stream.arrays(), w_q, key, value, carried)


def add_features(mine, theirs, w_mine, w_theirs, first, partial=None):
    rows, depth = mine.shape
    width = w_mine.shape[1]
    tile = min(512, width)

    def kernel(*refs):
        m_ref, t_ref, wm_ref, wt_ref = refs[:4]
        total = dot(m_ref[...], wm_ref[...]) + dot(t_ref[...], wt_ref[...])
        if partial is not None:
            total = total + refs[4][...]
        refs[-1][...] = total.astype(refs[-1].dtype)

    w_spec = pl.BlockSpec((depth, tile), lambda i: (0 if first else 1, i))
    sum_spec = pl.BlockSpec((rows, tile), lambda i: (0, i))
    return pl.pallas_call(
        kernel,
        out_shape=jax.ShapeDtypeStruct((rows, width), F32 if partial is None else BF16),
        grid=(width // tile,),
        in_specs=[pl.BlockSpec((rows, depth), lambda i: (0, 0))] * 2
        + [w_spec] * 2
        + ([] if partial is None else [sum_spec]),
        out_specs=sum_spec,
        cost_estimate=cost(4 * rows * depth * width, 4 * depth * width + 4 * rows * width),
        name="add_features",
    )(mine, theirs, w_mine, w_theirs, *([] if partial is None else [partial]))


def exclusive_prefix(value, groups):
    def shift(v, step):
        pairs = [(g * SUB + j, (g + step) * SUB + j) for g in range(groups - step) for j in range(SUB)]
        return lax.ppermute(v, "ctx", pairs)

    if groups == 1:
        return jnp.zeros_like(value)
    total = shift(value, 1)
    step = 1
    while step < groups - 1:
        total = total + shift(total, step)
        step *= 2
    return total


def local(tokens, w_query, w_key, w_value, w_out):
    n_ctx = lax.axis_size("ctx")
    groups = n_ctx // SUB
    rows, half = tokens.shape
    block = lax.axis_index("ctx") % SUB
    place = jnp.stack([block, lax.axis_index("groups"), lax.axis_index("head")]).astype(jnp.int32)

    def xor(value, step):
        return lax.ppermute(value, "ctx", [(i, i ^ step) for i in range(n_ctx)])

    def other_part(value):
        return lax.ppermute(value, "groups", [(0, 1), (1, 0)])

    def other_core(value):
        return lax.ppermute(value, "head", [(0, 1), (1, 0)])

    def spread(packed):
        return lax.all_to_all(packed, "ctx", 0, 0, tiled=True)

    cut = half // 2
    across = xor(tokens, 2)
    beside = xor(tokens, 1)
    kv_mine = spread(pack_columns(place, [w_key, w_value], n_ctx))
    q_packed = pack_columns(place, [w_query], n_ctx)
    across, beside, kv_mine, q_packed = lax.optimization_barrier((across, beside, kv_mine, q_packed))
    kv_other = other_part(kv_mine)
    q_mine = spread(q_packed)
    left = xor(across[:, :cut], 1)
    right = xor(beside[:, cut:], 2)
    left, right, q_mine, kv_other = lax.optimization_barrier((left, right, q_mine, kv_other))
    q_other = other_part(q_mine)

    out_keep, out_send = pack_rows(place, w_out)
    out_other = other_core(out_send)

    pieces = []
    for array, r, column in ((tokens, 0, 0), (beside, 1, 0), (across, 2, 0), (left, 3, 0), (right, 3, cut)):
        pieces += [(array, r, column), (other_core(array), r, half + column)]
    stream = Stream(pieces, rows, half)

    def exchange(normed):
        return jnp.concatenate([normed[0]] + [xor(normed[r], r) for r in range(1, SUB)], axis=1)

    k_mine, v_mine, state_mine = project(place, stream, kv_mine)
    carried_mine = exclusive_prefix(state_mine, groups)
    k_other, v_other, state_other = project(place, stream, kv_other)
    carried_other = exclusive_prefix(state_other, groups)
    mine = exchange(finish(place, stream, q_mine, k_mine, v_mine, carried_mine))
    partial = add_features(mine, other_core(mine), out_keep, out_other, True)
    theirs = exchange(finish(place, stream, q_other, k_other, v_other, carried_other))
    return add_features(theirs, other_core(theirs), out_keep, out_other, False, partial)


def solution(mesh):
    in_specs = (
        P(("groups", "ctx"), "head"),
        P("ctx", "head"),
        P("ctx", "head"),
        P("ctx", "head"),
        P("head", None),
    )
    out_specs = P(("groups", "ctx"), "head")
    return jax.shard_map(local, mesh=mesh, in_specs=in_specs, out_specs=out_specs, check_vma=False)
```

```python
import jax
import jax.numpy as jnp
from jax import lax
from jax.experimental import pallas as pl
from jax.experimental.pallas import tpu as pltpu
from jax.sharding import PartitionSpec as P

HDIM = 128
SUB = 4
F32 = jnp.float32
BF16 = jnp.bfloat16
MIB = 1 << 20
LIMIT = 8
ANY = pl.BlockSpec(memory_space=pl.ANY)
VMEM = pl.BlockSpec(memory_space=pltpu.VMEM)
SMEM = pl.BlockSpec(memory_space=pltpu.SMEM)


def dot(a, b, contract=((1,), (0,))):
    return lax.dot_general(a, b, (contract, ((), ())), preferred_element_type=F32)


def silu(u):
    return u / (1.0 + jnp.exp(-u))


def call(kernel, name, out_shape, in_specs, out_specs, limit, flops, moved, scratch=()):
    return pl.pallas_call(
        kernel,
        out_shape=out_shape,
        in_specs=in_specs,
        out_specs=out_specs,
        scratch_shapes=list(scratch),
        compiler_params=pltpu.CompilerParams(vmem_limit_bytes=limit * MIB),
        cost_estimate=pl.CostEstimate(flops=int(flops), bytes_accessed=int(moved), transcendentals=0),
        name=name,
    )


def pack_keys_values(place, w_key, w_value, count):
    depth = w_key.shape[0]

    def kernel(place_ref, key_ref, value_ref, out):
        for j in range(SUB):
            start = pl.multiple_of((2 * j + place_ref[1]) * HDIM, HDIM)
            key = key_ref[:, pl.ds(start, HDIM)]
            value = value_ref[:, pl.ds(start, HDIM)]
            for i in range(j, count, SUB):
                out[i * depth : (i + 1) * depth, :HDIM] = key
                out[i * depth : (i + 1) * depth, HDIM:] = value

    shape = jax.ShapeDtypeStruct((count * depth, 2 * HDIM), BF16)
    moved = count * depth * 2 * HDIM * 4
    return call(kernel, "pack_keys_values", shape, [SMEM, VMEM, VMEM], VMEM, LIMIT, 0, moved)(place, w_key, w_value)


def pack_queries(place, w_query):
    depth = w_query.shape[0]

    def kernel(place_ref, query_ref, *outs):
        for r, out in enumerate(outs):
            start = pl.multiple_of(jnp.bitwise_xor(place_ref[0], r) * 2 * HDIM, 2 * HDIM)
            out[...] = query_ref[:, pl.ds(start, 2 * HDIM)]

    shapes = [jax.ShapeDtypeStruct((depth, 2 * HDIM), BF16)] * SUB
    moved = SUB * depth * 2 * HDIM * 4
    return call(kernel, "pack_queries", shapes, [SMEM, VMEM], [VMEM] * SUB, LIMIT, 0, moved)(place, w_query)


def take_rows(place, w_out):
    rows, width = w_out.shape
    half = width // 2
    return lax.dynamic_slice(w_out, (0, (1 - place[2]) * half), (rows, half))


def stage_rows(place, w_out, w_far):
    rows, half = w_far.shape
    depth = rows // SUB

    def kernel(place_ref, out_ref, far_ref, keep, far, sems):
        column = pl.multiple_of(place_ref[2] * half, half)
        copies = []
        for r in range(SUB):
            row = pl.multiple_of(jnp.bitwise_xor(place_ref[0], r) * depth, depth)
            copies.append(
                pltpu.make_async_copy(out_ref.at[pl.ds(row, depth), pl.ds(column, half)], keep.at[r], sems.at[r])
            )
            copies.append(pltpu.make_async_copy(far_ref.at[pl.ds(row, depth), :], far.at[r], sems.at[SUB + r]))
        for copy in copies:
            copy.start()
        for copy in copies:
            copy.wait()

    shapes = [pltpu.VMEM((SUB, depth, half), BF16)] * 2
    sems = pltpu.SemaphoreType.DMA((2 * SUB,))
    return call(kernel, "stage_rows", shapes, [SMEM, ANY, ANY], [VMEM] * 2, 40, 0, rows * half * 8, [sems])(
        place, w_out, w_far
    )


def stage(pieces, rows, width):
    count = len(pieces)

    def kernel(*refs):
        out, sems = refs[count], refs[count + 1]
        copies = [
            pltpu.make_async_copy(ref, out.at[r, :, pl.ds(column, array.shape[1])], sems.at[i])
            for i, ((array, r, column), ref) in enumerate(zip(pieces, refs))
        ]
        for copy in copies:
            copy.start()
        for copy in copies:
            copy.wait()

    shape = pltpu.VMEM((SUB, rows, width), BF16)
    sems = pltpu.SemaphoreType.DMA((count,))
    return call(kernel, "stage", shape, [ANY] * count, VMEM, LIMIT, 0, SUB * rows * width * 4, [sems])(
        *[array for array, _, _ in pieces]
    )


def by_halves(place_ref, stream_ref, r, w_ref):
    half = w_ref.shape[0] // 2
    own = pl.multiple_of(place_ref[2] * half, half)
    far = pl.multiple_of((1 - place_ref[2]) * half, half)
    return dot(stream_ref[r, :, :half], w_ref[pl.ds(own, half), :]) + dot(
        stream_ref[r, :, half:], w_ref[pl.ds(far, half), :]
    )


def project(place, stream, kv):
    _, rows, width = stream.shape

    def kernel(place_ref, stream_ref, w_ref, key_ref, value_ref, before_ref, total_ref):
        states = []
        for r in range(SUB):
            both = by_halves(place_ref, stream_ref, r, w_ref)
            key = silu(both[:, :HDIM]).astype(BF16)
            value = both[:, HDIM:].astype(BF16)
            key_ref[r] = key
            value_ref[r] = value
            states.append(dot(key, value, ((0,), (0,))))
        total_ref[...] = (states[0] + states[1]) + (states[2] + states[3])
        block = place_ref[0]
        for r in range(SUB):
            before = jnp.zeros((HDIM, HDIM), F32)
            for other in range(SUB):
                if other != r:
                    is_before = jnp.bitwise_xor(block, other) < jnp.bitwise_xor(block, r)
                    before = before + jnp.where(is_before, states[other], 0.0)
            before_ref[r] = before

    shape = jax.ShapeDtypeStruct((SUB, rows, HDIM), BF16)
    shapes = [shape, shape, jax.ShapeDtypeStruct((SUB, HDIM, HDIM), F32), jax.ShapeDtypeStruct((HDIM, HDIM), F32)]
    flops = 4 * SUB * rows * width * HDIM
    return call(kernel, "project", shapes, [SMEM, VMEM, VMEM], [VMEM] * 4, LIMIT, flops, 2 * MIB)(place, stream, kv)


def queries(place, stream, pieces):
    _, rows, width = stream.shape
    count = len(pieces)
    depth = pieces[0].shape[0]
    half = width // 2

    def kernel(place_ref, stream_ref, *refs):
        ins, out, w_held = refs[:count], refs[count], refs[count + 1]
        for m, piece in enumerate(ins):
            row = jnp.bitwise_xor(place_ref[3], m) * depth
            far = jnp.where(row >= half, 1, 0) != place_ref[2]
            row = pl.multiple_of(lax.rem(row, half) + jnp.where(far, half, 0), depth)
            w_held[pl.ds(row, depth), :] = piece[...]
        swap = place_ref[1] == 1
        for r in range(SUB):
            both = silu(dot(stream_ref[r], w_held[...])).astype(BF16)
            out[r, :, :HDIM] = jnp.where(swap, both[:, HDIM:], both[:, :HDIM])
            out[r, :, HDIM:] = jnp.where(swap, both[:, :HDIM], both[:, HDIM:])

    shape = jax.ShapeDtypeStruct((SUB, rows, 2 * HDIM), BF16)
    flops = 4 * SUB * rows * width * HDIM
    held = pltpu.VMEM((width, 2 * HDIM), BF16)
    return call(
        kernel, "queries", shape, [SMEM, VMEM] + [VMEM] * count, VMEM, LIMIT, flops, 2 * MIB, [held]
    )(place, stream, *pieces)


def attend(place, blocks, query, parts):
    rows = query.shape[1]
    count = len(blocks)

    def kernel(place_ref, query_ref, *refs):
        ins, outs = refs[:8], refs[8:]
        causal = lax.broadcasted_iota(jnp.int32, (rows, rows), 1) <= lax.broadcasted_iota(
            jnp.int32, (rows, rows), 0
        )
        for i, r in enumerate(blocks):
            for h in range(2):
                key_ref, value_ref, before_ref, carried_ref = ins[4 * h : 4 * h + 4]
                columns = slice(h * HDIM, (h + 1) * HDIM)
                q = query_ref[r, :, columns]
                earlier = (before_ref[r] + carried_ref[...]).astype(BF16)
                scores = dot(q, key_ref[r], ((1,), (1,)))
                weights = jnp.where(causal, scores, 0.0).astype(BF16)
                mixed = dot(weights, value_ref[r]) + dot(q, earlier)
                scale = lax.rsqrt(jnp.mean(mixed * mixed, axis=-1, keepdims=True) + 1e-06)
                target = pl.multiple_of(jnp.bitwise_xor(place_ref[1], h) * HDIM, HDIM)
                outs[i][:, pl.ds(target, HDIM)] = (mixed * scale).astype(BF16)

    shapes = [jax.ShapeDtypeStruct((rows, 2 * HDIM), BF16)] * count
    flops = count * 4 * rows * HDIM * (2 * rows + HDIM)
    return call(kernel, "attend", shapes, [SMEM] + [VMEM] * 9, [VMEM] * count, LIMIT, flops, 2 * MIB)(
        place, query, *parts[0], *parts[1]
    )


def add_features(pieces, weight, partial=None):
    rows, depth = pieces[0].shape
    width = weight.shape[2]
    count = len(pieces)
    tile = min(512, width)

    def kernel(*refs):
        w_ref, out = refs[count], refs[-1]
        for start in range(0, width, tile):
            columns = slice(start, start + tile)
            total = refs[count + 1][:, columns] if partial is not None else jnp.zeros((rows, tile), F32)
            for i in range(count):
                total = total + dot(refs[i][...], w_ref[i, :, columns])
            out[:, columns] = total.astype(out.dtype)

    shape = pltpu.VMEM((rows, width), F32) if partial is None else jax.ShapeDtypeStruct((rows, width), BF16)
    args = [*pieces, weight] + ([] if partial is None else [partial])
    flops = 2 * count * depth * rows * width
    return call(kernel, "add_features", shape, [VMEM] * len(args), VMEM, LIMIT, flops, 8 * MIB)(*args)


def exclusive_prefix(value, groups):
    def shift(v, step):
        pairs = [(g * SUB + j, (g + step) * SUB + j) for g in range(groups - step) for j in range(SUB)]
        return lax.ppermute(v, "ctx", pairs)

    if groups == 1:
        return jnp.zeros_like(value)
    total = shift(value, 1)
    step = 1
    while step < groups - 1:
        total = total + shift(total, step)
        step *= 2
    return total


def local(tokens, w_query, w_key, w_value, w_out):
    n_ctx = lax.axis_size("ctx")
    groups = n_ctx // SUB
    rows, half = tokens.shape
    ctx = lax.axis_index("ctx")
    place = jnp.stack([ctx % SUB, lax.axis_index("groups"), lax.axis_index("head"), ctx]).astype(jnp.int32)

    def xor(value, step):
        return lax.ppermute(value, "ctx", [(i, i ^ step) for i in range(n_ctx)])

    def other_part(value):
        return lax.ppermute(value, "groups", [(0, 1), (1, 0)])

    def other_core(value):
        return lax.ppermute(value, "head", [(0, 1), (1, 0)])

    def spread(packed):
        return lax.all_to_all(packed, "ctx", 0, 0, tiled=True)

    def gather_queries(sent):
        block = ctx % SUB
        ordered = [lax.dynamic_index_in_dim(jnp.stack(sent), block ^ j, keepdims=False) for j in range(SUB)]
        whole = spread(jnp.concatenate(ordered * groups, axis=0)).reshape(n_ctx, -1, 2 * HDIM)
        return [lax.dynamic_index_in_dim(whole, ctx ^ m, keepdims=False) for m in range(n_ctx)]

    across = xor(tokens, 2)
    beside = xor(tokens, 1)
    kv_mine = spread(pack_keys_values(place, w_key, w_value, n_ctx))
    q_sent = pack_queries(place, w_query)
    across, beside, kv_mine, q_sent = lax.optimization_barrier((across, beside, kv_mine, q_sent))
    cut = half * 11 // 16 // HDIM * HDIM
    left = xor(across[:, :cut], 1)
    right = xor(beside[:, cut:], 2)
    kv_other = other_part(kv_mine)
    arrived = {m: xor(q_sent[m % SUB], m) for m in (4, 6, 5, 7, 2, 3, 1)} if n_ctx == 2 * SUB else {}
    if arrived:
        q_pieces = [q_sent[0]] + [arrived[m] for m in range(1, n_ctx)]
    else:
        q_pieces = gather_queries(q_sent)

    w_far = other_core(take_rows(place, w_out))

    pieces = []
    for array, r, column in ((tokens, 0, 0), (beside, 1, 0), (across, 2, 0), (left, 3, 0), (right, 3, cut)):
        pieces += [(array, r, column), (other_core(array), r, half + column)]
    stream = stage(pieces, rows, 2 * half)

    def keys_values(kv):
        key, value, before, total = project(place, stream, kv)
        return key, value, before, exclusive_prefix(total, groups)

    parts = [keys_values(kv_mine), keys_values(kv_other)]
    query = queries(place, stream, q_pieces)
    away = attend(place, (3, 1, 2), query, parts)
    home = attend(place, (0,), query, parts)
    normed = [home[0], xor(away[1], 1), xor(away[2], 2), xor(away[0], 3)]
    home_0, w_far = lax.optimization_barrier((home[0], w_far))
    out_keep, out_far = stage_rows(place, w_out, w_far)
    out_keep, out_far, *normed = lax.optimization_barrier((out_keep, out_far, home_0, *normed[1:]))
    partial = add_features(normed, out_keep)
    return add_features([other_core(n) for n in normed], out_far, partial)


def solution(mesh):
    in_specs = (
        P(("groups", "ctx"), "head"),
        P("ctx", "head"),
        P("ctx", "head"),
        P("ctx", "head"),
        P("head", None),
    )
    out_specs = P(("groups", "ctx"), "head")
    return jax.shard_map(local, mesh=mesh, in_specs=in_specs, out_specs=out_specs, check_vma=False)
```

```python
import jax
import jax.numpy as jnp
from jax import lax
from jax.experimental import pallas as pl
from jax.experimental.pallas import tpu as pltpu
from jax.sharding import PartitionSpec as P

HDIM = 128
SUB = 4
F32 = jnp.float32
BF16 = jnp.bfloat16
MIB = 1 << 20
LIMIT = 8
ANY = pl.BlockSpec(memory_space=pl.ANY)
VMEM = pl.BlockSpec(memory_space=pltpu.VMEM)
SMEM = pl.BlockSpec(memory_space=pltpu.SMEM)


def dot(a, b, contract=((1,), (0,))):
    return lax.dot_general(a, b, (contract, ((), ())), preferred_element_type=F32)


def silu(u):
    return u / (1.0 + jnp.exp(-u))


def call(kernel, name, out_shape, in_specs, out_specs, limit, flops, moved, scratch=()):
    return pl.pallas_call(
        kernel,
        out_shape=out_shape,
        in_specs=in_specs,
        out_specs=out_specs,
        scratch_shapes=list(scratch),
        compiler_params=pltpu.CompilerParams(vmem_limit_bytes=limit * MIB),
        cost_estimate=pl.CostEstimate(flops=int(flops), bytes_accessed=int(moved), transcendentals=0),
        name=name,
    )


def pack_keys_values(place, w_key, w_value, count):
    depth = w_key.shape[0]

    def kernel(place_ref, key_ref, value_ref, out):
        for j in range(SUB):
            start = pl.multiple_of((2 * j + place_ref[1]) * HDIM, HDIM)
            key = key_ref[:, pl.ds(start, HDIM)]
            value = value_ref[:, pl.ds(start, HDIM)]
            for i in range(j, count, SUB):
                out[i * depth : (i + 1) * depth, :HDIM] = key
                out[i * depth : (i + 1) * depth, HDIM:] = value

    shape = jax.ShapeDtypeStruct((count * depth, 2 * HDIM), BF16)
    moved = count * depth * 2 * HDIM * 4
    return call(kernel, "pack_keys_values", shape, [SMEM, VMEM, VMEM], VMEM, LIMIT, 0, moved)(place, w_key, w_value)


def pack_queries(place, w_query):
    depth = w_query.shape[0]

    def kernel(place_ref, query_ref, *outs):
        for r, out in enumerate(outs):
            start = pl.multiple_of(jnp.bitwise_xor(place_ref[0], r) * 2 * HDIM, 2 * HDIM)
            out[...] = query_ref[:, pl.ds(start, 2 * HDIM)]

    shapes = [jax.ShapeDtypeStruct((depth, 2 * HDIM), BF16)] * SUB
    moved = SUB * depth * 2 * HDIM * 4
    return call(kernel, "pack_queries", shapes, [SMEM, VMEM], [VMEM] * SUB, LIMIT, 0, moved)(place, w_query)


def take_rows(place, w_out):
    rows, width = w_out.shape
    half = width // 2
    return lax.dynamic_slice(w_out, (0, (1 - place[2]) * half), (rows, half))


def stage_rows(place, w_out, w_far):
    rows, half = w_far.shape
    depth = rows // SUB

    def kernel(place_ref, out_ref, far_ref, keep, far, sems):
        column = pl.multiple_of(place_ref[2] * half, half)
        copies = []
        for r in range(SUB):
            row = pl.multiple_of(jnp.bitwise_xor(place_ref[0], r) * depth, depth)
            copies.append(
                pltpu.make_async_copy(out_ref.at[pl.ds(row, depth), pl.ds(column, half)], keep.at[r], sems.at[r])
            )
            copies.append(pltpu.make_async_copy(far_ref.at[pl.ds(row, depth), :], far.at[r], sems.at[SUB + r]))
        for copy in copies:
            copy.start()
        for copy in copies:
            copy.wait()

    shapes = [pltpu.VMEM((SUB, depth, half), BF16)] * 2
    sems = pltpu.SemaphoreType.DMA((2 * SUB,))
    return call(kernel, "stage_rows", shapes, [SMEM, ANY, ANY], [VMEM] * 2, 40, 0, rows * half * 8, [sems])(
        place, w_out, w_far
    )


def stage(place, pieces, rows, width):
    count = len(pieces)
    half = width // 2

    def kernel(place_ref, *refs):
        out, sems = refs[count], refs[count + 1]
        copies = []
        for i, ((array, r, column, far), ref) in enumerate(zip(pieces, refs)):
            core = 1 - place_ref[2] if far else place_ref[2]
            start = pl.multiple_of(core * half + column, HDIM)
            copies.append(pltpu.make_async_copy(ref, out.at[r, :, pl.ds(start, array.shape[1])], sems.at[i]))
        for copy in copies:
            copy.start()
        for copy in copies:
            copy.wait()

    shape = pltpu.VMEM((SUB, rows, width), BF16)
    sems = pltpu.SemaphoreType.DMA((count,))
    return call(
        kernel, "stage", shape, [SMEM] + [ANY] * count, VMEM, LIMIT, 0, SUB * rows * width * 4, [sems]
    )(place, *[piece[0] for piece in pieces])


def project(place, stream, kv):
    _, rows, width = stream.shape

    def kernel(place_ref, stream_ref, w_ref, key_ref, value_ref, before_ref, total_ref):
        states = []
        for r in range(SUB):
            both = dot(stream_ref[r], w_ref[...])
            key = silu(both[:, :HDIM]).astype(BF16)
            value = both[:, HDIM:].astype(BF16)
            key_ref[r] = key
            value_ref[r] = value
            states.append(dot(key, value, ((0,), (0,))))
        total_ref[...] = (states[0] + states[1]) + (states[2] + states[3])
        block = place_ref[0]
        for r in range(SUB):
            before = jnp.zeros((HDIM, HDIM), F32)
            for other in range(SUB):
                if other != r:
                    is_before = jnp.bitwise_xor(block, other) < jnp.bitwise_xor(block, r)
                    before = before + jnp.where(is_before, states[other], 0.0)
            before_ref[r] = before

    shape = jax.ShapeDtypeStruct((SUB, rows, HDIM), BF16)
    shapes = [shape, shape, jax.ShapeDtypeStruct((SUB, HDIM, HDIM), F32), jax.ShapeDtypeStruct((HDIM, HDIM), F32)]
    flops = 4 * SUB * rows * width * HDIM
    return call(kernel, "project", shapes, [SMEM, VMEM, VMEM], [VMEM] * 4, LIMIT, flops, 2 * MIB)(place, stream, kv)


def queries(place, stream, pieces):
    _, rows, width = stream.shape
    count = len(pieces)
    depth = pieces[0].shape[0]

    def kernel(place_ref, stream_ref, *refs):
        ins, out, w_held = refs[:count], refs[count], refs[count + 1]
        for m, piece in enumerate(ins):
            row = pl.multiple_of(jnp.bitwise_xor(place_ref[3], m) * depth, depth)
            w_held[pl.ds(row, depth), :] = piece[...]
        swap = place_ref[1] == 1
        for r in range(SUB):
            both = silu(dot(stream_ref[r], w_held[...])).astype(BF16)
            out[r, :, :HDIM] = jnp.where(swap, both[:, HDIM:], both[:, :HDIM])
            out[r, :, HDIM:] = jnp.where(swap, both[:, :HDIM], both[:, HDIM:])

    shape = jax.ShapeDtypeStruct((SUB, rows, 2 * HDIM), BF16)
    flops = 4 * SUB * rows * width * HDIM
    held = pltpu.VMEM((width, 2 * HDIM), BF16)
    return call(
        kernel, "queries", shape, [SMEM, VMEM] + [VMEM] * count, VMEM, LIMIT, flops, 2 * MIB, [held]
    )(place, stream, *pieces)


def attend(place, blocks, query, parts):
    rows = query.shape[1]
    count = len(blocks)

    def kernel(place_ref, query_ref, *refs):
        ins, outs = refs[:8], refs[8:]
        causal = lax.broadcasted_iota(jnp.int32, (rows, rows), 1) <= lax.broadcasted_iota(
            jnp.int32, (rows, rows), 0
        )
        for i, r in enumerate(blocks):
            for h in range(2):
                key_ref, value_ref, before_ref, carried_ref = ins[4 * h : 4 * h + 4]
                columns = slice(h * HDIM, (h + 1) * HDIM)
                q = query_ref[r, :, columns]
                earlier = (before_ref[r] + carried_ref[...]).astype(BF16)
                scores = dot(q, key_ref[r], ((1,), (1,)))
                weights = jnp.where(causal, scores, 0.0).astype(BF16)
                mixed = dot(weights, value_ref[r]) + dot(q, earlier)
                scale = lax.rsqrt(jnp.mean(mixed * mixed, axis=-1, keepdims=True) + 1e-06)
                target = pl.multiple_of(jnp.bitwise_xor(place_ref[1], h) * HDIM, HDIM)
                outs[i][:, pl.ds(target, HDIM)] = (mixed * scale).astype(BF16)

    shapes = [jax.ShapeDtypeStruct((rows, 2 * HDIM), BF16)] * count
    flops = count * 4 * rows * HDIM * (2 * rows + HDIM)
    return call(kernel, "attend", shapes, [SMEM] + [VMEM] * 9, [VMEM] * count, LIMIT, flops, 2 * MIB)(
        place, query, *parts[0], *parts[1]
    )


def add_features(pieces, weight, partial=None):
    rows, depth = pieces[0].shape
    width = weight.shape[2]
    count = len(pieces)
    tile = min(512, width)

    def kernel(*refs):
        w_ref, out = refs[count], refs[-1]
        for start in range(0, width, tile):
            columns = slice(start, start + tile)
            total = refs[count + 1][:, columns] if partial is not None else jnp.zeros((rows, tile), F32)
            for i in range(count):
                total = total + dot(refs[i][...], w_ref[i, :, columns])
            out[:, columns] = total.astype(out.dtype)

    shape = pltpu.VMEM((rows, width), F32) if partial is None else jax.ShapeDtypeStruct((rows, width), BF16)
    args = [*pieces, weight] + ([] if partial is None else [partial])
    flops = 2 * count * depth * rows * width
    return call(kernel, "add_features", shape, [VMEM] * len(args), VMEM, LIMIT, flops, 8 * MIB)(*args)


def exclusive_prefix(value, groups):
    def shift(v, step):
        pairs = [(g * SUB + j, (g + step) * SUB + j) for g in range(groups - step) for j in range(SUB)]
        return lax.ppermute(v, "ctx", pairs)

    if groups == 1:
        return jnp.zeros_like(value)
    total = shift(value, 1)
    step = 1
    while step < groups - 1:
        total = total + shift(total, step)
        step *= 2
    return total


def local(tokens, w_query, w_key, w_value, w_out):
    n_ctx = lax.axis_size("ctx")
    groups = n_ctx // SUB
    rows, half = tokens.shape
    ctx = lax.axis_index("ctx")
    place = jnp.stack([ctx % SUB, lax.axis_index("groups"), lax.axis_index("head"), ctx]).astype(jnp.int32)

    def xor(value, step):
        return lax.ppermute(value, "ctx", [(i, i ^ step) for i in range(n_ctx)])

    def other_part(value):
        return lax.ppermute(value, "groups", [(0, 1), (1, 0)])

    def other_core(value):
        return lax.ppermute(value, "head", [(0, 1), (1, 0)])

    def spread(packed):
        return lax.all_to_all(packed, "ctx", 0, 0, tiled=True)

    def gather_queries(sent):
        block = ctx % SUB
        ordered = [lax.dynamic_index_in_dim(jnp.stack(sent), block ^ j, keepdims=False) for j in range(SUB)]
        whole = spread(jnp.concatenate(ordered * groups, axis=0)).reshape(n_ctx, -1, 2 * HDIM)
        return [lax.dynamic_index_in_dim(whole, ctx ^ m, keepdims=False) for m in range(n_ctx)]

    cut = half * 11 // 16 // HDIM * HDIM
    across = xor(tokens, 2)
    beside = xor(tokens, 1)
    kv_mine = spread(pack_keys_values(place, w_key, w_value, n_ctx))
    q_sent = pack_queries(place, w_query)
    w_far = other_core(take_rows(place, w_out))
    far_tokens = other_core(tokens)
    far_beside = other_core(beside)
    across, beside, kv_mine, q_sent, w_far, far_tokens, far_beside = lax.optimization_barrier(
        (across, beside, kv_mine, q_sent, w_far, far_tokens, far_beside)
    )
    left = xor(across[:, :cut], 1)
    right = xor(beside[:, cut:], 2)
    kv_other = other_part(kv_mine)
    far_across = other_core(across)
    if n_ctx == 2 * SUB:
        arrived = {0: q_sent[0]} | {m: xor(q_sent[m % SUB], m) for m in (4, 6)}
        left, right, arrived, q_sent = lax.optimization_barrier((left, right, arrived, q_sent))
        arrived = arrived | {m: xor(q_sent[m % SUB], m) for m in (5, 7, 2, 3, 1)}
        q_pieces = [arrived[m] for m in range(n_ctx)]
    else:
        q_pieces = gather_queries(q_sent)

    pieces = [(tokens, 0, 0, False), (far_tokens, 0, 0, True), (beside, 1, 0, False), (far_beside, 1, 0, True)]
    pieces += [(across, 2, 0, False), (far_across, 2, 0, True)]
    for array, column in ((left, 0), (right, cut)):
        pieces += [(array, 3, column, False), (other_core(array), 3, column, True)]
    stream = stage(place, pieces, rows, 2 * half)

    def keys_values(kv):
        key, value, before, total = project(place, stream, kv)
        return key, value, before, exclusive_prefix(total, groups)

    parts = [keys_values(kv_mine), keys_values(kv_other)]
    query = queries(place, stream, q_pieces)
    away = attend(place, (3, 1, 2), query, parts)
    home = attend(place, (0,), query, parts)
    normed = [home[0], xor(away[1], 1), xor(away[2], 2), xor(away[0], 3)]
    home_0, w_far = lax.optimization_barrier((home[0], w_far))
    out_keep, out_far = stage_rows(place, w_out, w_far)
    out_keep, out_far, *normed = lax.optimization_barrier((out_keep, out_far, home_0, *normed[1:]))
    partial = add_features(normed, out_keep)
    return add_features([other_core(n) for n in normed], out_far, partial)


def solution(mesh):
    in_specs = (
        P(("groups", "ctx"), "head"),
        P("ctx", "head"),
        P("ctx", "head"),
        P("ctx", "head"),
        P("head", None),
    )
    out_specs = P(("groups", "ctx"), "head")
    return jax.shard_map(local, mesh=mesh, in_specs=in_specs, out_specs=out_specs, check_vma=False)
```

```python
import jax
import jax.numpy as jnp
from jax import lax
from jax.experimental import pallas as pl
from jax.experimental.pallas import tpu as pltpu
from jax.sharding import PartitionSpec as P

HDIM = 128
SUB = 4
F32 = jnp.float32
BF16 = jnp.bfloat16
MIB = 1 << 20
LIMIT = 8
ANY = pl.BlockSpec(memory_space=pl.ANY)
VMEM = pl.BlockSpec(memory_space=pltpu.VMEM)
SMEM = pl.BlockSpec(memory_space=pltpu.SMEM)


def dot(a, b, contract=((1,), (0,))):
    return lax.dot_general(a, b, (contract, ((), ())), preferred_element_type=F32)


def silu(u):
    return u / (1.0 + jnp.exp(-u))


def call(kernel, name, out_shape, in_specs, out_specs, limit, flops, moved, scratch=()):
    return pl.pallas_call(
        kernel,
        out_shape=out_shape,
        in_specs=in_specs,
        out_specs=out_specs,
        scratch_shapes=list(scratch),
        compiler_params=pltpu.CompilerParams(vmem_limit_bytes=limit * MIB),
        cost_estimate=pl.CostEstimate(flops=int(flops), bytes_accessed=int(moved), transcendentals=0),
        name=name,
    )


def pack_keys_values(place, w_key, w_value, count):
    depth = w_key.shape[0]

    def kernel(place_ref, key_ref, value_ref, out):
        for j in range(SUB):
            start = pl.multiple_of((2 * j + place_ref[1]) * HDIM, HDIM)
            key = key_ref[:, pl.ds(start, HDIM)]
            value = value_ref[:, pl.ds(start, HDIM)]
            for i in range(j, count, SUB):
                out[i * depth : (i + 1) * depth, :HDIM] = key
                out[i * depth : (i + 1) * depth, HDIM:] = value

    shape = jax.ShapeDtypeStruct((count * depth, 2 * HDIM), BF16)
    moved = count * depth * 2 * HDIM * 4
    return call(kernel, "pack_keys_values", shape, [SMEM, VMEM, VMEM], VMEM, LIMIT, 0, moved)(place, w_key, w_value)


def pack_queries(place, w_query):
    depth = w_query.shape[0]

    def kernel(place_ref, query_ref, *outs):
        for r, out in enumerate(outs):
            start = pl.multiple_of(jnp.bitwise_xor(place_ref[0], r) * 2 * HDIM, 2 * HDIM)
            out[...] = query_ref[:, pl.ds(start, 2 * HDIM)]

    shapes = [jax.ShapeDtypeStruct((depth, 2 * HDIM), BF16)] * SUB
    moved = SUB * depth * 2 * HDIM * 4
    return call(kernel, "pack_queries", shapes, [SMEM, VMEM], [VMEM] * SUB, LIMIT, 0, moved)(place, w_query)


def take_rows(place, w_out):
    rows, width = w_out.shape
    half = width // 2
    return lax.dynamic_slice(w_out, (0, (1 - place[2]) * half), (rows, half))


def stage_rows(place, w_out, w_far):
    rows, half = w_far.shape
    depth = rows // SUB

    def kernel(place_ref, out_ref, far_ref, keep, far, sems):
        column = pl.multiple_of(place_ref[2] * half, half)
        copies = []
        for r in range(SUB):
            row = pl.multiple_of(jnp.bitwise_xor(place_ref[0], r) * depth, depth)
            copies.append(
                pltpu.make_async_copy(out_ref.at[pl.ds(row, depth), pl.ds(column, half)], keep.at[r], sems.at[r])
            )
            copies.append(pltpu.make_async_copy(far_ref.at[pl.ds(row, depth), :], far.at[r], sems.at[SUB + r]))
        for copy in copies:
            copy.start()
        for copy in copies:
            copy.wait()

    shapes = [pltpu.VMEM((SUB, depth, half), BF16)] * 2
    sems = pltpu.SemaphoreType.DMA((2 * SUB,))
    return call(kernel, "stage_rows", shapes, [SMEM, ANY, ANY], [VMEM] * 2, 40, 0, rows * half * 8, [sems])(
        place, w_out, w_far
    )


def stage(place, pieces, blocks, rows, width):
    count = len(pieces)
    half = width // 2

    def kernel(place_ref, *refs):
        out, sems = refs[count], refs[count + 1]
        copies = []
        for i, ((array, r, column, far), ref) in enumerate(zip(pieces, refs)):
            if far is None:
                target = out.at[r]
            else:
                core = 1 - place_ref[2] if far else place_ref[2]
                start = pl.multiple_of(core * half + column, HDIM)
                target = out.at[r, :, pl.ds(start, array.shape[1])]
            copies.append(pltpu.make_async_copy(ref, target, sems.at[i]))
        for copy in copies:
            copy.start()
        for copy in copies:
            copy.wait()

    shape = pltpu.VMEM((blocks, rows, width), BF16)
    sems = pltpu.SemaphoreType.DMA((count,))
    moved = blocks * rows * width * 4
    return call(kernel, "stage", shape, [SMEM] + [ANY] * count, VMEM, LIMIT, 0, moved, [sems])(
        place, *[piece[0] for piece in pieces]
    )


def project(stream, kv, total=None):
    blocks, rows, width = stream.shape
    kv = kv if isinstance(kv, list) else [kv]
    cuts = [sum(w.shape[0] for w in kv[:i]) for i in range(len(kv) + 1)]

    def kernel(stream_ref, *refs):
        key_ref, value_ref, state_ref, total_ref = refs[-4:]
        for r in range(blocks):
            both = sum(dot(stream_ref[r, :, cuts[i] : cuts[i + 1]], refs[i][...]) for i in range(len(kv)))
            key_ref[r] = silu(both[:, :HDIM]).astype(BF16)
            value_ref[r] = both[:, HDIM:].astype(BF16)
        added = jnp.zeros((HDIM, HDIM), F32) if total is None else refs[len(kv)][...]
        for r in range(blocks):
            state = dot(key_ref[r], value_ref[r], ((0,), (0,)))
            state_ref[r] = state
            added = added + state
        total_ref[...] = added

    shape = jax.ShapeDtypeStruct((blocks, rows, HDIM), BF16)
    state = jax.ShapeDtypeStruct((blocks, HDIM, HDIM), F32)
    shapes = [shape, shape, state, jax.ShapeDtypeStruct((HDIM, HDIM), F32)]
    args = [stream, *kv] + ([] if total is None else [total])
    flops = 4 * blocks * rows * width * HDIM
    return call(kernel, "project", shapes, [VMEM] * len(args), [VMEM] * 4, LIMIT, flops, 2 * MIB)(*args)


def queries(place, streams, pieces):
    _, rows, width = streams[0].shape
    count = len(pieces)
    depth = pieces[0].shape[0]

    def kernel(place_ref, *refs):
        sources, ins = refs[: len(streams)], refs[len(streams) : len(streams) + count]
        out, w_held = refs[-2:]
        for m, piece in enumerate(ins):
            row = pl.multiple_of(jnp.bitwise_xor(place_ref[3], m) * depth, depth)
            w_held[pl.ds(row, depth), :] = piece[...]
        swap = place_ref[1] == 1
        blocks = [(source, r) for source in sources for r in range(source.shape[0])]
        for i, (source, r) in enumerate(blocks):
            both = silu(dot(source[r], w_held[...])).astype(BF16)
            out[i, :, :HDIM] = jnp.where(swap, both[:, HDIM:], both[:, :HDIM])
            out[i, :, HDIM:] = jnp.where(swap, both[:, :HDIM], both[:, HDIM:])

    shape = jax.ShapeDtypeStruct((SUB, rows, 2 * HDIM), BF16)
    flops = 4 * SUB * rows * width * HDIM
    held = pltpu.VMEM((width, 2 * HDIM), BF16)
    specs = [SMEM] + [VMEM] * (len(streams) + count)
    return call(kernel, "queries", shape, specs, VMEM, LIMIT, flops, 2 * MIB, [held])(place, *streams, *pieces)


def attend(place, blocks, query, heads):
    rows = query.shape[1]
    count = len(blocks)
    flat, where = [], []
    for parts, carried in heads:
        index = []
        for part in parts:
            index += [(len(flat), r) for r in range(part[0].shape[0])]
            flat += part
        where.append((index, len(flat)))
        flat.append(carried)

    def kernel(place_ref, query_ref, *refs):
        ins, outs = refs[: len(flat)], refs[len(flat) :]
        causal = lax.broadcasted_iota(jnp.int32, (rows, rows), 1) <= lax.broadcasted_iota(
            jnp.int32, (rows, rows), 0
        )
        block = place_ref[0]
        for i, r in enumerate(blocks):
            for h, (index, carried) in enumerate(where):
                earlier = ins[carried][...]
                for other in range(SUB):
                    if other != r:
                        is_before = jnp.bitwise_xor(block, other) < jnp.bitwise_xor(block, r)
                        slot, j = index[other]
                        earlier = earlier + jnp.where(is_before, ins[slot + 2][j], 0.0)
                slot, j = index[r]
                key, value = ins[slot][j], ins[slot + 1][j]
                q = query_ref[r, :, h * HDIM : (h + 1) * HDIM]
                scores = dot(q, key, ((1,), (1,)))
                weights = jnp.where(causal, scores, 0.0).astype(BF16)
                mixed = dot(weights, value) + dot(q, earlier.astype(BF16))
                scale = lax.rsqrt(jnp.mean(mixed * mixed, axis=-1, keepdims=True) + 1e-06)
                target = pl.multiple_of(jnp.bitwise_xor(place_ref[1], h) * HDIM, HDIM)
                outs[i][:, pl.ds(target, HDIM)] = (mixed * scale).astype(BF16)

    shapes = [jax.ShapeDtypeStruct((rows, 2 * HDIM), BF16)] * count
    flops = count * 4 * rows * HDIM * (2 * rows + HDIM)
    specs = [SMEM] + [VMEM] * (1 + len(flat))
    return call(kernel, "attend", shapes, specs, [VMEM] * count, LIMIT, flops, 2 * MIB)(place, query, *flat)


def add_features(pieces, weight, partial=None):
    rows, depth = pieces[0].shape
    width = weight.shape[2]
    count = len(pieces)
    tile = min(512, width)

    def kernel(*refs):
        w_ref, out = refs[count], refs[-1]
        for start in range(0, width, tile):
            columns = slice(start, start + tile)
            total = refs[count + 1][:, columns] if partial is not None else jnp.zeros((rows, tile), F32)
            for i in range(count):
                total = total + dot(refs[i][...], w_ref[i, :, columns])
            out[:, columns] = total.astype(out.dtype)

    shape = pltpu.VMEM((rows, width), F32) if partial is None else jax.ShapeDtypeStruct((rows, width), BF16)
    args = [*pieces, weight] + ([] if partial is None else [partial])
    flops = 2 * count * depth * rows * width
    return call(kernel, "add_features", shape, [VMEM] * len(args), VMEM, LIMIT, flops, 8 * MIB)(*args)


def exclusive_prefix(value, groups):
    def shift(v, step):
        pairs = [(g * SUB + j, (g + step) * SUB + j) for g in range(groups - step) for j in range(SUB)]
        return lax.ppermute(v, "ctx", pairs)

    if groups == 1:
        return jnp.zeros_like(value)
    total = shift(value, 1)
    step = 1
    while step < groups - 1:
        total = total + shift(total, step)
        step *= 2
    return total


def local(tokens, w_query, w_key, w_value, w_out):
    n_ctx = lax.axis_size("ctx")
    groups = n_ctx // SUB
    rows, half = tokens.shape
    ctx = lax.axis_index("ctx")
    place = jnp.stack([ctx % SUB, lax.axis_index("groups"), lax.axis_index("head"), ctx]).astype(jnp.int32)

    def xor(value, step):
        return lax.ppermute(value, "ctx", [(i, i ^ step) for i in range(n_ctx)])

    def other_part(value):
        return lax.ppermute(value, "groups", [(0, 1), (1, 0)])

    def other_core(value):
        return lax.ppermute(value, "head", [(0, 1), (1, 0)])

    def spread(packed):
        return lax.all_to_all(packed, "ctx", 0, 0, tiled=True)

    def gather_queries(sent):
        block = ctx % SUB
        ordered = [lax.dynamic_index_in_dim(jnp.stack(sent), block ^ j, keepdims=False) for j in range(SUB)]
        whole = spread(jnp.concatenate(ordered * groups, axis=0)).reshape(n_ctx, -1, 2 * HDIM)
        return [lax.dynamic_index_in_dim(whole, ctx ^ m, keepdims=False) for m in range(n_ctx)]

    def both_cores(value):
        return lax.all_gather(value, "head", axis=1, tiled=True)

    cut = half * 11 // 16 // HDIM * HDIM
    across = xor(tokens, 2)
    beside = xor(tokens, 1)
    far_tokens = other_core(tokens)
    far_tokens, w_key, w_value = lax.optimization_barrier((far_tokens, w_key, w_value))
    kv_mine = spread(pack_keys_values(place, w_key, w_value, n_ctx))
    across, beside, kv_mine, w_query, w_out = lax.optimization_barrier((across, beside, kv_mine, w_query, w_out))
    middle = kv_mine.shape[0] // 2
    kv_upper = other_part(kv_mine[:middle])
    left = xor(across[:, :cut], 1)
    right = xor(beside[:, cut:], 2)
    q_sent = pack_queries(place, w_query)
    near = [(tokens, 0, 0, 0), (far_tokens, 0, 0, 1), (both_cores(beside), 1, 0, None), (both_cores(across), 2, 0, None)]
    near = stage(place, near, SUB - 1, rows, 2 * half)
    first = project(near, kv_mine)
    arrived = {m: xor(q_sent[m % SUB], m) for m in (4, 6)} if n_ctx == 2 * SUB else {}
    w_sent = take_rows(place, w_out)
    left, right, arrived, q_sent, w_sent, kv_upper, kv_mine, first = lax.optimization_barrier(
        (left, right, arrived, q_sent, w_sent, kv_upper, kv_mine, first)
    )
    kv_lower = other_part(kv_mine[middle:])
    corner = []
    for array, column in ((left, 0), (right, cut)):
        corner += [(array, 0, column, 0), (other_core(array), 0, column, 1)]
    corner = stage(place, corner, 1, rows, 2 * half)
    last = project(corner, kv_mine, first[3])
    if n_ctx == 2 * SUB:
        arrived = arrived | {m: xor(q_sent[m % SUB], m) for m in (5, 7, 2, 3, 1)}
        arrived, kv_lower, last, w_sent = lax.optimization_barrier((arrived, kv_lower, last, w_sent))
        q_pieces = [q_sent[0]] + [arrived[m] for m in range(1, n_ctx)]
    else:
        q_pieces = gather_queries(q_sent)
    w_far = other_core(w_sent)

    def head(near_part, corner_part):
        return [near_part[:3], corner_part[:3]], exclusive_prefix(corner_part[3], groups)

    kv_other = [kv_upper, kv_lower]
    second = project(near, kv_other)
    heads = [head(first, last), head(second, project(corner, kv_other, second[3]))]
    query = queries(place, [near, corner], q_pieces)
    away = attend(place, (3, 1, 2), query, heads)
    home = attend(place, (0,), query, heads)
    normed = [home[0], xor(away[1], 1), xor(away[2], 2), xor(away[0], 3)]
    home_0, w_far = lax.optimization_barrier((home[0], w_far))
    out_keep, out_far = stage_rows(place, w_out, w_far)
    out_keep, out_far, *normed = lax.optimization_barrier((out_keep, out_far, home_0, *normed[1:]))
    partial = add_features(normed, out_keep)
    return add_features([other_core(n) for n in normed], out_far, partial)


def solution(mesh):
    in_specs = (
        P(("groups", "ctx"), "head"),
        P("ctx", "head"),
        P("ctx", "head"),
        P("ctx", "head"),
        P("head", None),
    )
    out_specs = P(("groups", "ctx"), "head")
    return jax.shard_map(local, mesh=mesh, in_specs=in_specs, out_specs=out_specs, check_vma=False)
```

```python
import jax
import jax.numpy as jnp
from jax import lax
from jax.experimental import pallas as pl
from jax.experimental.pallas import tpu as pltpu
from jax.sharding import PartitionSpec as P

HDIM = 128
SUB = 4
F32 = jnp.float32
BF16 = jnp.bfloat16
MIB = 1 << 20
LIMIT = 8
ANY = pl.BlockSpec(memory_space=pl.ANY)
VMEM = pl.BlockSpec(memory_space=pltpu.VMEM)
SMEM = pl.BlockSpec(memory_space=pltpu.SMEM)


def dot(a, b, contract=((1,), (0,))):
    return lax.dot_general(a, b, (contract, ((), ())), preferred_element_type=F32)


def silu(u):
    return u / (1.0 + jnp.exp(-u))


def call(kernel, name, out_shape, in_specs, out_specs, limit, flops, moved, scratch=()):
    return pl.pallas_call(
        kernel,
        out_shape=out_shape,
        in_specs=in_specs,
        out_specs=out_specs,
        scratch_shapes=list(scratch),
        compiler_params=pltpu.CompilerParams(vmem_limit_bytes=limit * MIB),
        cost_estimate=pl.CostEstimate(flops=int(flops), bytes_accessed=int(moved), transcendentals=0),
        name=name,
    )


def pack_keys_values(place, w_key, w_value, count):
    depth = w_key.shape[0]

    def kernel(place_ref, key_ref, value_ref, out):
        for j in range(SUB):
            start = pl.multiple_of((2 * j + place_ref[1]) * HDIM, HDIM)
            key = key_ref[:, pl.ds(start, HDIM)]
            value = value_ref[:, pl.ds(start, HDIM)]
            for i in range(j, count, SUB):
                out[i * depth : (i + 1) * depth, :HDIM] = key
                out[i * depth : (i + 1) * depth, HDIM:] = value

    shape = jax.ShapeDtypeStruct((count * depth, 2 * HDIM), BF16)
    moved = count * depth * 2 * HDIM * 4
    return call(kernel, "pack_keys_values", shape, [SMEM, VMEM, VMEM], VMEM, LIMIT, 0, moved)(place, w_key, w_value)


def pack_queries(place, w_query):
    depth = w_query.shape[0]

    def kernel(place_ref, query_ref, *outs):
        for r, out in enumerate(outs):
            start = pl.multiple_of(jnp.bitwise_xor(place_ref[0], r) * 2 * HDIM, 2 * HDIM)
            out[...] = query_ref[:, pl.ds(start, 2 * HDIM)]

    shapes = [jax.ShapeDtypeStruct((depth, 2 * HDIM), BF16)] * SUB
    moved = SUB * depth * 2 * HDIM * 4
    return call(kernel, "pack_queries", shapes, [SMEM, VMEM], [VMEM] * SUB, LIMIT, 0, moved)(place, w_query)


def stage_rows(place, w_out, w_far):
    rows, width = w_out.shape
    depth, half = rows // SUB, width // 2

    def kernel(place_ref, out_ref, far_ref, keep, far, sems):
        column = pl.multiple_of(place_ref[2] * half, half)
        copies = []
        for r in range(SUB):
            row = pl.multiple_of(jnp.bitwise_xor(place_ref[0], r) * depth, depth)
            for i, (source, target) in enumerate(((out_ref, keep), (far_ref, far))):
                block = source.at[pl.ds(row, depth), pl.ds(column, half)]
                copies.append(pltpu.make_async_copy(block, target.at[r], sems.at[2 * r + i]))
        for copy in copies:
            copy.start()
        for copy in copies:
            copy.wait()

    shapes = [pltpu.VMEM((SUB, depth, half), BF16)] * 2
    sems = pltpu.SemaphoreType.DMA((2 * SUB,))
    return call(kernel, "stage_rows", shapes, [SMEM, ANY, ANY], [VMEM] * 2, 40, 0, rows * width * 4, [sems])(
        place, w_out, w_far
    )


def stage(place, pieces, blocks, rows, width):
    count = len(pieces)
    half = width // 2

    def kernel(place_ref, *refs):
        out, sems = refs[count], refs[count + 1]
        copies = []
        for i, ((array, r, column, far), ref) in enumerate(zip(pieces, refs)):
            if far is None:
                target = out.at[r]
            else:
                core = 1 - place_ref[2] if far else place_ref[2]
                start = pl.multiple_of(core * half + column, HDIM)
                target = out.at[r, :, pl.ds(start, array.shape[1])]
            copies.append(pltpu.make_async_copy(ref, target, sems.at[i]))
        for copy in copies:
            copy.start()
        for copy in copies:
            copy.wait()

    shape = pltpu.VMEM((blocks, rows, width), BF16)
    sems = pltpu.SemaphoreType.DMA((count,))
    moved = blocks * rows * width * 4
    return call(kernel, "stage", shape, [SMEM] + [ANY] * count, VMEM, 36 if blocks > 1 else LIMIT, 0, moved, [sems])(
        place, *[piece[0] for piece in pieces]
    )


def project(stream, kv, total=None):
    blocks, rows, width = stream.shape
    kv = kv if isinstance(kv, list) else [kv]
    cuts = [sum(w.shape[0] for w in kv[:i]) for i in range(len(kv) + 1)]

    def kernel(stream_ref, *refs):
        key_ref, value_ref, state_ref, total_ref = refs[-4:]
        for r in range(blocks):
            both = sum(dot(stream_ref[r, :, cuts[i] : cuts[i + 1]], refs[i][...]) for i in range(len(kv)))
            key_ref[r] = silu(both[:, :HDIM]).astype(BF16)
            value_ref[r] = both[:, HDIM:].astype(BF16)
        added = jnp.zeros((HDIM, HDIM), F32) if total is None else refs[len(kv)][...]
        for r in range(blocks):
            state = dot(key_ref[r], value_ref[r], ((0,), (0,)))
            state_ref[r] = state
            added = added + state
        total_ref[...] = added

    shape = jax.ShapeDtypeStruct((blocks, rows, HDIM), BF16)
    state = jax.ShapeDtypeStruct((blocks, HDIM, HDIM), F32)
    shapes = [shape, shape, state, jax.ShapeDtypeStruct((HDIM, HDIM), F32)]
    args = [stream, *kv] + ([] if total is None else [total])
    flops = 4 * blocks * rows * width * HDIM
    return call(kernel, "project", shapes, [VMEM] * len(args), [VMEM] * 4, LIMIT, flops, 2 * MIB)(*args)


def queries(place, streams, pieces):
    _, rows, width = streams[0].shape
    count = len(pieces)
    depth = pieces[0].shape[0]

    def kernel(place_ref, *refs):
        sources, ins = refs[: len(streams)], refs[len(streams) : len(streams) + count]
        out, w_held = refs[-2:]
        for m, piece in enumerate(ins):
            row = pl.multiple_of(jnp.bitwise_xor(place_ref[3], m) * depth, depth)
            w_held[pl.ds(row, depth), :] = piece[...]
        swap = place_ref[1] == 1
        blocks = [(source, r) for source in sources for r in range(source.shape[0])]
        for i, (source, r) in enumerate(blocks):
            both = silu(dot(source[r], w_held[...])).astype(BF16)
            out[i, :, :HDIM] = jnp.where(swap, both[:, HDIM:], both[:, :HDIM])
            out[i, :, HDIM:] = jnp.where(swap, both[:, :HDIM], both[:, HDIM:])

    shape = jax.ShapeDtypeStruct((SUB, rows, 2 * HDIM), BF16)
    flops = 4 * SUB * rows * width * HDIM
    held = pltpu.VMEM((width, 2 * HDIM), BF16)
    specs = [SMEM] + [VMEM] * (len(streams) + count)
    return call(kernel, "queries", shape, specs, VMEM, LIMIT, flops, 2 * MIB, [held])(place, *streams, *pieces)


def attend(place, blocks, query, heads):
    rows = query.shape[1]
    count = len(blocks)
    flat, where = [], []
    for parts, carried in heads:
        index = []
        for part in parts:
            index += [(len(flat), r) for r in range(part[0].shape[0])]
            flat += part
        where.append((index, len(flat)))
        flat.append(carried)

    def kernel(place_ref, query_ref, *refs):
        ins, outs = refs[: len(flat)], refs[len(flat) :]
        causal = lax.broadcasted_iota(jnp.int32, (rows, rows), 1) <= lax.broadcasted_iota(
            jnp.int32, (rows, rows), 0
        )
        block = place_ref[0]
        for i, r in enumerate(blocks):
            for h, (index, carried) in enumerate(where):
                earlier = ins[carried][...]
                for other in range(SUB):
                    if other != r:
                        is_before = jnp.bitwise_xor(block, other) < jnp.bitwise_xor(block, r)
                        slot, j = index[other]
                        earlier = earlier + jnp.where(is_before, ins[slot + 2][j], 0.0)
                slot, j = index[r]
                key, value = ins[slot][j], ins[slot + 1][j]
                q = query_ref[r, :, h * HDIM : (h + 1) * HDIM]
                scores = dot(q, key, ((1,), (1,)))
                weights = jnp.where(causal, scores, 0.0).astype(BF16)
                mixed = dot(weights, value) + dot(q, earlier.astype(BF16))
                scale = lax.rsqrt(jnp.mean(mixed * mixed, axis=-1, keepdims=True) + 1e-06)
                target = pl.multiple_of(jnp.bitwise_xor(place_ref[1], h) * HDIM, HDIM)
                outs[i][:, pl.ds(target, HDIM)] = (mixed * scale).astype(BF16)

    shapes = [jax.ShapeDtypeStruct((rows, 2 * HDIM), BF16)] * count
    flops = count * 4 * rows * HDIM * (2 * rows + HDIM)
    specs = [SMEM] + [VMEM] * (1 + len(flat))
    return call(kernel, "attend", shapes, specs, [VMEM] * count, LIMIT, flops, 2 * MIB)(place, query, *flat)


def add_features(pieces, weight, partial=None):
    rows, depth = pieces[0].shape
    width = weight.shape[2]
    count = len(pieces)
    tile = min(512, width)

    def kernel(*refs):
        w_ref, out = refs[count], refs[-1]
        for start in range(0, width, tile):
            columns = slice(start, start + tile)
            total = refs[count + 1][:, columns] if partial is not None else jnp.zeros((rows, tile), F32)
            for i in range(count):
                total = total + dot(refs[i][...], w_ref[i, :, columns])
            out[:, columns] = total.astype(out.dtype)

    shape = pltpu.VMEM((rows, width), F32) if partial is None else jax.ShapeDtypeStruct((rows, width), BF16)
    args = [*pieces, weight] + ([] if partial is None else [partial])
    flops = 2 * count * depth * rows * width
    return call(kernel, "add_features", shape, [VMEM] * len(args), VMEM, LIMIT, flops, 8 * MIB)(*args)


def exclusive_prefix(value, groups):
    def shift(v, step):
        pairs = [(g * SUB + j, (g + step) * SUB + j) for g in range(groups - step) for j in range(SUB)]
        return lax.ppermute(v, "ctx", pairs)

    if groups == 1:
        return jnp.zeros_like(value)
    total = shift(value, 1)
    step = 1
    while step < groups - 1:
        total = total + shift(total, step)
        step *= 2
    return total


def local(tokens, w_query, w_key, w_value, w_out):
    n_ctx = lax.axis_size("ctx")
    groups = n_ctx // SUB
    rows, half = tokens.shape
    ctx = lax.axis_index("ctx")
    place = jnp.stack([ctx % SUB, lax.axis_index("groups"), lax.axis_index("head"), ctx]).astype(jnp.int32)

    def xor(value, step):
        return lax.ppermute(value, "ctx", [(i, i ^ step) for i in range(n_ctx)])

    def other_part(value):
        return lax.ppermute(value, "groups", [(0, 1), (1, 0)])

    def other_core(value):
        return lax.ppermute(value, "head", [(0, 1), (1, 0)])

    def spread(packed):
        return lax.all_to_all(packed, "ctx", 0, 0, tiled=True)

    def gather_queries(sent):
        block = ctx % SUB
        ordered = [lax.dynamic_index_in_dim(jnp.stack(sent), block ^ j, keepdims=False) for j in range(SUB)]
        whole = spread(jnp.concatenate(ordered * groups, axis=0)).reshape(n_ctx, -1, 2 * HDIM)
        return [lax.dynamic_index_in_dim(whole, ctx ^ m, keepdims=False) for m in range(n_ctx)]

    cut = half * 11 // 16 // HDIM * HDIM
    across = xor(tokens, 2)
    beside = xor(tokens, 1)
    kv_mine = spread(pack_keys_values(place, w_key, w_value, n_ctx))
    q_sent = pack_queries(place, w_query)
    far_tokens = other_core(tokens)
    far_beside = other_core(beside)
    w_far = other_core(w_out)
    across, beside, kv_mine, q_sent, far_tokens, far_beside, w_far = lax.optimization_barrier(
        (across, beside, kv_mine, q_sent, far_tokens, far_beside, w_far)
    )
    kv_other = other_part(kv_mine)
    left = xor(across[:, :cut], 1)
    right = xor(beside[:, cut:], 2)
    near = [(tokens, 0, 0, 0), (far_tokens, 0, 0, 1), (beside, 1, 0, 0), (far_beside, 1, 0, 1)]
    near += [(lax.all_gather(across, "head", axis=1, tiled=True), 2, 0, None)]
    near = stage(place, near, SUB - 1, rows, 2 * half)
    if n_ctx == 2 * SUB:
        arrived = {0: q_sent[0]} | {m: xor(q_sent[m % SUB], m) for m in (4, 6)}
        left, right, arrived, q_sent = lax.optimization_barrier((left, right, arrived, q_sent))
        arrived = arrived | {m: xor(q_sent[m % SUB], m) for m in (5, 7)}
    far_left, far_right = other_core(left), other_core(right)
    if n_ctx == 2 * SUB:
        far_left, q_sent = lax.optimization_barrier((far_left, q_sent))
        arrived = arrived | {m: xor(q_sent[m % SUB], m) for m in (3, 2, 1)}
        q_pieces = [arrived[m] for m in range(n_ctx)]
    else:
        q_pieces = gather_queries(q_sent)
    corner = [(left, 0, 0, 0), (far_left, 0, 0, 1), (right, 0, cut, 0), (far_right, 0, cut, 1)]
    corner = stage(place, corner, 1, rows, 2 * half)

    def head(parts):
        return [part[:3] for part in parts], exclusive_prefix(parts[-1][3], groups)

    first = project(near, kv_mine)
    last = project(corner, kv_mine, first[3])
    kv_other, last = lax.optimization_barrier((kv_other, last))
    second = project(near, kv_other)
    heads = [head([first, last]), head([second, project(corner, kv_other, second[3])])]
    query = queries(place, [near, corner], q_pieces)
    away = attend(place, (3, 1, 2), query, heads)
    home = attend(place, (0,), query, heads)
    normed = [home[0], xor(away[1], 1), xor(away[2], 2), xor(away[0], 3)]
    home_0, w_far = lax.optimization_barrier((home[0], w_far))
    out_keep, out_far = stage_rows(place, w_out, w_far)
    out_keep, out_far, *normed = lax.optimization_barrier((out_keep, out_far, home_0, *normed[1:]))
    partial = add_features(normed, out_keep)
    return add_features([other_core(n) for n in normed], out_far, partial)


def solution(mesh):
    in_specs = (
        P(("groups", "ctx"), "head"),
        P("ctx", "head"),
        P("ctx", "head"),
        P("ctx", "head"),
        P("head", None),
    )
    out_specs = P(("groups", "ctx"), "head")
    return jax.shard_map(local, mesh=mesh, in_specs=in_specs, out_specs=out_specs, check_vma=False)
```

```python
import jax
import jax.numpy as jnp
from jax import lax
from jax.experimental import pallas as pl
from jax.experimental.pallas import tpu as pltpu
from jax.sharding import PartitionSpec as P

HDIM = 128
SUB = 4
F32 = jnp.float32
BF16 = jnp.bfloat16
MIB = 1 << 20
LIMIT = 8
ANY = pl.BlockSpec(memory_space=pl.ANY)
VMEM = pl.BlockSpec(memory_space=pltpu.VMEM)
SMEM = pl.BlockSpec(memory_space=pltpu.SMEM)


def dot(a, b, contract=((1,), (0,))):
    return lax.dot_general(a, b, (contract, ((), ())), preferred_element_type=F32)


def silu(u):
    return u / (1.0 + jnp.exp(-u))


def call(kernel, name, out_shape, in_specs, out_specs, limit, flops, moved, scratch=()):
    return pl.pallas_call(
        kernel,
        out_shape=out_shape,
        in_specs=in_specs,
        out_specs=out_specs,
        scratch_shapes=list(scratch),
        compiler_params=pltpu.CompilerParams(vmem_limit_bytes=limit * MIB),
        cost_estimate=pl.CostEstimate(flops=int(flops), bytes_accessed=int(moved), transcendentals=0),
        name=name,
    )


def pack_keys_values(place, w_key, w_value, count):
    depth = w_key.shape[0]

    def kernel(place_ref, key_ref, value_ref, out):
        for j in range(SUB):
            start = pl.multiple_of((2 * j + place_ref[1]) * HDIM, HDIM)
            key = key_ref[:, pl.ds(start, HDIM)]
            value = value_ref[:, pl.ds(start, HDIM)]
            for i in range(j, count, SUB):
                out[i * depth : (i + 1) * depth, :HDIM] = key
                out[i * depth : (i + 1) * depth, HDIM:] = value

    shape = jax.ShapeDtypeStruct((count * depth, 2 * HDIM), BF16)
    moved = count * depth * 2 * HDIM * 4
    return call(kernel, "pack_keys_values", shape, [SMEM, VMEM, VMEM], VMEM, LIMIT, 0, moved)(place, w_key, w_value)


def pack_queries(place, w_query):
    depth = w_query.shape[0]

    def kernel(place_ref, query_ref, *outs):
        for r, out in enumerate(outs):
            start = pl.multiple_of(jnp.bitwise_xor(place_ref[0], r) * 2 * HDIM, 2 * HDIM)
            out[...] = query_ref[:, pl.ds(start, 2 * HDIM)]

    shapes = [jax.ShapeDtypeStruct((depth, 2 * HDIM), BF16)] * SUB
    moved = SUB * depth * 2 * HDIM * 4
    return call(kernel, "pack_queries", shapes, [SMEM, VMEM], [VMEM] * SUB, LIMIT, 0, moved)(place, w_query)


def stage_rows(place, w_out, w_far):
    rows, width = w_out.shape
    depth, half = rows // SUB, width // 2

    def kernel(place_ref, out_ref, far_ref, keep, far, sems):
        column = pl.multiple_of(place_ref[2] * half, half)
        copies = []
        for r in range(SUB):
            row = pl.multiple_of(jnp.bitwise_xor(place_ref[0], r) * depth, depth)
            for i, (source, target) in enumerate(((out_ref, keep), (far_ref, far))):
                block = source.at[pl.ds(row, depth), pl.ds(column, half)]
                copies.append(pltpu.make_async_copy(block, target.at[r], sems.at[2 * r + i]))
        for copy in copies:
            copy.start()
        for copy in copies:
            copy.wait()

    shapes = [pltpu.VMEM((SUB, depth, half), BF16)] * 2
    sems = pltpu.SemaphoreType.DMA((2 * SUB,))
    return call(kernel, "stage_rows", shapes, [SMEM, ANY, ANY], [VMEM] * 2, 40, 0, rows * width * 4, [sems])(
        place, w_out, w_far
    )


def stage(place, pieces, blocks, rows, width):
    count = len(pieces)
    half = width // 2

    def kernel(place_ref, *refs):
        out, sems = refs[count], refs[count + 1]
        copies = []
        for i, ((array, r, column, far), ref) in enumerate(zip(pieces, refs)):
            if far is None:
                target = out.at[r]
            else:
                core = 1 - place_ref[2] if far else place_ref[2]
                start = pl.multiple_of(core * half + column, HDIM)
                target = out.at[r, :, pl.ds(start, array.shape[1])]
            copies.append(pltpu.make_async_copy(ref, target, sems.at[i]))
        for copy in copies:
            copy.start()
        for copy in copies:
            copy.wait()

    shape = pltpu.VMEM((blocks, rows, width), BF16)
    sems = pltpu.SemaphoreType.DMA((count,))
    moved = blocks * rows * width * 4
    return call(kernel, "stage", shape, [SMEM] + [ANY] * count, VMEM, 20 if blocks > 1 else LIMIT, 0, moved, [sems])(
        place, *[piece[0] for piece in pieces]
    )


def project(stream, kv, total=None):
    blocks, rows, width = stream.shape
    kv = kv if isinstance(kv, list) else [kv]
    cuts = [sum(w.shape[0] for w in kv[:i]) for i in range(len(kv) + 1)]

    def kernel(stream_ref, *refs):
        key_ref, value_ref, state_ref, total_ref = refs[-4:]
        for r in range(blocks):
            both = sum(dot(stream_ref[r, :, cuts[i] : cuts[i + 1]], refs[i][...]) for i in range(len(kv)))
            key_ref[r] = silu(both[:, :HDIM]).astype(BF16)
            value_ref[r] = both[:, HDIM:].astype(BF16)
        added = jnp.zeros((HDIM, HDIM), F32) if total is None else refs[len(kv)][...]
        for r in range(blocks):
            state = dot(key_ref[r], value_ref[r], ((0,), (0,)))
            state_ref[r] = state
            added = added + state
        total_ref[...] = added

    shape = jax.ShapeDtypeStruct((blocks, rows, HDIM), BF16)
    state = jax.ShapeDtypeStruct((blocks, HDIM, HDIM), F32)
    shapes = [shape, shape, state, jax.ShapeDtypeStruct((HDIM, HDIM), F32)]
    args = [stream, *kv] + ([] if total is None else [total])
    flops = 4 * blocks * rows * width * HDIM
    return call(kernel, "project", shapes, [VMEM] * len(args), [VMEM] * 4, LIMIT, flops, 2 * MIB)(*args)


def queries(place, streams, pieces):
    _, rows, width = streams[0].shape
    count = len(pieces)
    depth = pieces[0].shape[0]

    def kernel(place_ref, *refs):
        sources, ins = refs[: len(streams)], refs[len(streams) : len(streams) + count]
        out, w_held = refs[-2:]
        for m, piece in enumerate(ins):
            row = pl.multiple_of(jnp.bitwise_xor(place_ref[3], m) * depth, depth)
            w_held[pl.ds(row, depth), :] = piece[...]
        swap = place_ref[1] == 1
        blocks = [(source, r) for source in sources for r in range(source.shape[0])]
        for i, (source, r) in enumerate(blocks):
            both = silu(dot(source[r], w_held[...])).astype(BF16)
            out[i, :, :HDIM] = jnp.where(swap, both[:, HDIM:], both[:, :HDIM])
            out[i, :, HDIM:] = jnp.where(swap, both[:, :HDIM], both[:, HDIM:])

    shape = jax.ShapeDtypeStruct((SUB, rows, 2 * HDIM), BF16)
    flops = 4 * SUB * rows * width * HDIM
    held = pltpu.VMEM((width, 2 * HDIM), BF16)
    specs = [SMEM] + [VMEM] * (len(streams) + count)
    return call(kernel, "queries", shape, specs, VMEM, LIMIT, flops, 2 * MIB, [held])(place, *streams, *pieces)


def attend(place, blocks, query, heads):
    rows = query.shape[1]
    count = len(blocks)
    flat, where = [], []
    for parts, carried in heads:
        index = []
        for part in parts:
            index += [(len(flat), r) for r in range(part[0].shape[0])]
            flat += part
        where.append((index, len(flat)))
        flat.append(carried)

    def kernel(place_ref, query_ref, *refs):
        ins, outs = refs[: len(flat)], refs[len(flat) :]
        causal = lax.broadcasted_iota(jnp.int32, (rows, rows), 1) <= lax.broadcasted_iota(
            jnp.int32, (rows, rows), 0
        )
        block = place_ref[0]
        for i, r in enumerate(blocks):
            for h, (index, carried) in enumerate(where):
                earlier = ins[carried][...]
                for other in range(SUB):
                    if other != r:
                        is_before = jnp.bitwise_xor(block, other) < jnp.bitwise_xor(block, r)
                        slot, j = index[other]
                        earlier = earlier + jnp.where(is_before, ins[slot + 2][j], 0.0)
                slot, j = index[r]
                key, value = ins[slot][j], ins[slot + 1][j]
                q = query_ref[r, :, h * HDIM : (h + 1) * HDIM]
                scores = dot(q, key, ((1,), (1,)))
                weights = jnp.where(causal, scores, 0.0).astype(BF16)
                mixed = dot(weights, value) + dot(q, earlier.astype(BF16))
                scale = lax.rsqrt(jnp.mean(mixed * mixed, axis=-1, keepdims=True) + 1e-06)
                target = pl.multiple_of(jnp.bitwise_xor(place_ref[1], h) * HDIM, HDIM)
                outs[i][:, pl.ds(target, HDIM)] = (mixed * scale).astype(BF16)

    shapes = [jax.ShapeDtypeStruct((rows, 2 * HDIM), BF16)] * count
    flops = count * 4 * rows * HDIM * (2 * rows + HDIM)
    specs = [SMEM] + [VMEM] * (1 + len(flat))
    return call(kernel, "attend", shapes, specs, [VMEM] * count, LIMIT, flops, 2 * MIB)(place, query, *flat)


def add_features(pieces, weight, partial=None):
    rows, depth = pieces[0].shape
    width = weight.shape[2]
    count = len(pieces)
    tile = min(512, width)

    def kernel(*refs):
        w_ref, out = refs[count], refs[-1]
        for start in range(0, width, tile):
            columns = slice(start, start + tile)
            total = refs[count + 1][:, columns] if partial is not None else jnp.zeros((rows, tile), F32)
            for i in range(count):
                total = total + dot(refs[i][...], w_ref[i, :, columns])
            out[:, columns] = total.astype(out.dtype)

    shape = pltpu.VMEM((rows, width), F32) if partial is None else jax.ShapeDtypeStruct((rows, width), BF16)
    args = [*pieces, weight] + ([] if partial is None else [partial])
    flops = 2 * count * depth * rows * width
    return call(kernel, "add_features", shape, [VMEM] * len(args), VMEM, LIMIT, flops, 8 * MIB)(*args)


def exclusive_prefix(value, groups):
    def shift(v, step):
        pairs = [(g * SUB + j, (g + step) * SUB + j) for g in range(groups - step) for j in range(SUB)]
        return lax.ppermute(v, "ctx", pairs)

    if groups == 1:
        return jnp.zeros_like(value)
    total = shift(value, 1)
    step = 1
    while step < groups - 1:
        total = total + shift(total, step)
        step *= 2
    return total


def local(tokens, w_query, w_key, w_value, w_out):
    n_ctx = lax.axis_size("ctx")
    groups = n_ctx // SUB
    rows, half = tokens.shape
    ctx = lax.axis_index("ctx")
    place = jnp.stack([ctx % SUB, lax.axis_index("groups"), lax.axis_index("head"), ctx]).astype(jnp.int32)

    def xor(value, step):
        return lax.ppermute(value, "ctx", [(i, i ^ step) for i in range(n_ctx)])

    def other_part(value):
        return lax.ppermute(value, "groups", [(0, 1), (1, 0)])

    def other_core(value):
        return lax.ppermute(value, "head", [(0, 1), (1, 0)])

    def spread(packed):
        return lax.all_to_all(packed, "ctx", 0, 0, tiled=True)

    def gather_queries(sent):
        block = ctx % SUB
        ordered = [lax.dynamic_index_in_dim(jnp.stack(sent), block ^ j, keepdims=False) for j in range(SUB)]
        whole = spread(jnp.concatenate(ordered * groups, axis=0)).reshape(n_ctx, -1, 2 * HDIM)
        return [lax.dynamic_index_in_dim(whole, ctx ^ m, keepdims=False) for m in range(n_ctx)]

    cut = half * 11 // 16 // HDIM * HDIM
    across = xor(tokens, 2)
    beside = xor(tokens, 1)
    kv_mine = spread(pack_keys_values(place, w_key, w_value, n_ctx))
    q_sent = pack_queries(place, w_query)
    far_tokens = other_core(tokens)
    far_beside = other_core(beside)
    w_far = other_core(w_out)
    across, beside, kv_mine, q_sent, far_tokens, far_beside, w_far = lax.optimization_barrier(
        (across, beside, kv_mine, q_sent, far_tokens, far_beside, w_far)
    )
    kv_other = other_part(kv_mine)
    left = xor(across[:, :cut], 1)
    right = xor(beside[:, cut:], 2)
    near = [(tokens, 0, 0, 0), (far_tokens, 0, 0, 1), (beside, 1, 0, 0), (far_beside, 1, 0, 1)]
    near += [(across, 2, 0, 0), (other_core(across), 2, 0, 1)]
    near = stage(place, near, SUB - 1, rows, 2 * half)
    first = project(near, kv_mine)
    if n_ctx == 2 * SUB:
        arrived = {0: q_sent[0]} | {m: xor(q_sent[m % SUB], m) for m in (4, 6)}
        left, right, arrived, q_sent, first = lax.optimization_barrier((left, right, arrived, q_sent, first))
        arrived = arrived | {m: xor(q_sent[m % SUB], m) for m in (5, 7)}
    far_left, far_right = other_core(left), other_core(right)
    if n_ctx == 2 * SUB:
        far_left, q_sent = lax.optimization_barrier((far_left, q_sent))
        arrived = arrived | {m: xor(q_sent[m % SUB], m) for m in (3, 2, 1)}
        arrived, kv_other = lax.optimization_barrier((arrived, kv_other))
        q_pieces = [arrived[m] for m in range(n_ctx)]
    else:
        q_pieces = gather_queries(q_sent)
    corner = [(left, 0, 0, 0), (far_left, 0, 0, 1), (right, 0, cut, 0), (far_right, 0, cut, 1)]
    corner = stage(place, corner, 1, rows, 2 * half)

    def head(parts):
        return [part[:3] for part in parts], exclusive_prefix(parts[-1][3], groups)

    last = project(corner, kv_mine, first[3])
    kv_other, last = lax.optimization_barrier((kv_other, last))
    second = project(near, kv_other)
    heads = [head([first, last]), head([second, project(corner, kv_other, second[3])])]
    query = queries(place, [near, corner], q_pieces)
    away = attend(place, (3, 1, 2), query, heads)
    home = attend(place, (0,), query, heads)
    normed = [home[0], xor(away[1], 1), xor(away[2], 2), xor(away[0], 3)]
    home_0, w_far = lax.optimization_barrier((home[0], w_far))
    out_keep, out_far = stage_rows(place, w_out, w_far)
    out_keep, out_far, *normed = lax.optimization_barrier((out_keep, out_far, home_0, *normed[1:]))
    partial = add_features(normed, out_keep)
    return add_features([other_core(n) for n in normed], out_far, partial)


def solution(mesh):
    in_specs = (
        P(("groups", "ctx"), "head"),
        P("ctx", "head"),
        P("ctx", "head"),
        P("ctx", "head"),
        P("head", None),
    )
    out_specs = P(("groups", "ctx"), "head")
    return jax.shard_map(local, mesh=mesh, in_specs=in_specs, out_specs=out_specs, check_vma=False)
```

```python
import jax
import jax.numpy as jnp
from jax import lax
from jax.experimental import pallas as pl
from jax.experimental.pallas import tpu as pltpu
from jax.sharding import PartitionSpec as P

HDIM = 128
SUB = 4
F32 = jnp.float32
BF16 = jnp.bfloat16
MIB = 1 << 20
LIMIT = 8
ANY = pl.BlockSpec(memory_space=pl.ANY)
VMEM = pl.BlockSpec(memory_space=pltpu.VMEM)
SMEM = pl.BlockSpec(memory_space=pltpu.SMEM)


def dot(a, b, contract=((1,), (0,))):
    return lax.dot_general(a, b, (contract, ((), ())), preferred_element_type=F32)


def silu(u):
    return u / (1.0 + jnp.exp(-u))


def call(kernel, name, out_shape, in_specs, out_specs, limit, flops, moved, scratch=()):
    return pl.pallas_call(
        kernel,
        out_shape=out_shape,
        in_specs=in_specs,
        out_specs=out_specs,
        scratch_shapes=list(scratch),
        compiler_params=pltpu.CompilerParams(vmem_limit_bytes=limit * MIB),
        cost_estimate=pl.CostEstimate(flops=int(flops), bytes_accessed=int(moved), transcendentals=0),
        name=name,
    )


def pack_keys_values(place, w_key, w_value, count):
    depth = w_key.shape[0]

    def kernel(place_ref, key_ref, value_ref, out):
        for j in range(SUB):
            start = pl.multiple_of((2 * j + place_ref[1]) * HDIM, HDIM)
            key = key_ref[:, pl.ds(start, HDIM)]
            value = value_ref[:, pl.ds(start, HDIM)]
            for i in range(j, count, SUB):
                out[i * depth : (i + 1) * depth, :HDIM] = key
                out[i * depth : (i + 1) * depth, HDIM:] = value

    shape = jax.ShapeDtypeStruct((count * depth, 2 * HDIM), BF16)
    moved = count * depth * 2 * HDIM * 4
    return call(kernel, "pack_keys_values", shape, [SMEM, VMEM, VMEM], VMEM, LIMIT, 0, moved)(place, w_key, w_value)


def pack_queries(place, w_query):
    depth = w_query.shape[0]

    def kernel(place_ref, query_ref, *outs):
        for r, out in enumerate(outs):
            start = pl.multiple_of(jnp.bitwise_xor(place_ref[0], r) * 2 * HDIM, 2 * HDIM)
            out[...] = query_ref[:, pl.ds(start, 2 * HDIM)]

    shapes = [jax.ShapeDtypeStruct((depth, 2 * HDIM), BF16)] * SUB
    moved = SUB * depth * 2 * HDIM * 4
    return call(kernel, "pack_queries", shapes, [SMEM, VMEM], [VMEM] * SUB, LIMIT, 0, moved)(place, w_query)


def stage_rows(place, w_out, w_far):
    rows, width = w_out.shape
    depth, half = rows // SUB, width // 2

    def kernel(place_ref, out_ref, far_ref, keep, far, sems):
        column = pl.multiple_of(place_ref[2] * half, half)
        copies = []
        for r in range(SUB):
            row = pl.multiple_of(jnp.bitwise_xor(place_ref[0], r) * depth, depth)
            for i, (source, target) in enumerate(((out_ref, keep), (far_ref, far))):
                block = source.at[pl.ds(row, depth), pl.ds(column, half)]
                copies.append(pltpu.make_async_copy(block, target.at[r], sems.at[2 * r + i]))
        for copy in copies:
            copy.start()
        for copy in copies:
            copy.wait()

    shapes = [pltpu.VMEM((SUB, depth, half), BF16)] * 2
    sems = pltpu.SemaphoreType.DMA((2 * SUB,))
    return call(kernel, "stage_rows", shapes, [SMEM, ANY, ANY], [VMEM] * 2, 40, 0, rows * width * 4, [sems])(
        place, w_out, w_far
    )


def stage(place, pieces, blocks, rows, width):
    count = len(pieces)
    half = width // 2

    def kernel(place_ref, *refs):
        out, sems = refs[count], refs[count + 1]
        copies = []
        for i, ((array, r, column, far), ref) in enumerate(zip(pieces, refs)):
            if far is None:
                target = out.at[r]
            else:
                core = 1 - place_ref[2] if far else place_ref[2]
                start = pl.multiple_of(core * half + column, HDIM)
                target = out.at[r, :, pl.ds(start, array.shape[1])]
            copies.append(pltpu.make_async_copy(ref, target, sems.at[i]))
        for copy in copies:
            copy.start()
        for copy in copies:
            copy.wait()

    shape = pltpu.VMEM((blocks, rows, width), BF16)
    sems = pltpu.SemaphoreType.DMA((count,))
    moved = blocks * rows * width * 4
    return call(kernel, "stage", shape, [SMEM] + [ANY] * count, VMEM, 20 if blocks > 1 else LIMIT, 0, moved, [sems])(
        place, *[piece[0] for piece in pieces]
    )


def project(stream, kv, total=None):
    blocks, rows, width = stream.shape
    kv = kv if isinstance(kv, list) else [kv]
    cuts = [sum(w.shape[0] for w in kv[:i]) for i in range(len(kv) + 1)]

    def kernel(stream_ref, *refs):
        key_ref, value_ref, state_ref, total_ref = refs[-4:]
        for r in range(blocks):
            both = sum(dot(stream_ref[r, :, cuts[i] : cuts[i + 1]], refs[i][...]) for i in range(len(kv)))
            key_ref[r] = silu(both[:, :HDIM]).astype(BF16)
            value_ref[r] = both[:, HDIM:].astype(BF16)
        added = jnp.zeros((HDIM, HDIM), F32) if total is None else refs[len(kv)][...]
        for r in range(blocks):
            state = dot(key_ref[r], value_ref[r], ((0,), (0,)))
            state_ref[r] = state
            added = added + state
        total_ref[...] = added

    shape = jax.ShapeDtypeStruct((blocks, rows, HDIM), BF16)
    state = jax.ShapeDtypeStruct((blocks, HDIM, HDIM), F32)
    shapes = [shape, shape, state, jax.ShapeDtypeStruct((HDIM, HDIM), F32)]
    args = [stream, *kv] + ([] if total is None else [total])
    flops = 4 * blocks * rows * width * HDIM
    return call(kernel, "project", shapes, [VMEM] * len(args), [VMEM] * 4, LIMIT, flops, 2 * MIB)(*args)


def queries(place, streams, pieces):
    _, rows, width = streams[0].shape
    count = len(pieces)
    depth = pieces[0].shape[0]

    def kernel(place_ref, *refs):
        sources, ins = refs[: len(streams)], refs[len(streams) : len(streams) + count]
        out, w_held = refs[-2:]
        for m, piece in enumerate(ins):
            row = pl.multiple_of(jnp.bitwise_xor(place_ref[3], m) * depth, depth)
            w_held[pl.ds(row, depth), :] = piece[...]
        swap = place_ref[1] == 1
        blocks = [(source, r) for source in sources for r in range(source.shape[0])]
        for i, (source, r) in enumerate(blocks):
            both = silu(dot(source[r], w_held[...])).astype(BF16)
            out[i, :, :HDIM] = jnp.where(swap, both[:, HDIM:], both[:, :HDIM])
            out[i, :, HDIM:] = jnp.where(swap, both[:, :HDIM], both[:, HDIM:])

    shape = jax.ShapeDtypeStruct((SUB, rows, 2 * HDIM), BF16)
    flops = 4 * SUB * rows * width * HDIM
    held = pltpu.VMEM((width, 2 * HDIM), BF16)
    specs = [SMEM] + [VMEM] * (len(streams) + count)
    return call(kernel, "queries", shape, specs, VMEM, LIMIT, flops, 2 * MIB, [held])(place, *streams, *pieces)


def attend(place, blocks, query, heads):
    rows = query.shape[1]
    count = len(blocks)
    flat, where = [], []
    for parts, carried in heads:
        index = []
        for part in parts:
            index += [(len(flat), r) for r in range(part[0].shape[0])]
            flat += part
        where.append((index, len(flat)))
        flat.append(carried)

    def kernel(place_ref, query_ref, *refs):
        ins, outs = refs[: len(flat)], refs[len(flat) :]
        causal = lax.broadcasted_iota(jnp.int32, (rows, rows), 1) <= lax.broadcasted_iota(
            jnp.int32, (rows, rows), 0
        )
        block = place_ref[0]
        for i, r in enumerate(blocks):
            for h, (index, carried) in enumerate(where):
                earlier = ins[carried][...]
                for other in range(SUB):
                    if other != r:
                        is_before = jnp.bitwise_xor(block, other) < jnp.bitwise_xor(block, r)
                        slot, j = index[other]
                        earlier = earlier + jnp.where(is_before, ins[slot + 2][j], 0.0)
                slot, j = index[r]
                key, value = ins[slot][j], ins[slot + 1][j]
                q = query_ref[r, :, h * HDIM : (h + 1) * HDIM]
                scores = dot(q, key, ((1,), (1,)))
                weights = jnp.where(causal, scores, 0.0).astype(BF16)
                mixed = dot(weights, value) + dot(q, earlier.astype(BF16))
                scale = lax.rsqrt(jnp.mean(mixed * mixed, axis=-1, keepdims=True) + 1e-06)
                target = pl.multiple_of(jnp.bitwise_xor(place_ref[1], h) * HDIM, HDIM)
                outs[i][:, pl.ds(target, HDIM)] = (mixed * scale).astype(BF16)

    shapes = [jax.ShapeDtypeStruct((rows, 2 * HDIM), BF16)] * count
    flops = count * 4 * rows * HDIM * (2 * rows + HDIM)
    specs = [SMEM] + [VMEM] * (1 + len(flat))
    return call(kernel, "attend", shapes, specs, [VMEM] * count, LIMIT, flops, 2 * MIB)(place, query, *flat)


def add_features(pieces, weight, partial=None):
    rows, depth = pieces[0].shape
    width = weight.shape[2]
    count = len(pieces)
    tile = min(512, width)

    def kernel(*refs):
        w_ref, out = refs[count], refs[-1]
        for start in range(0, width, tile):
            columns = slice(start, start + tile)
            total = refs[count + 1][:, columns] if partial is not None else jnp.zeros((rows, tile), F32)
            for i in range(count):
                total = total + dot(refs[i][...], w_ref[i, :, columns])
            out[:, columns] = total.astype(out.dtype)

    shape = pltpu.VMEM((rows, width), F32) if partial is None else jax.ShapeDtypeStruct((rows, width), BF16)
    args = [*pieces, weight] + ([] if partial is None else [partial])
    flops = 2 * count * depth * rows * width
    return call(kernel, "add_features", shape, [VMEM] * len(args), VMEM, LIMIT, flops, 8 * MIB)(*args)


def exclusive_prefix(value, groups):
    def shift(v, step):
        pairs = [(g * SUB + j, (g + step) * SUB + j) for g in range(groups - step) for j in range(SUB)]
        return lax.ppermute(v, "ctx", pairs)

    if groups == 1:
        return jnp.zeros_like(value)
    total = shift(value, 1)
    step = 1
    while step < groups - 1:
        total = total + shift(total, step)
        step *= 2
    return total


def local(tokens, w_query, w_key, w_value, w_out):
    n_ctx = lax.axis_size("ctx")
    groups = n_ctx // SUB
    rows, half = tokens.shape
    ctx = lax.axis_index("ctx")
    place = jnp.stack([ctx % SUB, lax.axis_index("groups"), lax.axis_index("head"), ctx]).astype(jnp.int32)

    def xor(value, step):
        return lax.ppermute(value, "ctx", [(i, i ^ step) for i in range(n_ctx)])

    def other_part(value):
        return lax.ppermute(value, "groups", [(0, 1), (1, 0)])

    def other_core(value):
        return lax.ppermute(value, "head", [(0, 1), (1, 0)])

    def spread(packed):
        return lax.all_to_all(packed, "ctx", 0, 0, tiled=True)

    def gather_queries(sent):
        block = ctx % SUB
        ordered = [lax.dynamic_index_in_dim(jnp.stack(sent), block ^ j, keepdims=False) for j in range(SUB)]
        whole = spread(jnp.concatenate(ordered * groups, axis=0)).reshape(n_ctx, -1, 2 * HDIM)
        return [lax.dynamic_index_in_dim(whole, ctx ^ m, keepdims=False) for m in range(n_ctx)]

    cut = half * 11 // 16 // HDIM * HDIM
    pieced = n_ctx == 2 * SUB
    ob = lax.optimization_barrier

    across = xor(tokens, 2)
    beside = xor(tokens, 1)
    kv_mine = spread(pack_keys_values(place, w_key, w_value, n_ctx))
    far_tokens = other_core(tokens)
    w_far = other_core(w_out)
    beside, far_tokens, w_far, w_query = ob((beside, far_tokens, w_far, w_query))
    q_sent = pack_queries(place, w_query)
    far_beside = other_core(beside)

    def fetch(sent, *steps):
        if pieced:
            arrived.update({m: xor(sent[m % SUB], m) for m in steps})

    across, kv_mine, beside, far_beside, q_sent = ob((across, kv_mine, beside, far_beside, q_sent))
    arrived = {0: q_sent[0]}
    middle = kv_mine.shape[0] // 2
    kv_upper = other_part(kv_mine[:middle])
    left = xor(across[:, :cut], 1)
    right = xor(beside[:, cut:], 2)
    fetch(q_sent, 4, 6)
    left, right, arrived, kv_upper, kv_mine, across, q_sent = ob(
        (left, right, arrived, kv_upper, kv_mine, across, q_sent)
    )
    kv_lower = other_part(kv_mine[middle:])
    fetch(q_sent, 5, 7, 3, 2, 1)
    near = [(tokens, 0, 0, 0), (far_tokens, 0, 0, 1), (beside, 1, 0, 0), (far_beside, 1, 0, 1)]
    near += [(across, 2, 0, 0), (other_core(across), 2, 0, 1)]
    near = stage(place, near, SUB - 1, rows, 2 * half)
    corner = []
    for array, column in ((left, 0), (right, cut)):
        corner += [(array, 0, column, 0), (other_core(array), 0, column, 1)]
    corner = stage(place, corner, 1, rows, 2 * half)

    def head(parts):
        return [part[:3] for part in parts], exclusive_prefix(parts[-1][3], groups)

    first = project(near, kv_mine)
    last = project(corner, kv_mine, first[3])
    arrived, kv_lower, last = ob((arrived, kv_lower, last))
    q_pieces = [arrived[m] for m in range(n_ctx)] if pieced else gather_queries(q_sent)
    kv_other = [kv_upper, kv_lower]
    second = project(near, kv_other)
    heads = [head([first, last]), head([second, project(corner, kv_other, second[3])])]
    query = queries(place, [near, corner], q_pieces)
    away = attend(place, (3, 1, 2), query, heads)
    home = attend(place, (0,), query, heads)
    normed = [home[0], xor(away[1], 1), xor(away[2], 2), xor(away[0], 3)]
    home_0, w_far = lax.optimization_barrier((home[0], w_far))
    out_keep, out_far = stage_rows(place, w_out, w_far)
    out_keep, out_far, *normed = lax.optimization_barrier((out_keep, out_far, home_0, *normed[1:]))
    partial = add_features(normed, out_keep)
    return add_features([other_core(n) for n in normed], out_far, partial)


def solution(mesh):
    in_specs = (
        P(("groups", "ctx"), "head"),
        P("ctx", "head"),
        P("ctx", "head"),
        P("ctx", "head"),
        P("head", None),
    )
    out_specs = P(("groups", "ctx"), "head")
    return jax.shard_map(local, mesh=mesh, in_specs=in_specs, out_specs=out_specs, check_vma=False)
```

```python
import jax
import jax.numpy as jnp
from jax import lax
from jax.experimental import pallas as pl
from jax.experimental.pallas import tpu as pltpu
from jax.sharding import PartitionSpec as P

HDIM = 128
SUB = 4
F32 = jnp.float32
BF16 = jnp.bfloat16
MIB = 1 << 20
LIMIT = 8
ANY = pl.BlockSpec(memory_space=pl.ANY)
VMEM = pl.BlockSpec(memory_space=pltpu.VMEM)
SMEM = pl.BlockSpec(memory_space=pltpu.SMEM)


def dot(a, b, contract=((1,), (0,))):
    return lax.dot_general(a, b, (contract, ((), ())), preferred_element_type=F32)


def silu(u):
    return u / (1.0 + jnp.exp(-u))


def call(kernel, name, out_shape, in_specs, out_specs, limit, flops, moved, scratch=()):
    return pl.pallas_call(
        kernel,
        out_shape=out_shape,
        in_specs=in_specs,
        out_specs=out_specs,
        scratch_shapes=list(scratch),
        compiler_params=pltpu.CompilerParams(vmem_limit_bytes=limit * MIB),
        cost_estimate=pl.CostEstimate(flops=int(flops), bytes_accessed=int(moved), transcendentals=0),
        name=name,
    )


def pack_keys_values(place, w_key, w_value, count):
    depth = w_key.shape[0]

    def kernel(place_ref, key_ref, value_ref, out):
        for j in range(SUB):
            start = pl.multiple_of((2 * j + place_ref[1]) * HDIM, HDIM)
            key = key_ref[:, pl.ds(start, HDIM)]
            value = value_ref[:, pl.ds(start, HDIM)]
            for i in range(j, count, SUB):
                out[i * depth : (i + 1) * depth, :HDIM] = key
                out[i * depth : (i + 1) * depth, HDIM:] = value

    shape = jax.ShapeDtypeStruct((count * depth, 2 * HDIM), BF16)
    moved = count * depth * 2 * HDIM * 4
    return call(kernel, "pack_keys_values", shape, [SMEM, VMEM, VMEM], VMEM, LIMIT, 0, moved)(place, w_key, w_value)


def pack_queries(place, w_query):
    depth = w_query.shape[0]

    def kernel(place_ref, query_ref, *outs):
        for r, out in enumerate(outs):
            start = pl.multiple_of(jnp.bitwise_xor(place_ref[0], r) * 2 * HDIM, 2 * HDIM)
            out[...] = query_ref[:, pl.ds(start, 2 * HDIM)]

    shapes = [jax.ShapeDtypeStruct((depth, 2 * HDIM), BF16)] * SUB
    moved = SUB * depth * 2 * HDIM * 4
    return call(kernel, "pack_queries", shapes, [SMEM, VMEM], [VMEM] * SUB, LIMIT, 0, moved)(place, w_query)


def stage_rows(place, w_out, w_far):
    rows, width = w_out.shape
    depth, half = rows // SUB, width // 2

    def kernel(place_ref, out_ref, far_ref, keep, far, sems):
        column = pl.multiple_of(place_ref[2] * half, half)
        copies = []
        for r in range(SUB):
            row = pl.multiple_of(jnp.bitwise_xor(place_ref[0], r) * depth, depth)
            for i, (source, target) in enumerate(((out_ref, keep), (far_ref, far))):
                block = source.at[pl.ds(row, depth), pl.ds(column, half)]
                copies.append(pltpu.make_async_copy(block, target.at[r], sems.at[2 * r + i]))
        for copy in copies:
            copy.start()
        for copy in copies:
            copy.wait()

    shapes = [pltpu.VMEM((SUB, depth, half), BF16)] * 2
    sems = pltpu.SemaphoreType.DMA((2 * SUB,))
    return call(kernel, "stage_rows", shapes, [SMEM, ANY, ANY], [VMEM] * 2, 40, 0, rows * width * 4, [sems])(
        place, w_out, w_far
    )


def stage(place, pieces, blocks, rows, width):
    count = len(pieces)
    half = width // 2

    def kernel(place_ref, *refs):
        out, sems = refs[count], refs[count + 1]
        copies = []
        for i, ((array, r, column, far), ref) in enumerate(zip(pieces, refs)):
            if far is None:
                target = out.at[r]
            else:
                core = 1 - place_ref[2] if far else place_ref[2]
                start = pl.multiple_of(core * half + column, HDIM)
                target = out.at[r, :, pl.ds(start, array.shape[1])]
            copies.append(pltpu.make_async_copy(ref, target, sems.at[i]))
        for copy in copies:
            copy.start()
        for copy in copies:
            copy.wait()

    shape = pltpu.VMEM((blocks, rows, width), BF16)
    sems = pltpu.SemaphoreType.DMA((count,))
    moved = blocks * rows * width * 4
    return call(kernel, "stage", shape, [SMEM] + [ANY] * count, VMEM, 20 if blocks > 1 else LIMIT, 0, moved, [sems])(
        place, *[piece[0] for piece in pieces]
    )


def project(stream, kv, total=None):
    blocks, rows, width = stream.shape
    kv = kv if isinstance(kv, list) else [kv]
    cuts = [sum(w.shape[0] for w in kv[:i]) for i in range(len(kv) + 1)]

    def kernel(stream_ref, *refs):
        key_ref, value_ref, state_ref, total_ref = refs[-4:]
        for r in range(blocks):
            both = sum(dot(stream_ref[r, :, cuts[i] : cuts[i + 1]], refs[i][...]) for i in range(len(kv)))
            key_ref[r] = silu(both[:, :HDIM]).astype(BF16)
            value_ref[r] = both[:, HDIM:].astype(BF16)
        added = jnp.zeros((HDIM, HDIM), F32) if total is None else refs[len(kv)][...]
        for r in range(blocks):
            state = dot(key_ref[r], value_ref[r], ((0,), (0,)))
            state_ref[r] = state
            added = added + state
        total_ref[...] = added

    shape = jax.ShapeDtypeStruct((blocks, rows, HDIM), BF16)
    state = jax.ShapeDtypeStruct((blocks, HDIM, HDIM), F32)
    shapes = [shape, shape, state, jax.ShapeDtypeStruct((HDIM, HDIM), F32)]
    args = [stream, *kv] + ([] if total is None else [total])
    flops = 4 * blocks * rows * width * HDIM
    return call(kernel, "project", shapes, [VMEM] * len(args), [VMEM] * 4, LIMIT, flops, 2 * MIB)(*args)


def flat_blocks(streams):
    return [(stream, r) for stream in streams for r in range(stream.shape[0])]


def weighted(place_ref, source, r, refs, parts, base):
    total = base
    for ref, (weight, start) in zip(refs, parts):
        depth = weight.shape[0]
        if isinstance(start, tuple):
            lanes = pl.ds(pl.multiple_of(jnp.bitwise_xor(place_ref[3], start[0]) * depth, HDIM), depth)
        else:
            lanes = slice(start, start + depth)
        term = dot(source[r, :, lanes], ref[...])
        total = term if total is None else total + term
    return total


def run_blocks(kernel, name, place, streams, parts, base, out_shape):
    rows, width = streams[0].shape[1:]
    count = len(streams)
    args = [*streams, *[weight for weight, _ in parts], *([] if base is None else [base])]

    def body(place_ref, *refs):
        weights = refs[count : count + len(parts)]
        base_ref = None if base is None else refs[len(args) - 1]

        def sums():
            for i, (source, r) in enumerate(flat_blocks(refs[:count])):
                yield i, weighted(place_ref, source, r, weights, parts, None if base is None else base_ref[i])

        kernel(place_ref, sums, *refs[len(args) :])

    flops = 4 * SUB * rows * sum(weight.shape[0] for weight, _ in parts) * HDIM
    specs = [SMEM] + [VMEM] * len(args)
    outs = [VMEM] * len(out_shape) if isinstance(out_shape, list) else VMEM
    return call(body, name, out_shape, specs, outs, LIMIT, flops, 2 * MIB)(place, *args)


def begin(place, streams, parts):
    def kernel(place_ref, sums, out):
        for i, total in sums():
            out[i] = total

    shape = pltpu.VMEM((SUB, streams[0].shape[1], 2 * HDIM), F32)
    return run_blocks(kernel, "begin", place, streams, parts, None, shape)


def keys_values(place, streams, parts, base):
    rows = streams[0].shape[1]

    def kernel(place_ref, sums, key_ref, value_ref, state_ref, total_ref):
        for i, both in sums():
            key_ref[i] = silu(both[:, :HDIM]).astype(BF16)
            value_ref[i] = both[:, HDIM:].astype(BF16)
        added = jnp.zeros((HDIM, HDIM), F32)
        for i in range(SUB):
            state = dot(key_ref[i], value_ref[i], ((0,), (0,)))
            state_ref[i] = state
            added = added + state
        total_ref[...] = added

    shape = jax.ShapeDtypeStruct((SUB, rows, HDIM), BF16)
    shapes = [shape, shape, jax.ShapeDtypeStruct((SUB, HDIM, HDIM), F32), jax.ShapeDtypeStruct((HDIM, HDIM), F32)]
    return run_blocks(kernel, "keys_values", place, streams, parts, base, shapes)


def queries(place, streams, parts, base):
    def kernel(place_ref, sums, out):
        swap = place_ref[1] == 1
        for i, total in sums():
            both = silu(total).astype(BF16)
            out[i, :, :HDIM] = jnp.where(swap, both[:, HDIM:], both[:, :HDIM])
            out[i, :, HDIM:] = jnp.where(swap, both[:, :HDIM], both[:, HDIM:])

    shape = jax.ShapeDtypeStruct((SUB, streams[0].shape[1], 2 * HDIM), BF16)
    return run_blocks(kernel, "queries", place, streams, parts, base, shape)


def attend(place, blocks, query, heads):
    rows = query.shape[1]
    count = len(blocks)
    flat, where = [], []
    for parts, carried in heads:
        index = []
        for part in parts:
            index += [(len(flat), r) for r in range(part[0].shape[0])]
            flat += part
        where.append((index, len(flat)))
        flat.append(carried)

    def kernel(place_ref, query_ref, *refs):
        ins, outs = refs[: len(flat)], refs[len(flat) :]
        causal = lax.broadcasted_iota(jnp.int32, (rows, rows), 1) <= lax.broadcasted_iota(
            jnp.int32, (rows, rows), 0
        )
        block = place_ref[0]
        for i, r in enumerate(blocks):
            for h, (index, carried) in enumerate(where):
                earlier = ins[carried][...]
                for other in range(SUB):
                    if other != r:
                        is_before = jnp.bitwise_xor(block, other) < jnp.bitwise_xor(block, r)
                        slot, j = index[other]
                        earlier = earlier + jnp.where(is_before, ins[slot + 2][j], 0.0)
                slot, j = index[r]
                key, value = ins[slot][j], ins[slot + 1][j]
                q = query_ref[r, :, h * HDIM : (h + 1) * HDIM]
                scores = dot(q, key, ((1,), (1,)))
                weights = jnp.where(causal, scores, 0.0).astype(BF16)
                mixed = dot(weights, value) + dot(q, earlier.astype(BF16))
                scale = lax.rsqrt(jnp.mean(mixed * mixed, axis=-1, keepdims=True) + 1e-06)
                target = pl.multiple_of(jnp.bitwise_xor(place_ref[1], h) * HDIM, HDIM)
                outs[i][:, pl.ds(target, HDIM)] = (mixed * scale).astype(BF16)

    shapes = [jax.ShapeDtypeStruct((rows, 2 * HDIM), BF16)] * count
    flops = count * 4 * rows * HDIM * (2 * rows + HDIM)
    specs = [SMEM] + [VMEM] * (1 + len(flat))
    return call(kernel, "attend", shapes, specs, [VMEM] * count, LIMIT, flops, 2 * MIB)(place, query, *flat)


def add_features(pieces, weight, partial=None):
    rows, depth = pieces[0].shape
    width = weight.shape[2]
    count = len(pieces)
    tile = min(512, width)

    def kernel(*refs):
        w_ref, out = refs[count], refs[-1]
        for start in range(0, width, tile):
            columns = slice(start, start + tile)
            total = refs[count + 1][:, columns] if partial is not None else jnp.zeros((rows, tile), F32)
            for i in range(count):
                total = total + dot(refs[i][...], w_ref[i, :, columns])
            out[:, columns] = total.astype(out.dtype)

    shape = pltpu.VMEM((rows, width), F32) if partial is None else jax.ShapeDtypeStruct((rows, width), BF16)
    args = [*pieces, weight] + ([] if partial is None else [partial])
    flops = 2 * count * depth * rows * width
    return call(kernel, "add_features", shape, [VMEM] * len(args), VMEM, LIMIT, flops, 8 * MIB)(*args)


def exclusive_prefix(value, groups):
    def shift(v, step):
        pairs = [(g * SUB + j, (g + step) * SUB + j) for g in range(groups - step) for j in range(SUB)]
        return lax.ppermute(v, "ctx", pairs)

    if groups == 1:
        return jnp.zeros_like(value)
    total = shift(value, 1)
    step = 1
    while step < groups - 1:
        total = total + shift(total, step)
        step *= 2
    return total


def local(tokens, w_query, w_key, w_value, w_out):
    n_ctx = lax.axis_size("ctx")
    groups = n_ctx // SUB
    rows, half = tokens.shape
    ctx = lax.axis_index("ctx")
    place = jnp.stack([ctx % SUB, lax.axis_index("groups"), lax.axis_index("head"), ctx]).astype(jnp.int32)

    def xor(value, step):
        return lax.ppermute(value, "ctx", [(i, i ^ step) for i in range(n_ctx)])

    def other_part(value):
        return lax.ppermute(value, "groups", [(0, 1), (1, 0)])

    def other_core(value):
        return lax.ppermute(value, "head", [(0, 1), (1, 0)])

    def spread(packed):
        return lax.all_to_all(packed, "ctx", 0, 0, tiled=True)

    def gather_queries(sent):
        ordered = [lax.dynamic_index_in_dim(jnp.stack(sent), (ctx % SUB) ^ j, keepdims=False) for j in range(SUB)]
        return spread(jnp.concatenate(ordered * groups, axis=0))

    cut = half * 11 // 16 // HDIM * HDIM
    pieced = n_ctx == 2 * SUB
    ob = lax.optimization_barrier

    across = xor(tokens, 2)
    beside = xor(tokens, 1)
    kv_mine = spread(pack_keys_values(place, w_key, w_value, n_ctx))
    far_tokens = other_core(tokens)
    w_far = other_core(w_out)
    beside, far_tokens, w_far, w_query = ob((beside, far_tokens, w_far, w_query))
    q_sent = pack_queries(place, w_query)
    far_beside = other_core(beside)

    def fetch(sent, *steps):
        if pieced:
            arrived.update({m: xor(sent[m % SUB], m) for m in steps})

    across, kv_mine, beside, far_beside, q_sent = ob((across, kv_mine, beside, far_beside, q_sent))
    arrived = {0: q_sent[0]}
    middle = kv_mine.shape[0] // 2
    kv_upper = other_part(kv_mine[:middle])
    left = xor(across[:, :cut], 1)
    right = xor(beside[:, cut:], 2)
    fetch(q_sent, 4, 6)
    near = [(tokens, 0, 0, 0), (far_tokens, 0, 0, 1), (beside, 1, 0, 0), (far_beside, 1, 0, 1)]
    near += [(across, 2, 0, 0), (other_core(across), 2, 0, 1)]
    near = stage(place, near, SUB - 1, rows, 2 * half)
    first = project(near, kv_mine)
    left, right, arrived, kv_upper, kv_mine, q_sent, first = ob(
        (left, right, arrived, kv_upper, kv_mine, q_sent, first)
    )
    kv_lower = other_part(kv_mine[middle:])
    fetch(q_sent, 5, 7)
    far_left, far_right = other_core(left), other_core(right)
    far_left, q_sent = ob((far_left, q_sent))
    fetch(q_sent, 3, 2, 1)
    corner = [(left, 0, 0, 0), (far_left, 0, 0, 1), (right, 0, cut, 0), (far_right, 0, cut, 1)]
    corner = stage(place, corner, 1, rows, 2 * half)

    streams = [near, corner]
    last = project(corner, kv_mine, first[3])
    carried = exclusive_prefix(last[3], groups)
    kv_base = begin(place, streams, [(kv_upper, 0)])
    if pieced:
        early = (0, 4, 6)
        q_base = begin(place, streams, [(arrived[m], (m,)) for m in early])
        arrived, kv_lower, carried, kv_base, q_base = ob((arrived, kv_lower, carried, kv_base, q_base))
        q_parts = [(arrived[m], (m,)) for m in range(n_ctx) if m not in early]
    else:
        q_base, q_parts = None, [(gather_queries(q_sent), 0)]
    second = keys_values(place, streams, [(kv_lower, middle)], kv_base)
    heads = [([first[:3], last[:3]], carried), ([second[:3]], exclusive_prefix(second[3], groups))]
    query = queries(place, streams, q_parts, q_base)
    away = attend(place, (3, 1, 2), query, heads)
    home = attend(place, (0,), query, heads)
    normed = [home[0], xor(away[1], 1), xor(away[2], 2), xor(away[0], 3)]
    home_0, w_far = lax.optimization_barrier((home[0], w_far))
    out_keep, out_far = stage_rows(place, w_out, w_far)
    out_keep, out_far, *normed = lax.optimization_barrier((out_keep, out_far, home_0, *normed[1:]))
    partial = add_features(normed, out_keep)
    return add_features([other_core(n) for n in normed], out_far, partial)


def solution(mesh):
    in_specs = (
        P(("groups", "ctx"), "head"),
        P("ctx", "head"),
        P("ctx", "head"),
        P("ctx", "head"),
        P("head", None),
    )
    out_specs = P(("groups", "ctx"), "head")
    return jax.shard_map(local, mesh=mesh, in_specs=in_specs, out_specs=out_specs, check_vma=False)
```

```python
import jax
import jax.numpy as jnp
from jax import lax
from jax.experimental import pallas as pl
from jax.experimental.pallas import tpu as pltpu
from jax.sharding import PartitionSpec as P

HDIM = 128
SUB = 4
F32 = jnp.float32
BF16 = jnp.bfloat16
MIB = 1 << 20
LIMIT = 8
ANY = pl.BlockSpec(memory_space=pl.ANY)
VMEM = pl.BlockSpec(memory_space=pltpu.VMEM)
SMEM = pl.BlockSpec(memory_space=pltpu.SMEM)


def dot(a, b, contract=((1,), (0,))):
    return lax.dot_general(a, b, (contract, ((), ())), preferred_element_type=F32)


def silu(u):
    return u / (1.0 + jnp.exp(-u))


def call(kernel, name, out_shape, in_specs, out_specs, limit, flops, moved, scratch=()):
    return pl.pallas_call(
        kernel,
        out_shape=out_shape,
        in_specs=in_specs,
        out_specs=out_specs,
        scratch_shapes=list(scratch),
        compiler_params=pltpu.CompilerParams(vmem_limit_bytes=limit * MIB),
        cost_estimate=pl.CostEstimate(flops=int(flops), bytes_accessed=int(moved), transcendentals=0),
        name=name,
    )


def pack_keys_values(place, w_key, w_value, count):
    depth = w_key.shape[0]

    def kernel(place_ref, key_ref, value_ref, out):
        for j in range(SUB):
            start = pl.multiple_of((2 * j + place_ref[1]) * HDIM, HDIM)
            key = key_ref[:, pl.ds(start, HDIM)]
            value = value_ref[:, pl.ds(start, HDIM)]
            for i in range(j, count, SUB):
                out[i * depth : (i + 1) * depth, :HDIM] = key
                out[i * depth : (i + 1) * depth, HDIM:] = value

    shape = jax.ShapeDtypeStruct((count * depth, 2 * HDIM), BF16)
    moved = count * depth * 2 * HDIM * 4
    return call(kernel, "pack_keys_values", shape, [SMEM, VMEM, VMEM], VMEM, LIMIT, 0, moved)(place, w_key, w_value)


def pack_queries(place, w_query):
    depth = w_query.shape[0]

    def kernel(place_ref, query_ref, *outs):
        for r, out in enumerate(outs):
            start = pl.multiple_of(jnp.bitwise_xor(place_ref[0], r) * 2 * HDIM, 2 * HDIM)
            out[...] = query_ref[:, pl.ds(start, 2 * HDIM)]

    shapes = [jax.ShapeDtypeStruct((depth, 2 * HDIM), BF16)] * SUB
    moved = SUB * depth * 2 * HDIM * 4
    return call(kernel, "pack_queries", shapes, [SMEM, VMEM], [VMEM] * SUB, LIMIT, 0, moved)(place, w_query)


def stage_rows(place, w_out, w_far):
    rows, width = w_out.shape
    depth, half = rows // SUB, width // 2

    def kernel(place_ref, out_ref, far_ref, keep, far, sems):
        column = pl.multiple_of(place_ref[2] * half, half)
        copies = []
        for r in range(SUB):
            row = pl.multiple_of(jnp.bitwise_xor(place_ref[0], r) * depth, depth)
            for i, (source, target) in enumerate(((out_ref, keep), (far_ref, far))):
                block = source.at[pl.ds(row, depth), pl.ds(column, half)]
                copies.append(pltpu.make_async_copy(block, target.at[r], sems.at[2 * r + i]))
        for copy in copies:
            copy.start()
        for copy in copies:
            copy.wait()

    shapes = [pltpu.VMEM((SUB, depth, half), BF16)] * 2
    sems = pltpu.SemaphoreType.DMA((2 * SUB,))
    return call(kernel, "stage_rows", shapes, [SMEM, ANY, ANY], [VMEM] * 2, 40, 0, rows * width * 4, [sems])(
        place, w_out, w_far
    )


def stage(place, pieces, blocks, rows, width):
    count = len(pieces)
    half = width // 2

    def kernel(place_ref, *refs):
        out, sems = refs[count], refs[count + 1]
        copies = []
        for i, ((array, r, column, far), ref) in enumerate(zip(pieces, refs)):
            if far is None:
                target = out.at[r]
            else:
                core = 1 - place_ref[2] if far else place_ref[2]
                start = pl.multiple_of(core * half + column, HDIM)
                target = out.at[r, :, pl.ds(start, array.shape[1])]
            copies.append(pltpu.make_async_copy(ref, target, sems.at[i]))
        for copy in copies:
            copy.start()
        for copy in copies:
            copy.wait()

    shape = pltpu.VMEM((blocks, rows, width), BF16)
    sems = pltpu.SemaphoreType.DMA((count,))
    moved = blocks * rows * width * 4
    return call(kernel, "stage", shape, [SMEM] + [ANY] * count, VMEM, 20 if blocks > 1 else LIMIT, 0, moved, [sems])(
        place, *[piece[0] for piece in pieces]
    )


def project(stream, kv, total=None):
    blocks, rows, width = stream.shape
    kv = kv if isinstance(kv, list) else [kv]
    cuts = [sum(w.shape[0] for w in kv[:i]) for i in range(len(kv) + 1)]

    def kernel(stream_ref, *refs):
        key_ref, value_ref, state_ref, total_ref = refs[-4:]
        for r in range(blocks):
            both = sum(dot(stream_ref[r, :, cuts[i] : cuts[i + 1]], refs[i][...]) for i in range(len(kv)))
            key_ref[r] = silu(both[:, :HDIM]).astype(BF16)
            value_ref[r] = both[:, HDIM:].astype(BF16)
        added = jnp.zeros((HDIM, HDIM), F32) if total is None else refs[len(kv)][...]
        for r in range(blocks):
            state = dot(key_ref[r], value_ref[r], ((0,), (0,)))
            state_ref[r] = state
            added = added + state
        total_ref[...] = added

    shape = jax.ShapeDtypeStruct((blocks, rows, HDIM), BF16)
    state = jax.ShapeDtypeStruct((blocks, HDIM, HDIM), F32)
    shapes = [shape, shape, state, jax.ShapeDtypeStruct((HDIM, HDIM), F32)]
    args = [stream, *kv] + ([] if total is None else [total])
    flops = 4 * blocks * rows * width * HDIM
    return call(kernel, "project", shapes, [VMEM] * len(args), [VMEM] * 4, LIMIT, flops, 2 * MIB)(*args)


def flat_blocks(streams):
    return [(stream, r) for stream in streams for r in range(stream.shape[0])]


def weighted(place_ref, source, r, refs, parts, base):
    total = base
    for ref, (weight, start) in zip(refs, parts):
        depth = weight.shape[0]
        if isinstance(start, tuple):
            lanes = pl.ds(pl.multiple_of(jnp.bitwise_xor(place_ref[3], start[0]) * depth, HDIM), depth)
        else:
            lanes = slice(start, start + depth)
        term = dot(source[r, :, lanes], ref[...])
        total = term if total is None else total + term
    return total


def run_blocks(kernel, name, place, streams, parts, base, out_shape, more=()):
    rows, width = streams[0].shape[1:]
    count = len(streams)
    args = [*streams, *[weight for weight, _ in parts], *([] if base is None else [base])]
    given = len(args)
    args += more

    def body(place_ref, *refs):
        weights = refs[count : count + len(parts)]
        base_ref = None if base is None else refs[given - 1]

        def sums():
            for i, (source, r) in enumerate(flat_blocks(refs[:count])):
                yield i, weighted(place_ref, source, r, weights, parts, None if base is None else base_ref[i])

        kernel(place_ref, sums, *refs[given:])

    flops = 4 * SUB * rows * sum(weight.shape[0] for weight, _ in parts) * HDIM
    specs = [SMEM] + [VMEM] * len(args)
    outs = [VMEM] * len(out_shape) if isinstance(out_shape, list) else VMEM
    return call(body, name, out_shape, specs, outs, LIMIT, flops, 2 * MIB)(place, *args)


def begin(place, streams, parts):
    def kernel(place_ref, sums, out):
        for i, total in sums():
            out[i] = total

    shape = pltpu.VMEM((SUB, streams[0].shape[1], 2 * HDIM), F32)
    return run_blocks(kernel, "begin", place, streams, parts, None, shape)


def keys_values(place, streams, parts, base, total):
    rows = streams[0].shape[1]

    def kernel(place_ref, sums, given_ref, key_ref, value_ref, state_ref, total_ref):
        for i, both in sums():
            key_ref[i] = silu(both[:, :HDIM]).astype(BF16)
            value_ref[i] = both[:, HDIM:].astype(BF16)
        added = jnp.zeros((HDIM, HDIM), F32)
        for i in range(SUB):
            state = dot(key_ref[i], value_ref[i], ((0,), (0,)))
            state_ref[i] = state
            added = added + state
        total_ref[0] = given_ref[...]
        total_ref[1] = added

    shape = jax.ShapeDtypeStruct((SUB, rows, HDIM), BF16)
    shapes = [shape, shape] + [jax.ShapeDtypeStruct((n, HDIM, HDIM), F32) for n in (SUB, 2)]
    return run_blocks(kernel, "keys_values", place, streams, parts, base, shapes, [total])


def queries(place, streams, parts, base):
    def kernel(place_ref, sums, out):
        swap = place_ref[1] == 1
        for i, total in sums():
            both = silu(total).astype(BF16)
            out[i, :, :HDIM] = jnp.where(swap, both[:, HDIM:], both[:, :HDIM])
            out[i, :, HDIM:] = jnp.where(swap, both[:, :HDIM], both[:, HDIM:])

    shape = jax.ShapeDtypeStruct((SUB, streams[0].shape[1], 2 * HDIM), BF16)
    return run_blocks(kernel, "queries", place, streams, parts, base, shape)


def attend(place, blocks, query, heads, carried):
    rows = query.shape[1]
    count = len(blocks)
    flat, where = [], []
    for parts in heads:
        index = []
        for part in parts:
            index += [(len(flat), r) for r in range(part[0].shape[0])]
            flat += part
        where.append(index)
    flat.append(carried)

    def kernel(place_ref, query_ref, *refs):
        ins, outs = refs[: len(flat)], refs[len(flat) :]
        causal = lax.broadcasted_iota(jnp.int32, (rows, rows), 1) <= lax.broadcasted_iota(
            jnp.int32, (rows, rows), 0
        )
        block = place_ref[0]
        for i, r in enumerate(blocks):
            for h, index in enumerate(where):
                earlier = ins[-1][h]
                for other in range(SUB):
                    if other != r:
                        is_before = jnp.bitwise_xor(block, other) < jnp.bitwise_xor(block, r)
                        slot, j = index[other]
                        earlier = earlier + jnp.where(is_before, ins[slot + 2][j], 0.0)
                slot, j = index[r]
                key, value = ins[slot][j], ins[slot + 1][j]
                q = query_ref[r, :, h * HDIM : (h + 1) * HDIM]
                scores = dot(q, key, ((1,), (1,)))
                weights = jnp.where(causal, scores, 0.0).astype(BF16)
                mixed = dot(weights, value) + dot(q, earlier.astype(BF16))
                scale = lax.rsqrt(jnp.mean(mixed * mixed, axis=-1, keepdims=True) + 1e-06)
                target = pl.multiple_of(jnp.bitwise_xor(place_ref[1], h) * HDIM, HDIM)
                outs[i][:, pl.ds(target, HDIM)] = (mixed * scale).astype(BF16)

    shapes = [jax.ShapeDtypeStruct((rows, 2 * HDIM), BF16)] * count
    flops = count * 4 * rows * HDIM * (2 * rows + HDIM)
    specs = [SMEM] + [VMEM] * (1 + len(flat))
    return call(kernel, "attend", shapes, specs, [VMEM] * count, LIMIT, flops, 2 * MIB)(place, query, *flat)


def add_features(pieces, weight, partial=None):
    rows, depth = pieces[0].shape
    width = weight.shape[2]
    count = len(pieces)
    tile = min(512, width)

    def kernel(*refs):
        w_ref, out = refs[count], refs[-1]
        for start in range(0, width, tile):
            columns = slice(start, start + tile)
            total = refs[count + 1][:, columns] if partial is not None else jnp.zeros((rows, tile), F32)
            for i in range(count):
                total = total + dot(refs[i][...], w_ref[i, :, columns])
            out[:, columns] = total.astype(out.dtype)

    shape = pltpu.VMEM((rows, width), F32) if partial is None else jax.ShapeDtypeStruct((rows, width), BF16)
    args = [*pieces, weight] + ([] if partial is None else [partial])
    flops = 2 * count * depth * rows * width
    return call(kernel, "add_features", shape, [VMEM] * len(args), VMEM, LIMIT, flops, 8 * MIB)(*args)


def exclusive_prefix(value, groups):
    def shift(v, step):
        pairs = [(g * SUB + j, (g + step) * SUB + j) for g in range(groups - step) for j in range(SUB)]
        return lax.ppermute(v, "ctx", pairs)

    if groups == 1:
        return jnp.zeros_like(value)
    total = shift(value, 1)
    step = 1
    while step < groups - 1:
        total = total + shift(total, step)
        step *= 2
    return total


def local(tokens, w_query, w_key, w_value, w_out):
    n_ctx = lax.axis_size("ctx")
    groups = n_ctx // SUB
    rows, half = tokens.shape
    ctx = lax.axis_index("ctx")
    place = jnp.stack([ctx % SUB, lax.axis_index("groups"), lax.axis_index("head"), ctx]).astype(jnp.int32)

    def xor(value, step):
        return lax.ppermute(value, "ctx", [(i, i ^ step) for i in range(n_ctx)])

    def other_part(value):
        return lax.ppermute(value, "groups", [(0, 1), (1, 0)])

    def other_core(value):
        return lax.ppermute(value, "head", [(0, 1), (1, 0)])

    def spread(packed):
        return lax.all_to_all(packed, "ctx", 0, 0, tiled=True)

    def gather_queries(sent):
        ordered = [lax.dynamic_index_in_dim(jnp.stack(sent), (ctx % SUB) ^ j, keepdims=False) for j in range(SUB)]
        return spread(jnp.concatenate(ordered * groups, axis=0))

    cut = half * 11 // 16 // HDIM * HDIM
    pieced = n_ctx == 2 * SUB
    ob = lax.optimization_barrier

    across = xor(tokens, 2)
    beside = xor(tokens, 1)
    kv_mine = spread(pack_keys_values(place, w_key, w_value, n_ctx))
    far_tokens = other_core(tokens)
    w_far = other_core(w_out)
    beside, far_tokens, w_far, w_query = ob((beside, far_tokens, w_far, w_query))
    q_sent = pack_queries(place, w_query)
    far_beside = other_core(beside)

    def fetch(sent, *steps):
        if pieced:
            arrived.update({m: xor(sent[m % SUB], m) for m in steps})

    arrived = {0: q_sent[0]}
    fetch(q_sent, 1)
    across, kv_mine, beside, far_beside, q_sent, arrived = ob((across, kv_mine, beside, far_beside, q_sent, arrived))
    middle = kv_mine.shape[0] // 2
    kv_upper = other_part(kv_mine[:middle])
    left = xor(across[:, :cut], 1)
    right = xor(beside[:, cut:], 2)
    fetch(q_sent, 4, 6)
    near = [(tokens, 0, 0, 0), (far_tokens, 0, 0, 1), (beside, 1, 0, 0), (far_beside, 1, 0, 1)]
    near += [(across, 2, 0, 0), (other_core(across), 2, 0, 1)]
    near = stage(place, near, SUB - 1, rows, 2 * half)
    first = project(near, kv_mine)
    left, right, arrived, kv_upper, kv_mine, q_sent, first = ob(
        (left, right, arrived, kv_upper, kv_mine, q_sent, first)
    )
    kv_lower = other_part(kv_mine[middle:])
    fetch(q_sent, 5, 7)
    far_left, far_right = other_core(left), other_core(right)
    far_left, q_sent = ob((far_left, q_sent))
    fetch(q_sent, 3, 2)
    corner = [(left, 0, 0, 0), (far_left, 0, 0, 1), (right, 0, cut, 0), (far_right, 0, cut, 1)]
    corner = stage(place, corner, 1, rows, 2 * half)

    streams = [near, corner]
    last = project(corner, kv_mine, first[3])
    kv_base = begin(place, streams, [(kv_upper, 0)])
    if pieced:
        early = (0, 1, 4, 6)
        q_base = begin(place, streams, [(arrived[m], (m,)) for m in early])
        arrived, kv_lower, kv_base, q_base = ob((arrived, kv_lower, kv_base, q_base))
        q_parts = [(arrived[m], (m,)) for m in range(n_ctx) if m not in early]
    else:
        q_base, q_parts = None, [(gather_queries(q_sent), 0)]
    *second, totals = keys_values(place, streams, [(kv_lower, middle)], kv_base, last[3])
    carried = exclusive_prefix(totals, groups)
    heads = [[first[:3], last[:3]], [second]]
    query = queries(place, streams, q_parts, q_base)
    away = attend(place, (3, 1, 2), query, heads, carried)
    home = attend(place, (0,), query, heads, carried)
    normed = [home[0], xor(away[1], 1), xor(away[2], 2), xor(away[0], 3)]
    home_0, w_far = lax.optimization_barrier((home[0], w_far))
    out_keep, out_far = stage_rows(place, w_out, w_far)
    out_keep, out_far, *normed = lax.optimization_barrier((out_keep, out_far, home_0, *normed[1:]))
    partial = add_features(normed, out_keep)
    return add_features([other_core(n) for n in normed], out_far, partial)


def solution(mesh):
    in_specs = (
        P(("groups", "ctx"), "head"),
        P("ctx", "head"),
        P("ctx", "head"),
        P("ctx", "head"),
        P("head", None),
    )
    out_specs = P(("groups", "ctx"), "head")
    return jax.shard_map(local, mesh=mesh, in_specs=in_specs, out_specs=out_specs, check_vma=False)
```

```python
import jax
import jax.numpy as jnp
from jax import lax
from jax.experimental import pallas as pl
from jax.experimental.pallas import tpu as pltpu
from jax.sharding import PartitionSpec as P

HDIM = 128
SUB = 4
F32 = jnp.float32
BF16 = jnp.bfloat16
MIB = 1 << 20
LIMIT = 8
ANY = pl.BlockSpec(memory_space=pl.ANY)
VMEM = pl.BlockSpec(memory_space=pltpu.VMEM)
SMEM = pl.BlockSpec(memory_space=pltpu.SMEM)


def dot(a, b, contract=((1,), (0,))):
    return lax.dot_general(a, b, (contract, ((), ())), preferred_element_type=F32)


def silu(u):
    return u / (1.0 + jnp.exp(-u))


def call(kernel, name, out_shape, in_specs, out_specs, limit, flops, moved, scratch=()):
    return pl.pallas_call(
        kernel,
        out_shape=out_shape,
        in_specs=in_specs,
        out_specs=out_specs,
        scratch_shapes=list(scratch),
        compiler_params=pltpu.CompilerParams(vmem_limit_bytes=limit * MIB),
        cost_estimate=pl.CostEstimate(flops=int(flops), bytes_accessed=int(moved), transcendentals=0),
        name=name,
    )


def pack_keys_values(place, w_key, w_value, count):
    depth = w_key.shape[0]

    def kernel(place_ref, key_ref, value_ref, out):
        for j in range(SUB):
            start = pl.multiple_of((2 * j + place_ref[1]) * HDIM, HDIM)
            key = key_ref[:, pl.ds(start, HDIM)]
            value = value_ref[:, pl.ds(start, HDIM)]
            for i in range(j, count, SUB):
                out[i * depth : (i + 1) * depth, :HDIM] = key
                out[i * depth : (i + 1) * depth, HDIM:] = value

    shape = jax.ShapeDtypeStruct((count * depth, 2 * HDIM), BF16)
    moved = count * depth * 2 * HDIM * 4
    return call(kernel, "pack_keys_values", shape, [SMEM, VMEM, VMEM], VMEM, LIMIT, 0, moved)(place, w_key, w_value)


def pack_queries(place, w_query):
    depth = w_query.shape[0]

    def kernel(place_ref, query_ref, *outs):
        for r, out in enumerate(outs):
            start = pl.multiple_of(jnp.bitwise_xor(place_ref[0], r) * 2 * HDIM, 2 * HDIM)
            out[...] = query_ref[:, pl.ds(start, 2 * HDIM)]

    shapes = [jax.ShapeDtypeStruct((depth, 2 * HDIM), BF16)] * SUB
    moved = SUB * depth * 2 * HDIM * 4
    return call(kernel, "pack_queries", shapes, [SMEM, VMEM], [VMEM] * SUB, LIMIT, 0, moved)(place, w_query)


def stage_rows(place, w_out, w_far):
    rows, width = w_out.shape
    depth, half = rows // SUB, width // 2

    def kernel(place_ref, out_ref, far_ref, keep, far, sems):
        column = pl.multiple_of(place_ref[2] * half, half)
        copies = []
        for r in range(SUB):
            row = pl.multiple_of(jnp.bitwise_xor(place_ref[0], r) * depth, depth)
            for i, (source, target) in enumerate(((out_ref, keep), (far_ref, far))):
                block = source.at[pl.ds(row, depth), pl.ds(column, half)]
                copies.append(pltpu.make_async_copy(block, target.at[r], sems.at[2 * r + i]))
        for copy in copies:
            copy.start()
        for copy in copies:
            copy.wait()

    shapes = [pltpu.VMEM((SUB, depth, half), BF16)] * 2
    sems = pltpu.SemaphoreType.DMA((2 * SUB,))
    return call(kernel, "stage_rows", shapes, [SMEM, ANY, ANY], [VMEM] * 2, 40, 0, rows * width * 4, [sems])(
        place, w_out, w_far
    )


def stage(place, pieces, blocks, rows, width):
    count = len(pieces)
    half = width // 2

    def kernel(place_ref, *refs):
        out, sems = refs[count], refs[count + 1]
        copies = []
        for i, ((array, r, column, far), ref) in enumerate(zip(pieces, refs)):
            if far is None:
                target = out.at[r]
            else:
                core = 1 - place_ref[2] if far else place_ref[2]
                start = pl.multiple_of(core * half + column, HDIM)
                target = out.at[r, :, pl.ds(start, array.shape[1])]
            copies.append(pltpu.make_async_copy(ref, target, sems.at[i]))
        for copy in copies:
            copy.start()
        for copy in copies:
            copy.wait()

    shape = pltpu.VMEM((blocks, rows, width), BF16)
    sems = pltpu.SemaphoreType.DMA((count,))
    moved = blocks * rows * width * 4
    return call(kernel, "stage", shape, [SMEM] + [ANY] * count, VMEM, 20 if blocks > 1 else LIMIT, 0, moved, [sems])(
        place, *[piece[0] for piece in pieces]
    )


def project(stream, kv, total=None):
    blocks, rows, width = stream.shape
    kv = kv if isinstance(kv, list) else [kv]
    cuts = [sum(w.shape[0] for w in kv[:i]) for i in range(len(kv) + 1)]

    def kernel(stream_ref, *refs):
        key_ref, value_ref, state_ref, total_ref = refs[-4:]
        for r in range(blocks):
            both = sum(dot(stream_ref[r, :, cuts[i] : cuts[i + 1]], refs[i][...]) for i in range(len(kv)))
            key_ref[r] = silu(both[:, :HDIM]).astype(BF16)
            value_ref[r] = both[:, HDIM:].astype(BF16)
        added = jnp.zeros((HDIM, HDIM), F32) if total is None else refs[len(kv)][...]
        for r in range(blocks):
            state = dot(key_ref[r], value_ref[r], ((0,), (0,)))
            state_ref[r] = state
            added = added + state
        total_ref[...] = added

    shape = jax.ShapeDtypeStruct((blocks, rows, HDIM), BF16)
    state = jax.ShapeDtypeStruct((blocks, HDIM, HDIM), F32)
    shapes = [shape, shape, state, jax.ShapeDtypeStruct((HDIM, HDIM), F32)]
    args = [stream, *kv] + ([] if total is None else [total])
    flops = 4 * blocks * rows * width * HDIM
    return call(kernel, "project", shapes, [VMEM] * len(args), [VMEM] * 4, LIMIT, flops, 2 * MIB)(*args)


def flat_blocks(streams):
    return [(stream, r) for stream in streams for r in range(stream.shape[0])]


def weighted(place_ref, source, r, refs, parts, base):
    total = base
    for ref, (weight, start) in zip(refs, parts):
        depth = weight.shape[0]
        if isinstance(start, tuple):
            lanes = pl.ds(pl.multiple_of(jnp.bitwise_xor(place_ref[3], start[0]) * depth, HDIM), depth)
        else:
            lanes = slice(start, start + depth)
        term = dot(source[r, :, lanes], ref[...])
        total = term if total is None else total + term
    return total


def run_blocks(kernel, name, place, streams, parts, base, out_shape, more=()):
    rows, width = streams[0].shape[1:]
    count = len(streams)
    args = [*streams, *[weight for weight, _ in parts], *([] if base is None else [base])]
    given = len(args)
    args += more

    def body(place_ref, *refs):
        weights = refs[count : count + len(parts)]
        base_ref = None if base is None else refs[given - 1]

        def sums():
            for i, (source, r) in enumerate(flat_blocks(refs[:count])):
                yield i, weighted(place_ref, source, r, weights, parts, None if base is None else base_ref[i])

        kernel(place_ref, sums, *refs[given:])

    flops = 4 * SUB * rows * sum(weight.shape[0] for weight, _ in parts) * HDIM
    specs = [SMEM] + [VMEM] * len(args)
    outs = [VMEM] * len(out_shape) if isinstance(out_shape, list) else VMEM
    return call(body, name, out_shape, specs, outs, LIMIT, flops, 2 * MIB)(place, *args)


def begin(place, streams, parts):
    def kernel(place_ref, sums, out):
        for i, total in sums():
            out[i] = total

    shape = pltpu.VMEM((SUB, streams[0].shape[1], 2 * HDIM), F32)
    return run_blocks(kernel, "begin", place, streams, parts, None, shape)


def keys_values(place, streams, parts, base, total):
    rows = streams[0].shape[1]

    def kernel(place_ref, sums, given_ref, key_ref, value_ref, state_ref, total_ref):
        for i, both in sums():
            key_ref[i] = silu(both[:, :HDIM]).astype(BF16)
            value_ref[i] = both[:, HDIM:].astype(BF16)
        added = jnp.zeros((HDIM, HDIM), F32)
        for i in range(SUB):
            state = dot(key_ref[i], value_ref[i], ((0,), (0,)))
            state_ref[i] = state
            added = added + state
        total_ref[0] = given_ref[...]
        total_ref[1] = added

    shape = jax.ShapeDtypeStruct((SUB, rows, HDIM), BF16)
    shapes = [shape, shape] + [jax.ShapeDtypeStruct((n, HDIM, HDIM), F32) for n in (SUB, 2)]
    return run_blocks(kernel, "keys_values", place, streams, parts, base, shapes, [total])


def queries(place, streams, parts, base):
    def kernel(place_ref, sums, out):
        swap = place_ref[1] == 1
        for i, total in sums():
            both = silu(total).astype(BF16)
            out[i, :, :HDIM] = jnp.where(swap, both[:, HDIM:], both[:, :HDIM])
            out[i, :, HDIM:] = jnp.where(swap, both[:, :HDIM], both[:, HDIM:])

    shape = jax.ShapeDtypeStruct((SUB, streams[0].shape[1], 2 * HDIM), BF16)
    return run_blocks(kernel, "queries", place, streams, parts, base, shape)


def attend(place, blocks, query, heads, carried):
    rows = query.shape[1]
    count = len(blocks)
    flat, where = [], []
    for parts in heads:
        index = []
        for part in parts:
            index += [(len(flat), r) for r in range(part[0].shape[0])]
            flat += part
        where.append(index)
    flat.append(carried)

    def kernel(place_ref, query_ref, *refs):
        ins, outs = refs[: len(flat)], refs[len(flat) :]
        causal = lax.broadcasted_iota(jnp.int32, (rows, rows), 1) <= lax.broadcasted_iota(
            jnp.int32, (rows, rows), 0
        )
        block = place_ref[0]
        for i, r in enumerate(blocks):
            for h, index in enumerate(where):
                earlier = ins[-1][h]
                for other in range(SUB):
                    if other != r:
                        is_before = jnp.bitwise_xor(block, other) < jnp.bitwise_xor(block, r)
                        slot, j = index[other]
                        earlier = earlier + jnp.where(is_before, ins[slot + 2][j], 0.0)
                slot, j = index[r]
                key, value = ins[slot][j], ins[slot + 1][j]
                q = query_ref[r, :, h * HDIM : (h + 1) * HDIM]
                scores = dot(q, key, ((1,), (1,)))
                weights = jnp.where(causal, scores, 0.0).astype(BF16)
                mixed = dot(weights, value) + dot(q, earlier.astype(BF16))
                scale = lax.rsqrt(jnp.mean(mixed * mixed, axis=-1, keepdims=True) + 1e-06)
                target = pl.multiple_of(jnp.bitwise_xor(place_ref[1], h) * HDIM, HDIM)
                outs[i][:, pl.ds(target, HDIM)] = (mixed * scale).astype(BF16)

    shapes = [jax.ShapeDtypeStruct((rows, 2 * HDIM), BF16)] * count
    flops = count * 4 * rows * HDIM * (2 * rows + HDIM)
    specs = [SMEM] + [VMEM] * (1 + len(flat))
    return call(kernel, "attend", shapes, specs, [VMEM] * count, LIMIT, flops, 2 * MIB)(place, query, *flat)


def add_features(pieces, weight, partial=None):
    rows, depth = pieces[0].shape
    width = weight.shape[2]
    count = len(pieces)
    tile = min(512, width)

    def kernel(*refs):
        w_ref, out = refs[count], refs[-1]
        for start in range(0, width, tile):
            columns = slice(start, start + tile)
            total = refs[count + 1][:, columns] if partial is not None else jnp.zeros((rows, tile), F32)
            for i in range(count):
                total = total + dot(refs[i][...], w_ref[i, :, columns])
            out[:, columns] = total.astype(out.dtype)

    shape = pltpu.VMEM((rows, width), F32) if partial is None else jax.ShapeDtypeStruct((rows, width), BF16)
    args = [*pieces, weight] + ([] if partial is None else [partial])
    flops = 2 * count * depth * rows * width
    return call(kernel, "add_features", shape, [VMEM] * len(args), VMEM, LIMIT, flops, 8 * MIB)(*args)


def exclusive_prefix(value, groups):
    def shift(v, step):
        pairs = [(g * SUB + j, (g + step) * SUB + j) for g in range(groups - step) for j in range(SUB)]
        return lax.ppermute(v, "ctx", pairs)

    if groups == 1:
        return jnp.zeros_like(value)
    total = shift(value, 1)
    step = 1
    while step < groups - 1:
        total = total + shift(total, step)
        step *= 2
    return total


def local(tokens, w_query, w_key, w_value, w_out):
    n_ctx = lax.axis_size("ctx")
    groups = n_ctx // SUB
    rows, half = tokens.shape
    ctx = lax.axis_index("ctx")
    place = jnp.stack([ctx % SUB, lax.axis_index("groups"), lax.axis_index("head"), ctx]).astype(jnp.int32)

    def xor(value, step):
        return lax.ppermute(value, "ctx", [(i, i ^ step) for i in range(n_ctx)])

    def other_part(value):
        return lax.ppermute(value, "groups", [(0, 1), (1, 0)])

    def other_core(value):
        return lax.ppermute(value, "head", [(0, 1), (1, 0)])

    def spread(packed):
        return lax.all_to_all(packed, "ctx", 0, 0, tiled=True)

    def gather_queries(sent):
        ordered = [lax.dynamic_index_in_dim(jnp.stack(sent), (ctx % SUB) ^ j, keepdims=False) for j in range(SUB)]
        return spread(jnp.concatenate(ordered * groups, axis=0))

    cut = half * 11 // 16 // HDIM * HDIM
    pieced = n_ctx == 2 * SUB
    ob = lax.optimization_barrier

    across = xor(tokens, 2)
    beside = xor(tokens, 1)
    kv_mine = spread(pack_keys_values(place, w_key, w_value, n_ctx))
    far_tokens = other_core(tokens)
    w_far = other_core(w_out)
    beside, far_tokens, w_far, w_query = ob((beside, far_tokens, w_far, w_query))
    q_sent = pack_queries(place, w_query)
    far_beside = other_core(beside)

    def fetch(sent, *steps):
        if pieced:
            arrived.update({m: xor(sent[m % SUB], m) for m in steps})

    arrived = {0: q_sent[0]}
    fetch(q_sent, 4, 1)
    across, kv_mine, beside, far_beside, q_sent, arrived = ob((across, kv_mine, beside, far_beside, q_sent, arrived))
    kv_other = other_part(kv_mine)
    left = xor(across[:, :cut], 1)
    right = xor(beside[:, cut:], 2)
    fetch(q_sent, 6, 5)
    near = [(tokens, 0, 0, 0), (far_tokens, 0, 0, 1), (beside, 1, 0, 0), (far_beside, 1, 0, 1)]
    near += [(across, 2, 0, 0), (other_core(across), 2, 0, 1)]
    near = stage(place, near, SUB - 1, rows, 2 * half)
    first = project(near, kv_mine)
    left, right, arrived, q_sent, first = ob((left, right, arrived, q_sent, first))
    fetch(q_sent, 7)
    far_left, far_right = other_core(left), other_core(right)
    far_left, q_sent = ob((far_left, q_sent))
    fetch(q_sent, 3, 2)
    corner = [(left, 0, 0, 0), (far_left, 0, 0, 1), (right, 0, cut, 0), (far_right, 0, cut, 1)]
    corner = stage(place, corner, 1, rows, 2 * half)

    streams = [near, corner]
    last = project(corner, kv_mine, first[3])
    if pieced:
        early = (0, 1, 4, 5, 6)
        q_base = begin(place, streams, [(arrived[m], (m,)) for m in early])
        arrived, kv_other, q_base = ob((arrived, kv_other, q_base))
        q_parts = [(arrived[m], (m,)) for m in range(n_ctx) if m not in early]
    else:
        q_base, q_parts = None, [(gather_queries(q_sent), 0)]
    *second, totals = keys_values(place, streams, [(kv_other, 0)], None, last[3])
    carried = exclusive_prefix(totals, groups)
    heads = [[first[:3], last[:3]], [second]]
    query = queries(place, streams, q_parts, q_base)
    away = attend(place, (3, 1, 2), query, heads, carried)
    home = attend(place, (0,), query, heads, carried)
    normed = [home[0], xor(away[1], 1), xor(away[2], 2), xor(away[0], 3)]
    home_0, w_far = lax.optimization_barrier((home[0], w_far))
    out_keep, out_far = stage_rows(place, w_out, w_far)
    out_keep, out_far, *normed = lax.optimization_barrier((out_keep, out_far, home_0, *normed[1:]))
    partial = add_features(normed, out_keep)
    return add_features([other_core(n) for n in normed], out_far, partial)


def solution(mesh):
    in_specs = (
        P(("groups", "ctx"), "head"),
        P("ctx", "head"),
        P("ctx", "head"),
        P("ctx", "head"),
        P("head", None),
    )
    out_specs = P(("groups", "ctx"), "head")
    return jax.shard_map(local, mesh=mesh, in_specs=in_specs, out_specs=out_specs, check_vma=False)
```

```python
import jax
import jax.numpy as jnp
from jax import lax
from jax.experimental import pallas as pl
from jax.experimental.pallas import tpu as pltpu
from jax.sharding import PartitionSpec as P

HDIM = 128
SUB = 4
F32 = jnp.float32
BF16 = jnp.bfloat16
MIB = 1 << 20
LIMIT = 8
ANY = pl.BlockSpec(memory_space=pl.ANY)
VMEM = pl.BlockSpec(memory_space=pltpu.VMEM)
SMEM = pl.BlockSpec(memory_space=pltpu.SMEM)


def dot(a, b, contract=((1,), (0,))):
    return lax.dot_general(a, b, (contract, ((), ())), preferred_element_type=F32)


def silu(u):
    return u / (1.0 + jnp.exp(-u))


def call(kernel, name, out_shape, in_specs, out_specs, limit, flops, moved, scratch=()):
    return pl.pallas_call(
        kernel,
        out_shape=out_shape,
        in_specs=in_specs,
        out_specs=out_specs,
        scratch_shapes=list(scratch),
        compiler_params=pltpu.CompilerParams(vmem_limit_bytes=limit * MIB),
        cost_estimate=pl.CostEstimate(flops=int(flops), bytes_accessed=int(moved), transcendentals=0),
        name=name,
    )


def pack_keys_values(place, w_key, w_value, count):
    depth = w_key.shape[0]

    def kernel(place_ref, key_ref, value_ref, out, sems):
        copies = []
        for i in range(count):
            start = pl.multiple_of((2 * (i % SUB) + place_ref[1]) * HDIM, HDIM)
            for h, ref in enumerate((key_ref, value_ref)):
                target = out.at[pl.ds(i * depth, depth), pl.ds(h * HDIM, HDIM)]
                copies.append(pltpu.make_async_copy(ref.at[:, pl.ds(start, HDIM)], target, sems.at[2 * i + h]))
        for copy in copies:
            copy.start()
        for copy in copies:
            copy.wait()

    shape = jax.ShapeDtypeStruct((count * depth, 2 * HDIM), BF16)
    moved = count * depth * 2 * HDIM * 4
    sems = pltpu.SemaphoreType.DMA((2 * count,))
    return call(kernel, "pack_keys_values", shape, [SMEM, ANY, ANY], ANY, 56, 0, moved, [sems])(
        place, w_key, w_value
    )


def pack_queries(place, w_query):
    depth = w_query.shape[0]

    def kernel(place_ref, query_ref, *outs):
        for r, out in enumerate(outs):
            start = pl.multiple_of(jnp.bitwise_xor(place_ref[0], r) * 2 * HDIM, 2 * HDIM)
            out[...] = query_ref[:, pl.ds(start, 2 * HDIM)]

    shapes = [jax.ShapeDtypeStruct((depth, 2 * HDIM), BF16)] * SUB
    moved = SUB * depth * 2 * HDIM * 4
    return call(kernel, "pack_queries", shapes, [SMEM, VMEM], [VMEM] * SUB, LIMIT, 0, moved)(place, w_query)


def stage_rows(place, w_out, w_far):
    rows, width = w_out.shape
    depth, half = rows // SUB, width // 2

    def kernel(place_ref, out_ref, far_ref, keep, far, sems):
        column = pl.multiple_of(place_ref[2] * half, half)
        copies = []
        for r in range(SUB):
            row = pl.multiple_of(jnp.bitwise_xor(place_ref[0], r) * depth, depth)
            for i, (source, target) in enumerate(((out_ref, keep), (far_ref, far))):
                block = source.at[pl.ds(row, depth), pl.ds(column, half)]
                copies.append(pltpu.make_async_copy(block, target.at[r], sems.at[2 * r + i]))
        for copy in copies:
            copy.start()
        for copy in copies:
            copy.wait()

    shapes = [pltpu.VMEM((SUB, depth, half), BF16)] * 2
    sems = pltpu.SemaphoreType.DMA((2 * SUB,))
    return call(kernel, "stage_rows", shapes, [SMEM, ANY, ANY], [VMEM] * 2, 40, 0, rows * width * 4, [sems])(
        place, w_out, w_far
    )


def stage(place, pieces, blocks, rows, width):
    count = len(pieces)
    half = width // 2

    def kernel(place_ref, *refs):
        out, sems = refs[count], refs[count + 1]
        copies = []
        for i, ((array, r, column, far), ref) in enumerate(zip(pieces, refs)):
            if far is None:
                target = out.at[r]
            else:
                core = 1 - place_ref[2] if far else place_ref[2]
                start = pl.multiple_of(core * half + column, HDIM)
                target = out.at[r, :, pl.ds(start, array.shape[1])]
            copies.append(pltpu.make_async_copy(ref, target, sems.at[i]))
        for copy in copies:
            copy.start()
        for copy in copies:
            copy.wait()

    shape = pltpu.VMEM((blocks, rows, width), BF16)
    sems = pltpu.SemaphoreType.DMA((count,))
    moved = blocks * rows * width * 4
    return call(kernel, "stage", shape, [SMEM] + [ANY] * count, VMEM, 20 if blocks > 1 else LIMIT, 0, moved, [sems])(
        place, *[piece[0] for piece in pieces]
    )


def project(stream, kv, total=None):
    blocks, rows, width = stream.shape
    kv = kv if isinstance(kv, list) else [kv]
    cuts = [sum(w.shape[0] for w in kv[:i]) for i in range(len(kv) + 1)]

    def kernel(stream_ref, *refs):
        key_ref, value_ref, state_ref, total_ref = refs[-4:]
        for r in range(blocks):
            both = sum(dot(stream_ref[r, :, cuts[i] : cuts[i + 1]], refs[i][...]) for i in range(len(kv)))
            key_ref[r] = silu(both[:, :HDIM]).astype(BF16)
            value_ref[r] = both[:, HDIM:].astype(BF16)
        added = jnp.zeros((HDIM, HDIM), F32) if total is None else refs[len(kv)][...]
        for r in range(blocks):
            state = dot(key_ref[r], value_ref[r], ((0,), (0,)))
            state_ref[r] = state
            added = added + state
        total_ref[...] = added

    shape = jax.ShapeDtypeStruct((blocks, rows, HDIM), BF16)
    state = jax.ShapeDtypeStruct((blocks, HDIM, HDIM), F32)
    shapes = [shape, shape, state, jax.ShapeDtypeStruct((HDIM, HDIM), F32)]
    args = [stream, *kv] + ([] if total is None else [total])
    flops = 4 * blocks * rows * width * HDIM
    return call(kernel, "project", shapes, [VMEM] * len(args), [VMEM] * 4, LIMIT, flops, 2 * MIB)(*args)


def flat_blocks(streams):
    return [(stream, r) for stream in streams for r in range(stream.shape[0])]


def weighted(place_ref, source, r, refs, parts, base):
    total = base
    for ref, (weight, start) in zip(refs, parts):
        depth = weight.shape[0]
        if isinstance(start, tuple):
            lanes = pl.ds(pl.multiple_of(jnp.bitwise_xor(place_ref[3], start[0]) * depth, HDIM), depth)
        else:
            lanes = slice(start, start + depth)
        term = dot(source[r, :, lanes], ref[...])
        total = term if total is None else total + term
    return total


def run_blocks(kernel, name, place, streams, parts, base, out_shape, more=()):
    rows, width = streams[0].shape[1:]
    count = len(streams)
    args = [*streams, *[weight for weight, _ in parts], *([] if base is None else [base])]
    given = len(args)
    args += more

    def body(place_ref, *refs):
        weights = refs[count : count + len(parts)]
        base_ref = None if base is None else refs[given - 1]

        def sums():
            for i, (source, r) in enumerate(flat_blocks(refs[:count])):
                yield i, weighted(place_ref, source, r, weights, parts, None if base is None else base_ref[i])

        kernel(place_ref, sums, *refs[given:])

    flops = 4 * SUB * rows * sum(weight.shape[0] for weight, _ in parts) * HDIM
    specs = [SMEM] + [VMEM] * len(args)
    outs = [VMEM] * len(out_shape) if isinstance(out_shape, list) else VMEM
    return call(body, name, out_shape, specs, outs, LIMIT, flops, 2 * MIB)(place, *args)


def begin(place, streams, parts):
    def kernel(place_ref, sums, out):
        for i, total in sums():
            out[i] = total

    shape = pltpu.VMEM((SUB, streams[0].shape[1], 2 * HDIM), F32)
    return run_blocks(kernel, "begin", place, streams, parts, None, shape)


def keys_values(place, streams, parts, base, total):
    rows = streams[0].shape[1]

    def kernel(place_ref, sums, given_ref, key_ref, value_ref, state_ref, total_ref):
        for i, both in sums():
            key_ref[i] = silu(both[:, :HDIM]).astype(BF16)
            value_ref[i] = both[:, HDIM:].astype(BF16)
        added = jnp.zeros((HDIM, HDIM), F32)
        for i in range(SUB):
            state = dot(key_ref[i], value_ref[i], ((0,), (0,)))
            state_ref[i] = state
            added = added + state
        total_ref[0] = given_ref[...]
        total_ref[1] = added

    shape = jax.ShapeDtypeStruct((SUB, rows, HDIM), BF16)
    shapes = [shape, shape] + [jax.ShapeDtypeStruct((n, HDIM, HDIM), F32) for n in (SUB, 2)]
    return run_blocks(kernel, "keys_values", place, streams, parts, base, shapes, [total])


def queries(place, streams, parts, base):
    def kernel(place_ref, sums, out):
        swap = place_ref[1] == 1
        for i, total in sums():
            both = silu(total).astype(BF16)
            out[i, :, :HDIM] = jnp.where(swap, both[:, HDIM:], both[:, :HDIM])
            out[i, :, HDIM:] = jnp.where(swap, both[:, :HDIM], both[:, HDIM:])

    shape = jax.ShapeDtypeStruct((SUB, streams[0].shape[1], 2 * HDIM), BF16)
    return run_blocks(kernel, "queries", place, streams, parts, base, shape)


def attend(place, blocks, query, heads, carried):
    rows = query.shape[1]
    count = len(blocks)
    flat, where = [], []
    for parts in heads:
        index = []
        for part in parts:
            index += [(len(flat), r) for r in range(part[0].shape[0])]
            flat += part
        where.append(index)
    flat.append(carried)

    def kernel(place_ref, query_ref, *refs):
        ins, outs = refs[: len(flat)], refs[len(flat) :]
        causal = lax.broadcasted_iota(jnp.int32, (rows, rows), 1) <= lax.broadcasted_iota(
            jnp.int32, (rows, rows), 0
        )
        block = place_ref[0]
        for i, r in enumerate(blocks):
            for h, index in enumerate(where):
                earlier = ins[-1][h]
                for other in range(SUB):
                    if other != r:
                        is_before = jnp.bitwise_xor(block, other) < jnp.bitwise_xor(block, r)
                        slot, j = index[other]
                        earlier = earlier + jnp.where(is_before, ins[slot + 2][j], 0.0)
                slot, j = index[r]
                key, value = ins[slot][j], ins[slot + 1][j]
                q = query_ref[r, :, h * HDIM : (h + 1) * HDIM]
                scores = dot(q, key, ((1,), (1,)))
                weights = jnp.where(causal, scores, 0.0).astype(BF16)
                mixed = dot(weights, value) + dot(q, earlier.astype(BF16))
                scale = lax.rsqrt(jnp.mean(mixed * mixed, axis=-1, keepdims=True) + 1e-06)
                target = pl.multiple_of(jnp.bitwise_xor(place_ref[1], h) * HDIM, HDIM)
                outs[i][:, pl.ds(target, HDIM)] = (mixed * scale).astype(BF16)

    shapes = [jax.ShapeDtypeStruct((rows, 2 * HDIM), BF16)] * count
    flops = count * 4 * rows * HDIM * (2 * rows + HDIM)
    specs = [SMEM] + [VMEM] * (1 + len(flat))
    return call(kernel, "attend", shapes, specs, [VMEM] * count, LIMIT, flops, 2 * MIB)(place, query, *flat)


def add_features(pieces, weight, partial=None):
    rows, depth = pieces[0].shape
    width = weight.shape[2]
    count = len(pieces)
    tile = min(512, width)

    def kernel(*refs):
        w_ref, out = refs[count], refs[-1]
        for start in range(0, width, tile):
            columns = slice(start, start + tile)
            total = refs[count + 1][:, columns] if partial is not None else jnp.zeros((rows, tile), F32)
            for i in range(count):
                total = total + dot(refs[i][...], w_ref[i, :, columns])
            out[:, columns] = total.astype(out.dtype)

    shape = pltpu.VMEM((rows, width), F32) if partial is None else jax.ShapeDtypeStruct((rows, width), BF16)
    args = [*pieces, weight] + ([] if partial is None else [partial])
    flops = 2 * count * depth * rows * width
    return call(kernel, "add_features", shape, [VMEM] * len(args), VMEM, LIMIT, flops, 8 * MIB)(*args)


def exclusive_prefix(value, groups):
    def shift(v, step):
        pairs = [(g * SUB + j, (g + step) * SUB + j) for g in range(groups - step) for j in range(SUB)]
        return lax.ppermute(v, "ctx", pairs)

    if groups == 1:
        return jnp.zeros_like(value)
    total = shift(value, 1)
    step = 1
    while step < groups - 1:
        total = total + shift(total, step)
        step *= 2
    return total


def local(tokens, w_query, w_key, w_value, w_out):
    n_ctx = lax.axis_size("ctx")
    groups = n_ctx // SUB
    rows, half = tokens.shape
    ctx = lax.axis_index("ctx")
    place = jnp.stack([ctx % SUB, lax.axis_index("groups"), lax.axis_index("head"), ctx]).astype(jnp.int32)

    def xor(value, step):
        return lax.ppermute(value, "ctx", [(i, i ^ step) for i in range(n_ctx)])

    def other_part(value):
        return lax.ppermute(value, "groups", [(0, 1), (1, 0)])

    def other_core(value):
        return lax.ppermute(value, "head", [(0, 1), (1, 0)])

    def spread(packed):
        return lax.all_to_all(packed, "ctx", 0, 0, tiled=True)

    def gather_queries(sent):
        ordered = [lax.dynamic_index_in_dim(jnp.stack(sent), (ctx % SUB) ^ j, keepdims=False) for j in range(SUB)]
        return spread(jnp.concatenate(ordered * groups, axis=0))

    cut = half * 11 // 16 // HDIM * HDIM
    pieced = n_ctx == 2 * SUB
    ob = lax.optimization_barrier

    across = xor(tokens, 2)
    beside = xor(tokens, 1)
    kv_mine = spread(pack_keys_values(place, w_key, w_value, n_ctx))
    far_tokens = other_core(tokens)
    w_far = other_core(w_out)
    beside, far_tokens, w_far, w_query = ob((beside, far_tokens, w_far, w_query))
    q_sent = pack_queries(place, w_query)
    far_beside = other_core(beside)

    def fetch(sent, *steps):
        if pieced:
            arrived.update({m: xor(sent[m % SUB], m) for m in steps})

    arrived = {0: q_sent[0]}
    fetch(q_sent, 1)
    beside_cut = beside[:, cut:]
    across, kv_mine, beside, far_beside, q_sent, arrived, beside_cut = ob(
        (across, kv_mine, beside, far_beside, q_sent, arrived, beside_cut)
    )
    middle = kv_mine.shape[0] // 2
    kv_upper = other_part(kv_mine[:middle])
    left = xor(across[:, :cut], 1)
    right = xor(beside_cut, 2)
    fetch(q_sent, 4, 6)
    near = [(tokens, 0, 0, 0), (far_tokens, 0, 0, 1), (beside, 1, 0, 0), (far_beside, 1, 0, 1)]
    near += [(across, 2, 0, 0), (other_core(across), 2, 0, 1)]
    near = stage(place, near, SUB - 1, rows, 2 * half)
    first = project(near, kv_mine)
    left, right, arrived, kv_upper, kv_mine, q_sent, first = ob(
        (left, right, arrived, kv_upper, kv_mine, q_sent, first)
    )
    kv_lower = other_part(kv_mine[middle:])
    fetch(q_sent, 5, 7)
    far_left, far_right = other_core(left), other_core(right)
    far_left, q_sent = ob((far_left, q_sent))
    fetch(q_sent, 3, 2)
    corner = [(left, 0, 0, 0), (far_left, 0, 0, 1), (right, 0, cut, 0), (far_right, 0, cut, 1)]
    corner = stage(place, corner, 1, rows, 2 * half)

    streams = [near, corner]
    last = project(corner, kv_mine, first[3])
    kv_base = begin(place, streams, [(kv_upper, 0)])
    if pieced:
        early = (0, 1, 4, 6)
        q_base = begin(place, streams, [(arrived[m], (m,)) for m in early])
        arrived, kv_lower, kv_base, q_base = ob((arrived, kv_lower, kv_base, q_base))
        q_parts = [(arrived[m], (m,)) for m in range(n_ctx) if m not in early]
    else:
        q_base, q_parts = None, [(gather_queries(q_sent), 0)]
    *second, totals = keys_values(place, streams, [(kv_lower, middle)], kv_base, last[3])
    carried = exclusive_prefix(totals, groups)
    heads = [[first[:3], last[:3]], [second]]
    query = queries(place, streams, q_parts, q_base)
    normed = [attend(place, (r,), query, heads, carried)[0] for r in (3, 1, 2, 0)]
    normed = [normed[3], xor(normed[1], 1), xor(normed[2], 2), xor(normed[0], 3)]
    home_0, w_far = lax.optimization_barrier((normed[0], w_far))
    out_keep, out_far = stage_rows(place, w_out, w_far)
    out_keep, out_far, *normed = lax.optimization_barrier((out_keep, out_far, home_0, *normed[1:]))
    partial = add_features(normed, out_keep)
    return add_features([other_core(n) for n in normed], out_far, partial)


def solution(mesh):
    in_specs = (
        P(("groups", "ctx"), "head"),
        P("ctx", "head"),
        P("ctx", "head"),
        P("ctx", "head"),
        P("head", None),
    )
    out_specs = P(("groups", "ctx"), "head")
    return jax.shard_map(local, mesh=mesh, in_specs=in_specs, out_specs=out_specs, check_vma=False)
```

```python
import jax
import jax.numpy as jnp
from jax import lax
from jax.experimental import pallas as pl
from jax.experimental.pallas import tpu as pltpu
from jax.sharding import PartitionSpec as P

HDIM = 128
SUB = 4
F32 = jnp.float32
BF16 = jnp.bfloat16
MIB = 1 << 20
LIMIT = 8
ANY = pl.BlockSpec(memory_space=pl.ANY)
VMEM = pl.BlockSpec(memory_space=pltpu.VMEM)
SMEM = pl.BlockSpec(memory_space=pltpu.SMEM)


def dot(a, b, contract=((1,), (0,))):
    return lax.dot_general(a, b, (contract, ((), ())), preferred_element_type=F32)


def silu(u):
    return u / (1.0 + jnp.exp(-u))


def call(kernel, name, out_shape, in_specs, out_specs, limit, flops, moved, scratch=()):
    return pl.pallas_call(
        kernel,
        out_shape=out_shape,
        in_specs=in_specs,
        out_specs=out_specs,
        scratch_shapes=list(scratch),
        compiler_params=pltpu.CompilerParams(vmem_limit_bytes=limit * MIB),
        cost_estimate=pl.CostEstimate(flops=int(flops), bytes_accessed=int(moved), transcendentals=0),
        name=name,
    )


def pack_keys_values(place, w_key, w_value, count):
    depth = w_key.shape[0]

    def kernel(place_ref, key_ref, value_ref, out):
        for j in range(SUB):
            start = pl.multiple_of((2 * j + place_ref[1]) * HDIM, HDIM)
            key = key_ref[:, pl.ds(start, HDIM)]
            value = value_ref[:, pl.ds(start, HDIM)]
            for i in range(j, count, SUB):
                out[i * depth : (i + 1) * depth, :HDIM] = key
                out[i * depth : (i + 1) * depth, HDIM:] = value

    shape = jax.ShapeDtypeStruct((count * depth, 2 * HDIM), BF16)
    moved = count * depth * 2 * HDIM * 4
    return call(kernel, "pack_keys_values", shape, [SMEM, VMEM, VMEM], VMEM, LIMIT, 0, moved)(place, w_key, w_value)


def pack_queries(place, w_query):
    depth = w_query.shape[0]

    def kernel(place_ref, query_ref, *outs):
        for r, out in enumerate(outs):
            start = pl.multiple_of(jnp.bitwise_xor(place_ref[0], r) * 2 * HDIM, 2 * HDIM)
            out[...] = query_ref[:, pl.ds(start, 2 * HDIM)]

    shapes = [jax.ShapeDtypeStruct((depth, 2 * HDIM), BF16)] * SUB
    moved = SUB * depth * 2 * HDIM * 4
    return call(kernel, "pack_queries", shapes, [SMEM, VMEM], [VMEM] * SUB, LIMIT, 0, moved)(place, w_query)


def stage_rows(place, w_out, w_far):
    rows, width = w_out.shape
    depth, half = rows // SUB, width // 2

    def kernel(place_ref, out_ref, far_ref, keep, far, sems):
        column = pl.multiple_of(place_ref[2] * half, half)
        copies = []
        for r in range(SUB):
            row = pl.multiple_of(jnp.bitwise_xor(place_ref[0], r) * depth, depth)
            for i, (source, target) in enumerate(((out_ref, keep), (far_ref, far))):
                block = source.at[pl.ds(row, depth), pl.ds(column, half)]
                copies.append(pltpu.make_async_copy(block, target.at[r], sems.at[2 * r + i]))
        for copy in copies:
            copy.start()
        for copy in copies:
            copy.wait()

    shapes = [pltpu.VMEM((SUB, depth, half), BF16)] * 2
    sems = pltpu.SemaphoreType.DMA((2 * SUB,))
    return call(kernel, "stage_rows", shapes, [SMEM, ANY, ANY], [VMEM] * 2, 40, 0, rows * width * 4, [sems])(
        place, w_out, w_far
    )


def stage(place, pieces, blocks, rows, width):
    count = len(pieces)
    half = width // 2

    def kernel(place_ref, *refs):
        out, sems = refs[count], refs[count + 1]
        copies = []
        for i, ((array, r, column, far), ref) in enumerate(zip(pieces, refs)):
            if far is None:
                target = out.at[r]
            else:
                core = 1 - place_ref[2] if far else place_ref[2]
                start = pl.multiple_of(core * half + column, HDIM)
                target = out.at[r, :, pl.ds(start, array.shape[1])]
            copies.append(pltpu.make_async_copy(ref, target, sems.at[i]))
        for copy in copies:
            copy.start()
        for copy in copies:
            copy.wait()

    shape = pltpu.VMEM((blocks, rows, width), BF16)
    sems = pltpu.SemaphoreType.DMA((count,))
    moved = blocks * rows * width * 4
    return call(kernel, "stage", shape, [SMEM] + [ANY] * count, VMEM, 20 if blocks > 1 else LIMIT, 0, moved, [sems])(
        place, *[piece[0] for piece in pieces]
    )


def project(stream, kv, total=None):
    blocks, rows, width = stream.shape
    kv = kv if isinstance(kv, list) else [kv]
    cuts = [sum(w.shape[0] for w in kv[:i]) for i in range(len(kv) + 1)]

    def kernel(stream_ref, *refs):
        key_ref, value_ref, state_ref, total_ref = refs[-4:]
        for r in range(blocks):
            both = sum(dot(stream_ref[r, :, cuts[i] : cuts[i + 1]], refs[i][...]) for i in range(len(kv)))
            key_ref[r] = silu(both[:, :HDIM]).astype(BF16)
            value_ref[r] = both[:, HDIM:].astype(BF16)
        added = jnp.zeros((HDIM, HDIM), F32) if total is None else refs[len(kv)][...]
        for r in range(blocks):
            state = dot(key_ref[r], value_ref[r], ((0,), (0,)))
            state_ref[r] = state
            added = added + state
        total_ref[...] = added

    shape = jax.ShapeDtypeStruct((blocks, rows, HDIM), BF16)
    state = jax.ShapeDtypeStruct((blocks, HDIM, HDIM), F32)
    shapes = [shape, shape, state, jax.ShapeDtypeStruct((HDIM, HDIM), F32)]
    args = [stream, *kv] + ([] if total is None else [total])
    flops = 4 * blocks * rows * width * HDIM
    return call(kernel, "project", shapes, [VMEM] * len(args), [VMEM] * 4, LIMIT, flops, 2 * MIB)(*args)


def flat_blocks(streams):
    return [(stream, r) for stream in streams for r in range(stream.shape[0])]


def weighted(place_ref, source, r, refs, parts, base):
    total = base
    for ref, (weight, start) in zip(refs, parts):
        depth = weight.shape[0]
        if isinstance(start, tuple):
            lanes = pl.ds(pl.multiple_of(jnp.bitwise_xor(place_ref[3], start[0]) * depth, HDIM), depth)
        else:
            lanes = slice(start, start + depth)
        term = dot(source[r, :, lanes], ref[...])
        total = term if total is None else total + term
    return total


def run_blocks(kernel, name, place, streams, parts, base, out_shape, more=()):
    rows, width = streams[0].shape[1:]
    count = len(streams)
    args = [*streams, *[weight for weight, _ in parts], *([] if base is None else [base])]
    given = len(args)
    args += more

    def body(place_ref, *refs):
        weights = refs[count : count + len(parts)]
        base_ref = None if base is None else refs[given - 1]

        def sums():
            for i, (source, r) in enumerate(flat_blocks(refs[:count])):
                yield i, weighted(place_ref, source, r, weights, parts, None if base is None else base_ref[i])

        kernel(place_ref, sums, *refs[given:])

    flops = 4 * SUB * rows * sum(weight.shape[0] for weight, _ in parts) * HDIM
    specs = [SMEM] + [VMEM] * len(args)
    outs = [VMEM] * len(out_shape) if isinstance(out_shape, list) else VMEM
    return call(body, name, out_shape, specs, outs, LIMIT, flops, 2 * MIB)(place, *args)


def begin(place, streams, parts):
    def kernel(place_ref, sums, out):
        for i, total in sums():
            out[i] = total

    shape = pltpu.VMEM((SUB, streams[0].shape[1], 2 * HDIM), F32)
    return run_blocks(kernel, "begin", place, streams, parts, None, shape)


def keys_values(place, streams, parts, base, total):
    rows = streams[0].shape[1]

    def kernel(place_ref, sums, given_ref, key_ref, value_ref, state_ref, total_ref):
        for i, both in sums():
            key_ref[i] = silu(both[:, :HDIM]).astype(BF16)
            value_ref[i] = both[:, HDIM:].astype(BF16)
        added = jnp.zeros((HDIM, HDIM), F32)
        for i in range(SUB):
            state = dot(key_ref[i], value_ref[i], ((0,), (0,)))
            state_ref[i] = state
            added = added + state
        total_ref[0] = given_ref[...]
        total_ref[1] = added

    shape = jax.ShapeDtypeStruct((SUB, rows, HDIM), BF16)
    shapes = [shape, shape] + [jax.ShapeDtypeStruct((n, HDIM, HDIM), F32) for n in (SUB, 2)]
    return run_blocks(kernel, "keys_values", place, streams, parts, base, shapes, [total])


def queries(place, streams, parts, base):
    def kernel(place_ref, sums, out):
        swap = place_ref[1] == 1
        for i, total in sums():
            both = silu(total).astype(BF16)
            out[i, :, :HDIM] = jnp.where(swap, both[:, HDIM:], both[:, :HDIM])
            out[i, :, HDIM:] = jnp.where(swap, both[:, :HDIM], both[:, HDIM:])

    shape = jax.ShapeDtypeStruct((SUB, streams[0].shape[1], 2 * HDIM), BF16)
    return run_blocks(kernel, "queries", place, streams, parts, base, shape)


def attend(place, blocks, query, heads, carried):
    rows = query.shape[1]
    count = len(blocks)
    flat, where = [], []
    for parts in heads:
        index = []
        for part in parts:
            index += [(len(flat), r) for r in range(part[0].shape[0])]
            flat += part
        where.append(index)
    flat.append(carried)

    def kernel(place_ref, query_ref, *refs):
        ins, outs = refs[: len(flat)], refs[len(flat) :]
        causal = lax.broadcasted_iota(jnp.int32, (rows, rows), 1) <= lax.broadcasted_iota(
            jnp.int32, (rows, rows), 0
        )
        block = place_ref[0]
        for i, r in enumerate(blocks):
            for h, index in enumerate(where):
                earlier = ins[-1][h]
                for other in range(SUB):
                    if other != r:
                        is_before = jnp.bitwise_xor(block, other) < jnp.bitwise_xor(block, r)
                        slot, j = index[other]
                        earlier = earlier + jnp.where(is_before, ins[slot + 2][j], 0.0)
                slot, j = index[r]
                key, value = ins[slot][j], ins[slot + 1][j]
                q = query_ref[r, :, h * HDIM : (h + 1) * HDIM]
                scores = dot(q, key, ((1,), (1,)))
                weights = jnp.where(causal, scores, 0.0).astype(BF16)
                mixed = dot(weights, value) + dot(q, earlier.astype(BF16))
                scale = lax.rsqrt(jnp.mean(mixed * mixed, axis=-1, keepdims=True) + 1e-06)
                target = pl.multiple_of(jnp.bitwise_xor(place_ref[1], h) * HDIM, HDIM)
                outs[i][:, pl.ds(target, HDIM)] = (mixed * scale).astype(BF16)

    shapes = [jax.ShapeDtypeStruct((rows, 2 * HDIM), BF16)] * count
    flops = count * 4 * rows * HDIM * (2 * rows + HDIM)
    specs = [SMEM] + [VMEM] * (1 + len(flat))
    return call(kernel, "attend", shapes, specs, [VMEM] * count, LIMIT, flops, 2 * MIB)(place, query, *flat)


def add_features(pieces, weight, partial=None):
    rows, depth = pieces[0].shape
    width = weight.shape[2]
    count = len(pieces)
    tile = min(512, width)

    def kernel(*refs):
        w_ref, out = refs[count], refs[-1]
        for start in range(0, width, tile):
            columns = slice(start, start + tile)
            total = refs[count + 1][:, columns] if partial is not None else jnp.zeros((rows, tile), F32)
            for i in range(count):
                total = total + dot(refs[i][...], w_ref[i, :, columns])
            out[:, columns] = total.astype(out.dtype)

    shape = pltpu.VMEM((rows, width), F32) if partial is None else jax.ShapeDtypeStruct((rows, width), BF16)
    args = [*pieces, weight] + ([] if partial is None else [partial])
    flops = 2 * count * depth * rows * width
    return call(kernel, "add_features", shape, [VMEM] * len(args), VMEM, LIMIT, flops, 8 * MIB)(*args)


def exclusive_prefix(value, groups):
    def shift(v, step):
        pairs = [(g * SUB + j, (g + step) * SUB + j) for g in range(groups - step) for j in range(SUB)]
        return lax.ppermute(v, "ctx", pairs)

    if groups == 1:
        return jnp.zeros_like(value)
    total = shift(value, 1)
    step = 1
    while step < groups - 1:
        total = total + shift(total, step)
        step *= 2
    return total


def local(tokens, w_query, w_key, w_value, w_out):
    n_ctx = lax.axis_size("ctx")
    groups = n_ctx // SUB
    rows, half = tokens.shape
    ctx = lax.axis_index("ctx")
    place = jnp.stack([ctx % SUB, lax.axis_index("groups"), lax.axis_index("head"), ctx]).astype(jnp.int32)

    def xor(value, step):
        return lax.ppermute(value, "ctx", [(i, i ^ step) for i in range(n_ctx)])

    def other_part(value):
        return lax.ppermute(value, "groups", [(0, 1), (1, 0)])

    def other_core(value):
        return lax.ppermute(value, "head", [(0, 1), (1, 0)])

    def spread(packed):
        return lax.all_to_all(packed, "ctx", 0, 0, tiled=True)

    def gather_queries(sent):
        ordered = [lax.dynamic_index_in_dim(jnp.stack(sent), (ctx % SUB) ^ j, keepdims=False) for j in range(SUB)]
        return spread(jnp.concatenate(ordered * groups, axis=0))

    cut = half * 11 // 16 // HDIM * HDIM
    pieced = n_ctx == 2 * SUB
    ob = lax.optimization_barrier

    across = xor(tokens, 2)
    beside = xor(tokens, 1)
    kv_mine = spread(pack_keys_values(place, w_key, w_value, n_ctx))
    far_tokens = other_core(tokens)
    w_far = other_core(w_out)
    beside, far_tokens, w_far, w_query = ob((beside, far_tokens, w_far, w_query))
    q_sent = pack_queries(place, w_query)
    far_beside = other_core(beside)

    def fetch(sent, *steps):
        if pieced:
            arrived.update({m: xor(sent[m % SUB], m) for m in steps})

    arrived = {0: q_sent[0]}
    fetch(q_sent, 1)
    beside_cut = beside[:, cut:]
    across, kv_mine, beside, far_beside, q_sent, arrived, beside_cut = ob(
        (across, kv_mine, beside, far_beside, q_sent, arrived, beside_cut)
    )
    middle = kv_mine.shape[0] // 2
    kv_upper = other_part(kv_mine[:middle])
    left = xor(across[:, :cut], 1)
    right = xor(beside_cut, 2)
    fetch(q_sent, 4, 6)
    near = [(tokens, 0, 0, 0), (far_tokens, 0, 0, 1), (beside, 1, 0, 0), (far_beside, 1, 0, 1)]
    near += [(across, 2, 0, 0), (other_core(across), 2, 0, 1)]
    near = stage(place, near, SUB - 1, rows, 2 * half)
    first = project(near, kv_mine)
    left, right, arrived, kv_upper, kv_mine, q_sent, first = ob(
        (left, right, arrived, kv_upper, kv_mine, q_sent, first)
    )
    kv_lower = other_part(kv_mine[middle:])
    fetch(q_sent, 5, 7)
    far_left, far_right = other_core(left), other_core(right)
    far_left, q_sent = ob((far_left, q_sent))
    fetch(q_sent, 3, 2)
    corner = [(left, 0, 0, 0), (far_left, 0, 0, 1), (right, 0, cut, 0), (far_right, 0, cut, 1)]
    corner = stage(place, corner, 1, rows, 2 * half)

    streams = [near, corner]
    last = project(corner, kv_mine, first[3])
    kv_base = begin(place, streams, [(kv_upper, 0)])
    if pieced:
        early = (0, 1, 4, 6)
        q_base = begin(place, streams, [(arrived[m], (m,)) for m in early])
        arrived, kv_lower, kv_base, q_base = ob((arrived, kv_lower, kv_base, q_base))
        q_parts = [(arrived[m], (m,)) for m in range(n_ctx) if m not in early]
    else:
        q_base, q_parts = None, [(gather_queries(q_sent), 0)]
    *second, totals = keys_values(place, streams, [(kv_lower, middle)], kv_base, last[3])
    carried = exclusive_prefix(totals, groups)
    heads = [[first[:3], last[:3]], [second]]
    query = queries(place, streams, q_parts, q_base)
    normed = [attend(place, (r,), query, heads, carried)[0] for r in (3, 1, 2, 0)]
    normed = [normed[3], xor(normed[1], 1), xor(normed[2], 2), xor(normed[0], 3)]
    home_0, w_far = lax.optimization_barrier((normed[0], w_far))
    out_keep, out_far = stage_rows(place, w_out, w_far)
    out_keep, out_far, *normed = lax.optimization_barrier((out_keep, out_far, home_0, *normed[1:]))
    partial = add_features(normed, out_keep)
    return add_features([other_core(n) for n in normed], out_far, partial)


def solution(mesh):
    in_specs = (
        P(("groups", "ctx"), "head"),
        P("ctx", "head"),
        P("ctx", "head"),
        P("ctx", "head"),
        P("head", None),
    )
    out_specs = P(("groups", "ctx"), "head")
    return jax.shard_map(local, mesh=mesh, in_specs=in_specs, out_specs=out_specs, check_vma=False)
```

```python
import jax
import jax.numpy as jnp
from jax import lax
from jax.experimental import pallas as pl
from jax.experimental.pallas import tpu as pltpu
from jax.sharding import PartitionSpec as P

HDIM = 128
SUB = 4
F32 = jnp.float32
BF16 = jnp.bfloat16
MIB = 1 << 20
LIMIT = 8
ANY = pl.BlockSpec(memory_space=pl.ANY)
VMEM = pl.BlockSpec(memory_space=pltpu.VMEM)
SMEM = pl.BlockSpec(memory_space=pltpu.SMEM)


def dot(a, b, contract=((1,), (0,))):
    return lax.dot_general(a, b, (contract, ((), ())), preferred_element_type=F32)


def silu(u):
    return u / (1.0 + jnp.exp(-u))


def call(kernel, name, out_shape, in_specs, out_specs, limit, flops, moved, scratch=()):
    return pl.pallas_call(
        kernel,
        out_shape=out_shape,
        in_specs=in_specs,
        out_specs=out_specs,
        scratch_shapes=list(scratch),
        compiler_params=pltpu.CompilerParams(vmem_limit_bytes=limit * MIB),
        cost_estimate=pl.CostEstimate(flops=int(flops), bytes_accessed=int(moved), transcendentals=0),
        name=name,
    )


def pack_keys_values(place, w_key, w_value, count):
    depth = w_key.shape[0]

    def kernel(place_ref, key_ref, value_ref, out):
        for j in range(SUB):
            start = pl.multiple_of((2 * j + place_ref[1]) * HDIM, HDIM)
            key = key_ref[:, pl.ds(start, HDIM)]
            value = value_ref[:, pl.ds(start, HDIM)]
            for i in range(j, count, SUB):
                out[i * depth : (i + 1) * depth, :HDIM] = key
                out[i * depth : (i + 1) * depth, HDIM:] = value

    shape = jax.ShapeDtypeStruct((count * depth, 2 * HDIM), BF16)
    moved = count * depth * 2 * HDIM * 4
    return call(kernel, "pack_keys_values", shape, [SMEM, VMEM, VMEM], VMEM, LIMIT, 0, moved)(place, w_key, w_value)


def pack_queries(place, w_query):
    depth = w_query.shape[0]

    def kernel(place_ref, query_ref, *outs):
        for r, out in enumerate(outs):
            start = pl.multiple_of(jnp.bitwise_xor(place_ref[0], r) * 2 * HDIM, 2 * HDIM)
            out[...] = query_ref[:, pl.ds(start, 2 * HDIM)]

    shapes = [jax.ShapeDtypeStruct((depth, 2 * HDIM), BF16)] * SUB
    moved = SUB * depth * 2 * HDIM * 4
    return call(kernel, "pack_queries", shapes, [SMEM, VMEM], [VMEM] * SUB, LIMIT, 0, moved)(place, w_query)


def stage_rows(place, w_out, w_far):
    rows, width = w_out.shape
    depth, half = rows // SUB, width // 2

    def kernel(place_ref, out_ref, far_ref, keep, far, sems):
        column = pl.multiple_of(place_ref[2] * half, half)
        copies = []
        for r in range(SUB):
            row = pl.multiple_of(jnp.bitwise_xor(place_ref[0], r) * depth, depth)
            for i, (source, target) in enumerate(((out_ref, keep), (far_ref, far))):
                block = source.at[pl.ds(row, depth), pl.ds(column, half)]
                copies.append(pltpu.make_async_copy(block, target.at[r], sems.at[2 * r + i]))
        for copy in copies:
            copy.start()
        for copy in copies:
            copy.wait()

    shapes = [pltpu.VMEM((SUB, depth, half), BF16)] * 2
    sems = pltpu.SemaphoreType.DMA((2 * SUB,))
    return call(kernel, "stage_rows", shapes, [SMEM, ANY, ANY], [VMEM] * 2, 40, 0, rows * width * 4, [sems])(
        place, w_out, w_far
    )


def stage(place, pieces, blocks, rows, width):
    count = len(pieces)
    half = width // 2

    def kernel(place_ref, *refs):
        out, sems = refs[count], refs[count + 1]
        copies = []
        for i, ((array, r, column, far), ref) in enumerate(zip(pieces, refs)):
            if far is None:
                target = out.at[r]
            else:
                core = 1 - place_ref[2] if far else place_ref[2]
                start = pl.multiple_of(core * half + column, HDIM)
                target = out.at[r, :, pl.ds(start, array.shape[1])]
            copies.append(pltpu.make_async_copy(ref, target, sems.at[i]))
        for copy in copies:
            copy.start()
        for copy in copies:
            copy.wait()

    shape = pltpu.VMEM((blocks, rows, width), BF16)
    sems = pltpu.SemaphoreType.DMA((count,))
    moved = blocks * rows * width * 4
    return call(kernel, "stage", shape, [SMEM] + [ANY] * count, VMEM, 20 if blocks > 1 else LIMIT, 0, moved, [sems])(
        place, *[piece[0] for piece in pieces]
    )


def project(stream, kv, total=None):
    blocks, rows, width = stream.shape
    kv = kv if isinstance(kv, list) else [kv]
    cuts = [sum(w.shape[0] for w in kv[:i]) for i in range(len(kv) + 1)]

    def kernel(stream_ref, *refs):
        key_ref, value_ref, state_ref, total_ref = refs[-4:]
        for r in range(blocks):
            both = sum(dot(stream_ref[r, :, cuts[i] : cuts[i + 1]], refs[i][...]) for i in range(len(kv)))
            key_ref[r] = silu(both[:, :HDIM]).astype(BF16)
            value_ref[r] = both[:, HDIM:].astype(BF16)
        added = jnp.zeros((HDIM, HDIM), F32) if total is None else refs[len(kv)][...]
        for r in range(blocks):
            state = dot(key_ref[r], value_ref[r], ((0,), (0,)))
            state_ref[r] = state
            added = added + state
        total_ref[...] = added

    shape = jax.ShapeDtypeStruct((blocks, rows, HDIM), BF16)
    state = jax.ShapeDtypeStruct((blocks, HDIM, HDIM), F32)
    shapes = [shape, shape, state, jax.ShapeDtypeStruct((HDIM, HDIM), F32)]
    args = [stream, *kv] + ([] if total is None else [total])
    flops = 4 * blocks * rows * width * HDIM
    return call(kernel, "project", shapes, [VMEM] * len(args), [VMEM] * 4, LIMIT, flops, 2 * MIB)(*args)


def flat_blocks(streams):
    return [(stream, r) for stream in streams for r in range(stream.shape[0])]


def weighted(place_ref, source, r, refs, parts, base):
    total = base
    for ref, (weight, start) in zip(refs, parts):
        depth = weight.shape[0]
        if isinstance(start, tuple):
            lanes = pl.ds(pl.multiple_of(jnp.bitwise_xor(place_ref[3], start[0]) * depth, HDIM), depth)
        else:
            lanes = slice(start, start + depth)
        term = dot(source[r, :, lanes], ref[...])
        total = term if total is None else total + term
    return total


def run_blocks(kernel, name, place, streams, parts, base, out_shape, more=()):
    rows, width = streams[0].shape[1:]
    count = len(streams)
    args = [*streams, *[weight for weight, _ in parts], *([] if base is None else [base])]
    given = len(args)
    args += more

    def body(place_ref, *refs):
        weights = refs[count : count + len(parts)]
        base_ref = None if base is None else refs[given - 1]

        def sums():
            for i, (source, r) in enumerate(flat_blocks(refs[:count])):
                yield i, weighted(place_ref, source, r, weights, parts, None if base is None else base_ref[i])

        kernel(place_ref, sums, *refs[given:])

    flops = 4 * SUB * rows * sum(weight.shape[0] for weight, _ in parts) * HDIM
    specs = [SMEM] + [VMEM] * len(args)
    outs = [VMEM] * len(out_shape) if isinstance(out_shape, list) else VMEM
    return call(body, name, out_shape, specs, outs, LIMIT, flops, 2 * MIB)(place, *args)


def begin(place, streams, parts, base=None):
    def kernel(place_ref, sums, out):
        for i, total in sums():
            out[i] = total

    shape = pltpu.VMEM((SUB, streams[0].shape[1], 2 * HDIM), F32)
    return run_blocks(kernel, "begin", place, streams, parts, base, shape)


def keys_values(place, streams, parts, base, total):
    rows = streams[0].shape[1]

    def kernel(place_ref, sums, given_ref, key_ref, value_ref, state_ref, total_ref):
        for i, both in sums():
            key_ref[i] = silu(both[:, :HDIM]).astype(BF16)
            value_ref[i] = both[:, HDIM:].astype(BF16)
        added = jnp.zeros((HDIM, HDIM), F32)
        for i in range(SUB):
            state = dot(key_ref[i], value_ref[i], ((0,), (0,)))
            state_ref[i] = state
            added = added + state
        total_ref[0] = given_ref[...]
        total_ref[1] = added

    shape = jax.ShapeDtypeStruct((SUB, rows, HDIM), BF16)
    shapes = [shape, shape] + [jax.ShapeDtypeStruct((n, HDIM, HDIM), F32) for n in (SUB, 2)]
    return run_blocks(kernel, "keys_values", place, streams, parts, base, shapes, [total])


def queries(place, streams, parts, base):
    def kernel(place_ref, sums, out):
        swap = place_ref[1] == 1
        for i, total in sums():
            both = silu(total).astype(BF16)
            out[i, :, :HDIM] = jnp.where(swap, both[:, HDIM:], both[:, :HDIM])
            out[i, :, HDIM:] = jnp.where(swap, both[:, :HDIM], both[:, HDIM:])

    shape = jax.ShapeDtypeStruct((SUB, streams[0].shape[1], 2 * HDIM), BF16)
    return run_blocks(kernel, "queries", place, streams, parts, base, shape)


def attend(place, blocks, query, heads, carried):
    rows = query.shape[1]
    count = len(blocks)
    flat, where = [], []
    for parts in heads:
        index = []
        for part in parts:
            index += [(len(flat), r) for r in range(part[0].shape[0])]
            flat += part
        where.append(index)
    flat.append(carried)

    def kernel(place_ref, query_ref, *refs):
        ins, outs = refs[: len(flat)], refs[len(flat) :]
        causal = lax.broadcasted_iota(jnp.int32, (rows, rows), 1) <= lax.broadcasted_iota(
            jnp.int32, (rows, rows), 0
        )
        block = place_ref[0]
        for i, r in enumerate(blocks):
            for h, index in enumerate(where):
                earlier = ins[-1][h]
                for other in range(SUB):
                    if other != r:
                        is_before = jnp.bitwise_xor(block, other) < jnp.bitwise_xor(block, r)
                        slot, j = index[other]
                        earlier = earlier + jnp.where(is_before, ins[slot + 2][j], 0.0)
                slot, j = index[r]
                key, value = ins[slot][j], ins[slot + 1][j]
                q = query_ref[r, :, h * HDIM : (h + 1) * HDIM]
                scores = dot(q, key, ((1,), (1,)))
                weights = jnp.where(causal, scores, 0.0).astype(BF16)
                mixed = dot(weights, value) + dot(q, earlier.astype(BF16))
                scale = lax.rsqrt(jnp.mean(mixed * mixed, axis=-1, keepdims=True) + 1e-06)
                target = pl.multiple_of(jnp.bitwise_xor(place_ref[1], h) * HDIM, HDIM)
                outs[i][:, pl.ds(target, HDIM)] = (mixed * scale).astype(BF16)

    shapes = [jax.ShapeDtypeStruct((rows, 2 * HDIM), BF16)] * count
    flops = count * 4 * rows * HDIM * (2 * rows + HDIM)
    specs = [SMEM] + [VMEM] * (1 + len(flat))
    return call(kernel, "attend", shapes, specs, [VMEM] * count, LIMIT, flops, 2 * MIB)(place, query, *flat)


def add_features(pieces, weight, partial=None):
    rows, depth = pieces[0].shape
    width = weight.shape[2]
    count = len(pieces)
    tile = min(512, width)

    def kernel(*refs):
        w_ref, out = refs[count], refs[-1]
        for start in range(0, width, tile):
            columns = slice(start, start + tile)
            total = refs[count + 1][:, columns] if partial is not None else jnp.zeros((rows, tile), F32)
            for i in range(count):
                total = total + dot(refs[i][...], w_ref[i, :, columns])
            out[:, columns] = total.astype(out.dtype)

    shape = pltpu.VMEM((rows, width), F32) if partial is None else jax.ShapeDtypeStruct((rows, width), BF16)
    args = [*pieces, weight] + ([] if partial is None else [partial])
    flops = 2 * count * depth * rows * width
    return call(kernel, "add_features", shape, [VMEM] * len(args), VMEM, LIMIT, flops, 8 * MIB)(*args)


def exclusive_prefix(value, groups):
    def shift(v, step):
        pairs = [(g * SUB + j, (g + step) * SUB + j) for g in range(groups - step) for j in range(SUB)]
        return lax.ppermute(v, "ctx", pairs)

    if groups == 1:
        return jnp.zeros_like(value)
    total = shift(value, 1)
    step = 1
    while step < groups - 1:
        total = total + shift(total, step)
        step *= 2
    return total


def local(tokens, w_query, w_key, w_value, w_out):
    n_ctx = lax.axis_size("ctx")
    groups = n_ctx // SUB
    rows, half = tokens.shape
    ctx = lax.axis_index("ctx")
    place = jnp.stack([ctx % SUB, lax.axis_index("groups"), lax.axis_index("head"), ctx]).astype(jnp.int32)

    def xor(value, step):
        return lax.ppermute(value, "ctx", [(i, i ^ step) for i in range(n_ctx)])

    def other_part(value):
        return lax.ppermute(value, "groups", [(0, 1), (1, 0)])

    def other_core(value):
        return lax.ppermute(value, "head", [(0, 1), (1, 0)])

    def spread(packed):
        return lax.all_to_all(packed, "ctx", 0, 0, tiled=True)

    def gather_queries(sent):
        ordered = [lax.dynamic_index_in_dim(jnp.stack(sent), (ctx % SUB) ^ j, keepdims=False) for j in range(SUB)]
        return spread(jnp.concatenate(ordered * groups, axis=0))

    cut = half * 11 // 16 // HDIM * HDIM
    pieced = n_ctx == 2 * SUB
    ob = lax.optimization_barrier

    across = xor(tokens, 2)
    beside = xor(tokens, 1)
    kv_mine = spread(pack_keys_values(place, w_key, w_value, n_ctx))
    far_tokens = other_core(tokens)
    w_far = other_core(w_out)
    beside, far_tokens, w_far, w_query = ob((beside, far_tokens, w_far, w_query))
    q_sent = pack_queries(place, w_query)
    far_beside = other_core(beside)

    def fetch(sent, *steps):
        if pieced:
            arrived.update({m: xor(sent[m % SUB], m) for m in steps})

    arrived = {0: q_sent[0]}
    fetch(q_sent, 1)
    beside_cut = beside[:, cut:]
    across, kv_mine, beside, far_beside, q_sent, arrived, beside_cut = ob(
        (across, kv_mine, beside, far_beside, q_sent, arrived, beside_cut)
    )
    middle = kv_mine.shape[0] // 2
    kv_upper = other_part(kv_mine[:middle])
    left = xor(across[:, :cut], 1)
    right = xor(beside_cut, 2)
    fetch(q_sent, 4, 6)
    near = [(tokens, 0, 0, 0), (far_tokens, 0, 0, 1), (beside, 1, 0, 0), (far_beside, 1, 0, 1)]
    near += [(across, 2, 0, 0), (other_core(across), 2, 0, 1)]
    near = stage(place, near, SUB - 1, rows, 2 * half)
    first = project(near, kv_mine)
    left, right, arrived, kv_upper, kv_mine, q_sent, first = ob(
        (left, right, arrived, kv_upper, kv_mine, q_sent, first)
    )
    kv_lower = other_part(kv_mine[middle:])
    fetch(q_sent, 5, 7)
    far_left, far_right = other_core(left), other_core(right)
    far_left, q_sent = ob((far_left, q_sent))
    fetch(q_sent, 3, 2)
    corner = [(left, 0, 0, 0), (far_left, 0, 0, 1), (right, 0, cut, 0), (far_right, 0, cut, 1)]
    corner = stage(place, corner, 1, rows, 2 * half)

    streams = [near, corner]
    last = project(corner, kv_mine, first[3])
    kv_base = begin(place, streams, [(kv_upper, 0)])
    if pieced:
        early = (0, 1, 4, 6)
        q_base = begin(place, streams, [(arrived[m], (m,)) for m in early])
        latest = arrived.pop(7)
        arrived, kv_lower, kv_base, q_base = ob((arrived, kv_lower, kv_base, q_base))
        q_base = begin(place, streams, [(arrived[m], (m,)) for m in sorted(arrived) if m not in early], q_base)
        q_parts = [(latest, (7,))]
    else:
        q_base, q_parts = None, [(gather_queries(q_sent), 0)]
    *second, totals = keys_values(place, streams, [(kv_lower, middle)], kv_base, last[3])
    carried = exclusive_prefix(totals, groups)
    heads = [[first[:3], last[:3]], [second]]
    query = queries(place, streams, q_parts, q_base)
    normed = [attend(place, (r,), query, heads, carried)[0] for r in (3, 1, 2, 0)]
    normed = [normed[3], xor(normed[1], 1), xor(normed[2], 2), xor(normed[0], 3)]
    home_0, w_far = lax.optimization_barrier((normed[0], w_far))
    out_keep, out_far = stage_rows(place, w_out, w_far)
    out_keep, out_far, *normed = lax.optimization_barrier((out_keep, out_far, home_0, *normed[1:]))
    partial = add_features(normed, out_keep)
    return add_features([other_core(n) for n in normed], out_far, partial)


def solution(mesh):
    in_specs = (
        P(("groups", "ctx"), "head"),
        P("ctx", "head"),
        P("ctx", "head"),
        P("ctx", "head"),
        P("head", None),
    )
    out_specs = P(("groups", "ctx"), "head")
    return jax.shard_map(local, mesh=mesh, in_specs=in_specs, out_specs=out_specs, check_vma=False)
```

```python
import jax
import jax.numpy as jnp
from jax import lax
from jax.experimental import pallas as pl
from jax.experimental.pallas import tpu as pltpu
from jax.sharding import PartitionSpec as P

HDIM = 128
SUB = 4
F32 = jnp.float32
BF16 = jnp.bfloat16
MIB = 1 << 20
LIMIT = 8
ANY = pl.BlockSpec(memory_space=pl.ANY)
VMEM = pl.BlockSpec(memory_space=pltpu.VMEM)
SMEM = pl.BlockSpec(memory_space=pltpu.SMEM)


def dot(a, b, contract=((1,), (0,))):
    return lax.dot_general(a, b, (contract, ((), ())), preferred_element_type=F32)


def silu(u):
    return u / (1.0 + jnp.exp(-u))


def call(kernel, name, out_shape, in_specs, out_specs, limit, flops, moved, scratch=()):
    return pl.pallas_call(
        kernel,
        out_shape=out_shape,
        in_specs=in_specs,
        out_specs=out_specs,
        scratch_shapes=list(scratch),
        compiler_params=pltpu.CompilerParams(vmem_limit_bytes=limit * MIB),
        cost_estimate=pl.CostEstimate(flops=int(flops), bytes_accessed=int(moved), transcendentals=0),
        name=name,
    )


def pack_keys_values(place, w_key, w_value, count):
    depth = w_key.shape[0]

    def kernel(place_ref, key_ref, value_ref, out):
        for j in range(SUB):
            start = pl.multiple_of((2 * j + place_ref[1]) * HDIM, HDIM)
            key = key_ref[:, pl.ds(start, HDIM)]
            value = value_ref[:, pl.ds(start, HDIM)]
            for i in range(j, count, SUB):
                out[i * depth : (i + 1) * depth, :HDIM] = key
                out[i * depth : (i + 1) * depth, HDIM:] = value

    shape = jax.ShapeDtypeStruct((count * depth, 2 * HDIM), BF16)
    moved = count * depth * 2 * HDIM * 4
    return call(kernel, "pack_keys_values", shape, [SMEM, VMEM, VMEM], VMEM, LIMIT, 0, moved)(place, w_key, w_value)


def pack_queries(place, w_query):
    depth = w_query.shape[0]

    def kernel(place_ref, query_ref, *outs):
        for r, out in enumerate(outs):
            start = pl.multiple_of(jnp.bitwise_xor(place_ref[0], r) * 2 * HDIM, 2 * HDIM)
            out[...] = query_ref[:, pl.ds(start, 2 * HDIM)]

    shapes = [jax.ShapeDtypeStruct((depth, 2 * HDIM), BF16)] * SUB
    moved = SUB * depth * 2 * HDIM * 4
    return call(kernel, "pack_queries", shapes, [SMEM, VMEM], [VMEM] * SUB, LIMIT, 0, moved)(place, w_query)


def stage_rows(place, w_out, w_far):
    rows, width = w_out.shape
    depth, half = rows // SUB, width // 2

    def kernel(place_ref, out_ref, far_ref, keep, far, sems):
        column = pl.multiple_of(place_ref[2] * half, half)
        copies = []
        for r in range(SUB):
            row = pl.multiple_of(jnp.bitwise_xor(place_ref[0], r) * depth, depth)
            for i, (source, target) in enumerate(((out_ref, keep), (far_ref, far))):
                block = source.at[pl.ds(row, depth), pl.ds(column, half)]
                copies.append(pltpu.make_async_copy(block, target.at[r], sems.at[2 * r + i]))
        for copy in copies:
            copy.start()
        for copy in copies:
            copy.wait()

    shapes = [pltpu.VMEM((SUB, depth, half), BF16)] * 2
    sems = pltpu.SemaphoreType.DMA((2 * SUB,))
    return call(kernel, "stage_rows", shapes, [SMEM, ANY, ANY], [VMEM] * 2, 40, 0, rows * width * 4, [sems])(
        place, w_out, w_far
    )


def stage(place, pieces, blocks, rows, width):
    count = len(pieces)
    half = width // 2

    def kernel(place_ref, *refs):
        out, sems = refs[count], refs[count + 1]
        copies = []
        for i, ((array, r, column, far), ref) in enumerate(zip(pieces, refs)):
            if far is None:
                target = out.at[r]
            else:
                core = 1 - place_ref[2] if far else place_ref[2]
                start = pl.multiple_of(core * half + column, HDIM)
                target = out.at[r, :, pl.ds(start, array.shape[1])]
            copies.append(pltpu.make_async_copy(ref, target, sems.at[i]))
        for copy in copies:
            copy.start()
        for copy in copies:
            copy.wait()

    shape = pltpu.VMEM((blocks, rows, width), BF16)
    sems = pltpu.SemaphoreType.DMA((count,))
    moved = blocks * rows * width * 4
    return call(kernel, "stage", shape, [SMEM] + [ANY] * count, VMEM, 20 if blocks > 1 else LIMIT, 0, moved, [sems])(
        place, *[piece[0] for piece in pieces]
    )


def project(stream, kv, total=None):
    blocks, rows, width = stream.shape
    kv = kv if isinstance(kv, list) else [kv]
    cuts = [sum(w.shape[0] for w in kv[:i]) for i in range(len(kv) + 1)]

    def kernel(stream_ref, *refs):
        key_ref, value_ref, state_ref, total_ref = refs[-4:]
        for r in range(blocks):
            both = sum(dot(stream_ref[r, :, cuts[i] : cuts[i + 1]], refs[i][...]) for i in range(len(kv)))
            key_ref[r] = silu(both[:, :HDIM]).astype(BF16)
            value_ref[r] = both[:, HDIM:].astype(BF16)
        added = jnp.zeros((HDIM, HDIM), F32) if total is None else refs[len(kv)][...]
        for r in range(blocks):
            state = dot(key_ref[r], value_ref[r], ((0,), (0,)))
            state_ref[r] = state
            added = added + state
        total_ref[...] = added

    shape = jax.ShapeDtypeStruct((blocks, rows, HDIM), BF16)
    state = jax.ShapeDtypeStruct((blocks, HDIM, HDIM), F32)
    shapes = [shape, shape, state, jax.ShapeDtypeStruct((HDIM, HDIM), F32)]
    args = [stream, *kv] + ([] if total is None else [total])
    flops = 4 * blocks * rows * width * HDIM
    return call(kernel, "project", shapes, [VMEM] * len(args), [VMEM] * 4, LIMIT, flops, 2 * MIB)(*args)


def flat_blocks(streams):
    return [(stream, r) for stream in streams for r in range(stream.shape[0])]


def weighted(place_ref, source, r, refs, parts, base):
    total = base
    for ref, (weight, start) in zip(refs, parts):
        depth = weight.shape[0]
        if isinstance(start, tuple):
            lanes = pl.ds(pl.multiple_of(jnp.bitwise_xor(place_ref[3], start[0]) * depth, HDIM), depth)
        else:
            lanes = slice(start, start + depth)
        term = dot(source[r, :, lanes], ref[...])
        total = term if total is None else total + term
    return total


def run_blocks(kernel, name, place, streams, parts, base, out_shape, more=()):
    rows, width = streams[0].shape[1:]
    count = len(streams)
    args = [*streams, *[weight for weight, _ in parts], *([] if base is None else [base])]
    given = len(args)
    args += more

    def body(place_ref, *refs):
        weights = refs[count : count + len(parts)]
        base_ref = None if base is None else refs[given - 1]

        def sums():
            for i, (source, r) in enumerate(flat_blocks(refs[:count])):
                yield i, weighted(place_ref, source, r, weights, parts, None if base is None else base_ref[i])

        kernel(place_ref, sums, *refs[given:])

    flops = 4 * SUB * rows * sum(weight.shape[0] for weight, _ in parts) * HDIM
    specs = [SMEM] + [VMEM] * len(args)
    outs = [VMEM] * len(out_shape) if isinstance(out_shape, list) else VMEM
    return call(body, name, out_shape, specs, outs, LIMIT, flops, 2 * MIB)(place, *args)


def begin(place, streams, parts, base=None):
    def kernel(place_ref, sums, out):
        for i, total in sums():
            out[i] = total

    shape = pltpu.VMEM((SUB, streams[0].shape[1], 2 * HDIM), F32)
    return run_blocks(kernel, "begin", place, streams, parts, base, shape)


def keys_values(place, streams, parts, base, total):
    rows = streams[0].shape[1]

    def kernel(place_ref, sums, given_ref, key_ref, value_ref, state_ref, total_ref):
        for i, both in sums():
            key_ref[i] = silu(both[:, :HDIM]).astype(BF16)
            value_ref[i] = both[:, HDIM:].astype(BF16)
        added = jnp.zeros((HDIM, HDIM), F32)
        for i in range(SUB):
            state = dot(key_ref[i], value_ref[i], ((0,), (0,)))
            state_ref[i] = state
            added = added + state
        total_ref[0] = given_ref[...]
        total_ref[1] = added

    shape = jax.ShapeDtypeStruct((SUB, rows, HDIM), BF16)
    shapes = [shape, shape] + [jax.ShapeDtypeStruct((n, HDIM, HDIM), F32) for n in (SUB, 2)]
    return run_blocks(kernel, "keys_values", place, streams, parts, base, shapes, [total])


def queries(place, streams, parts, base):
    def kernel(place_ref, sums, out):
        swap = place_ref[1] == 1
        for i, total in sums():
            both = silu(total).astype(BF16)
            out[i, :, :HDIM] = jnp.where(swap, both[:, HDIM:], both[:, :HDIM])
            out[i, :, HDIM:] = jnp.where(swap, both[:, :HDIM], both[:, HDIM:])

    shape = jax.ShapeDtypeStruct((SUB, streams[0].shape[1], 2 * HDIM), BF16)
    return run_blocks(kernel, "queries", place, streams, parts, base, shape)


def attend(place, blocks, query, heads, carried):
    rows = query.shape[1]
    count = len(blocks)
    flat, where = [], []
    for parts in heads:
        index = []
        for part in parts:
            index += [(len(flat), r) for r in range(part[0].shape[0])]
            flat += part
        where.append(index)
    flat.append(carried)

    def kernel(place_ref, query_ref, *refs):
        ins, outs = refs[: len(flat)], refs[len(flat) :]
        causal = lax.broadcasted_iota(jnp.int32, (rows, rows), 1) <= lax.broadcasted_iota(
            jnp.int32, (rows, rows), 0
        )
        block = place_ref[0]
        for i, r in enumerate(blocks):
            for h, index in enumerate(where):
                earlier = ins[-1][h]
                for other in range(SUB):
                    if other != r:
                        is_before = jnp.bitwise_xor(block, other) < jnp.bitwise_xor(block, r)
                        slot, j = index[other]
                        earlier = earlier + jnp.where(is_before, ins[slot + 2][j], 0.0)
                slot, j = index[r]
                key, value = ins[slot][j], ins[slot + 1][j]
                q = query_ref[r, :, h * HDIM : (h + 1) * HDIM]
                scores = dot(q, key, ((1,), (1,)))
                weights = jnp.where(causal, scores, 0.0).astype(BF16)
                mixed = dot(weights, value) + dot(q, earlier.astype(BF16))
                scale = lax.rsqrt(jnp.mean(mixed * mixed, axis=-1, keepdims=True) + 1e-06)
                target = pl.multiple_of(jnp.bitwise_xor(place_ref[1], h) * HDIM, HDIM)
                outs[i][:, pl.ds(target, HDIM)] = (mixed * scale).astype(BF16)

    shapes = [jax.ShapeDtypeStruct((rows, 2 * HDIM), BF16)] * count
    flops = count * 4 * rows * HDIM * (2 * rows + HDIM)
    specs = [SMEM] + [VMEM] * (1 + len(flat))
    return call(kernel, "attend", shapes, specs, [VMEM] * count, LIMIT, flops, 2 * MIB)(place, query, *flat)


def add_features(pieces, weight, partial=None):
    rows, depth = pieces[0].shape
    width = weight.shape[2]
    count = len(pieces)
    tile = min(512, width)

    def kernel(*refs):
        w_ref, out = refs[count], refs[-1]
        for start in range(0, width, tile):
            columns = slice(start, start + tile)
            total = refs[count + 1][:, columns] if partial is not None else jnp.zeros((rows, tile), F32)
            for i in range(count):
                total = total + dot(refs[i][...], w_ref[i, :, columns])
            out[:, columns] = total.astype(out.dtype)

    shape = pltpu.VMEM((rows, width), F32) if partial is None else jax.ShapeDtypeStruct((rows, width), BF16)
    args = [*pieces, weight] + ([] if partial is None else [partial])
    flops = 2 * count * depth * rows * width
    return call(kernel, "add_features", shape, [VMEM] * len(args), VMEM, LIMIT, flops, 8 * MIB)(*args)


def exclusive_prefix(value, groups):
    def shift(v, step):
        pairs = [(g * SUB + j, (g + step) * SUB + j) for g in range(groups - step) for j in range(SUB)]
        return lax.ppermute(v, "ctx", pairs)

    if groups == 1:
        return jnp.zeros_like(value)
    total = shift(value, 1)
    step = 1
    while step < groups - 1:
        total = total + shift(total, step)
        step *= 2
    return total


def local(tokens, w_query, w_key, w_value, w_out):
    n_ctx = lax.axis_size("ctx")
    groups = n_ctx // SUB
    rows, half = tokens.shape
    ctx = lax.axis_index("ctx")
    place = jnp.stack([ctx % SUB, lax.axis_index("groups"), lax.axis_index("head"), ctx]).astype(jnp.int32)

    def xor(value, step):
        return lax.ppermute(value, "ctx", [(i, i ^ step) for i in range(n_ctx)])

    def other_part(value):
        return lax.ppermute(value, "groups", [(0, 1), (1, 0)])

    def other_core(value):
        return lax.ppermute(value, "head", [(0, 1), (1, 0)])

    def spread(packed):
        return lax.all_to_all(packed, "ctx", 0, 0, tiled=True)

    def gather_queries(sent):
        ordered = [lax.dynamic_index_in_dim(jnp.stack(sent), (ctx % SUB) ^ j, keepdims=False) for j in range(SUB)]
        return spread(jnp.concatenate(ordered * groups, axis=0))

    cut = half * 11 // 16 // HDIM * HDIM
    pieced = n_ctx == 2 * SUB
    ob = lax.optimization_barrier

    across = xor(tokens, 2)
    beside = xor(tokens, 1)
    kv_mine = spread(pack_keys_values(place, w_key, w_value, n_ctx))
    far_tokens = other_core(tokens)
    w_far = other_core(w_out)
    beside, far_tokens, w_far, w_query = ob((beside, far_tokens, w_far, w_query))
    q_sent = pack_queries(place, w_query)
    far_beside = other_core(beside)

    def fetch(sent, *steps):
        if pieced:
            arrived.update({m: xor(sent[m % SUB], m) for m in steps})

    arrived = {0: q_sent[0]}
    fetch(q_sent, 1)
    beside_cut = beside[:, cut:]
    across, kv_mine, beside, far_beside, q_sent, arrived, beside_cut = ob(
        (across, kv_mine, beside, far_beside, q_sent, arrived, beside_cut)
    )
    middle = kv_mine.shape[0] // 2
    kv_upper = other_part(kv_mine[:middle])
    left = xor(across[:, :cut], 1)
    right = xor(beside_cut, 2)
    fetch(q_sent, 4, 6)
    near = [(tokens, 0, 0, 0), (far_tokens, 0, 0, 1), (beside, 1, 0, 0), (far_beside, 1, 0, 1)]
    near += [(across, 2, 0, 0), (other_core(across), 2, 0, 1)]
    near = stage(place, near, SUB - 1, rows, 2 * half)
    first = project(near, kv_mine)
    left, right, arrived, kv_upper, kv_mine, q_sent, first = ob(
        (left, right, arrived, kv_upper, kv_mine, q_sent, first)
    )
    kv_lower = other_part(kv_mine[middle:])
    fetch(q_sent, 5, 7)
    far_left, far_right = other_core(left), other_core(right)
    far_left, q_sent = ob((far_left, q_sent))
    fetch(q_sent, 3, 2)
    corner = [(left, 0, 0, 0), (far_left, 0, 0, 1), (right, 0, cut, 0), (far_right, 0, cut, 1)]
    corner = stage(place, corner, 1, rows, 2 * half)

    streams = [near, corner]
    last = project(corner, kv_mine, first[3])
    kv_base = begin(place, streams, [(kv_upper, 0)])
    if pieced:
        early = (0, 1, 4, 6)
        q_base = begin(place, streams, [(arrived[m], (m,)) for m in early])
        latest = {m: arrived.pop(m) for m in (3, 7)}
        arrived, kv_lower, kv_base, q_base = ob((arrived, kv_lower, kv_base, q_base))
        q_base = begin(place, streams, [(arrived[m], (m,)) for m in sorted(arrived) if m not in early], q_base)
        q_parts = [(piece, (m,)) for m, piece in latest.items()]
    else:
        q_base, q_parts = None, [(gather_queries(q_sent), 0)]
    *second, totals = keys_values(place, streams, [(kv_lower, middle)], kv_base, last[3])
    carried = exclusive_prefix(totals, groups)
    heads = [[first[:3], last[:3]], [second]]
    query = queries(place, streams, q_parts, q_base)
    normed = [attend(place, (r,), query, heads, carried)[0] for r in (3, 1, 2, 0)]
    normed = [normed[3], xor(normed[1], 1), xor(normed[2], 2), xor(normed[0], 3)]
    home_0, w_far = lax.optimization_barrier((normed[0], w_far))
    out_keep, out_far = stage_rows(place, w_out, w_far)
    out_keep, out_far, *normed = lax.optimization_barrier((out_keep, out_far, home_0, *normed[1:]))
    partial = add_features(normed, out_keep)
    return add_features([other_core(n) for n in normed], out_far, partial)


def solution(mesh):
    in_specs = (
        P(("groups", "ctx"), "head"),
        P("ctx", "head"),
        P("ctx", "head"),
        P("ctx", "head"),
        P("head", None),
    )
    out_specs = P(("groups", "ctx"), "head")
    return jax.shard_map(local, mesh=mesh, in_specs=in_specs, out_specs=out_specs, check_vma=False)
```

```python
import jax
import jax.numpy as jnp
from jax import lax
from jax.experimental import pallas as pl
from jax.experimental.pallas import tpu as pltpu
from jax.sharding import PartitionSpec as P

HDIM = 128
SUB = 4
F32 = jnp.float32
BF16 = jnp.bfloat16
MIB = 1 << 20
LIMIT = 8
ANY = pl.BlockSpec(memory_space=pl.ANY)
VMEM = pl.BlockSpec(memory_space=pltpu.VMEM)
SMEM = pl.BlockSpec(memory_space=pltpu.SMEM)


def dot(a, b, contract=((1,), (0,))):
    return lax.dot_general(a, b, (contract, ((), ())), preferred_element_type=F32)


def silu(u):
    return u / (1.0 + jnp.exp(-u))


def call(kernel, name, out_shape, in_specs, out_specs, limit, flops, moved, scratch=()):
    return pl.pallas_call(
        kernel,
        out_shape=out_shape,
        in_specs=in_specs,
        out_specs=out_specs,
        scratch_shapes=list(scratch),
        compiler_params=pltpu.CompilerParams(vmem_limit_bytes=limit * MIB),
        cost_estimate=pl.CostEstimate(flops=int(flops), bytes_accessed=int(moved), transcendentals=0),
        name=name,
    )


def pack_keys_values(place, w_key, w_value, count):
    depth = w_key.shape[0]

    def kernel(place_ref, key_ref, value_ref, out):
        for j in range(SUB):
            start = pl.multiple_of((2 * j + place_ref[1]) * HDIM, HDIM)
            key = key_ref[:, pl.ds(start, HDIM)]
            value = value_ref[:, pl.ds(start, HDIM)]
            for i in range(j, count, SUB):
                out[i * depth : (i + 1) * depth, :HDIM] = key
                out[i * depth : (i + 1) * depth, HDIM:] = value

    shape = jax.ShapeDtypeStruct((count * depth, 2 * HDIM), BF16)
    moved = count * depth * 2 * HDIM * 4
    return call(kernel, "pack_keys_values", shape, [SMEM, VMEM, VMEM], VMEM, LIMIT, 0, moved)(place, w_key, w_value)


def pack_queries(place, w_query):
    depth = w_query.shape[0]

    def kernel(place_ref, query_ref, *outs):
        for r, out in enumerate(outs):
            start = pl.multiple_of(jnp.bitwise_xor(place_ref[0], r) * 2 * HDIM, 2 * HDIM)
            out[...] = query_ref[:, pl.ds(start, 2 * HDIM)]

    shapes = [jax.ShapeDtypeStruct((depth, 2 * HDIM), BF16)] * SUB
    moved = SUB * depth * 2 * HDIM * 4
    return call(kernel, "pack_queries", shapes, [SMEM, VMEM], [VMEM] * SUB, LIMIT, 0, moved)(place, w_query)


def stage_rows(place, w_out, w_far):
    rows, width = w_out.shape
    depth, half = rows // SUB, width // 2

    def kernel(place_ref, out_ref, far_ref, keep, far, sems):
        column = pl.multiple_of(place_ref[2] * half, half)
        copies = []
        for r in range(SUB):
            row = pl.multiple_of(jnp.bitwise_xor(place_ref[0], r) * depth, depth)
            for i, (source, target) in enumerate(((out_ref, keep), (far_ref, far))):
                block = source.at[pl.ds(row, depth), pl.ds(column, half)]
                copies.append(pltpu.make_async_copy(block, target.at[r], sems.at[2 * r + i]))
        for copy in copies:
            copy.start()
        for copy in copies:
            copy.wait()

    shapes = [pltpu.VMEM((SUB, depth, half), BF16)] * 2
    sems = pltpu.SemaphoreType.DMA((2 * SUB,))
    return call(kernel, "stage_rows", shapes, [SMEM, ANY, ANY], [VMEM] * 2, 40, 0, rows * width * 4, [sems])(
        place, w_out, w_far
    )


def stage(place, pieces, blocks, rows, width):
    count = len(pieces)
    half = width // 2

    def kernel(place_ref, *refs):
        out, sems = refs[count], refs[count + 1]
        copies = []
        for i, ((array, r, column, far), ref) in enumerate(zip(pieces, refs)):
            if far is None:
                target = out.at[r]
            else:
                core = 1 - place_ref[2] if far else place_ref[2]
                start = pl.multiple_of(core * half + column, HDIM)
                target = out.at[r, :, pl.ds(start, array.shape[1])]
            copies.append(pltpu.make_async_copy(ref, target, sems.at[i]))
        for copy in copies:
            copy.start()
        for copy in copies:
            copy.wait()

    shape = pltpu.VMEM((blocks, rows, width), BF16)
    sems = pltpu.SemaphoreType.DMA((count,))
    moved = blocks * rows * width * 4
    return call(kernel, "stage", shape, [SMEM] + [ANY] * count, VMEM, 20 if blocks > 1 else LIMIT, 0, moved, [sems])(
        place, *[piece[0] for piece in pieces]
    )


def project(stream, kv, total=None):
    blocks, rows, width = stream.shape
    kv = kv if isinstance(kv, list) else [kv]
    cuts = [sum(w.shape[0] for w in kv[:i]) for i in range(len(kv) + 1)]

    def kernel(stream_ref, *refs):
        key_ref, value_ref, state_ref, total_ref = refs[-4:]
        for r in range(blocks):
            both = sum(dot(stream_ref[r, :, cuts[i] : cuts[i + 1]], refs[i][...]) for i in range(len(kv)))
            key_ref[r] = silu(both[:, :HDIM]).astype(BF16)
            value_ref[r] = both[:, HDIM:].astype(BF16)
        added = jnp.zeros((HDIM, HDIM), F32) if total is None else refs[len(kv)][...]
        for r in range(blocks):
            state = dot(key_ref[r], value_ref[r], ((0,), (0,)))
            state_ref[r] = state
            added = added + state
        total_ref[...] = added

    shape = jax.ShapeDtypeStruct((blocks, rows, HDIM), BF16)
    state = jax.ShapeDtypeStruct((blocks, HDIM, HDIM), F32)
    shapes = [shape, shape, state, jax.ShapeDtypeStruct((HDIM, HDIM), F32)]
    args = [stream, *kv] + ([] if total is None else [total])
    flops = 4 * blocks * rows * width * HDIM
    return call(kernel, "project", shapes, [VMEM] * len(args), [VMEM] * 4, LIMIT, flops, 2 * MIB)(*args)


def flat_blocks(streams):
    return [(stream, r) for stream in streams for r in range(stream.shape[0])]


def weighted(place_ref, source, r, refs, parts, base):
    total = base
    for ref, (weight, start) in zip(refs, parts):
        depth = weight.shape[0]
        if isinstance(start, tuple):
            lanes = pl.ds(pl.multiple_of(jnp.bitwise_xor(place_ref[3], start[0]) * depth, HDIM), depth)
        else:
            lanes = slice(start, start + depth)
        term = dot(source[r, :, lanes], ref[...])
        total = term if total is None else total + term
    return total


def run_blocks(kernel, name, place, streams, parts, base, out_shape, more=()):
    rows, width = streams[0].shape[1:]
    count = len(streams)
    args = [*streams, *[weight for weight, _ in parts], *([] if base is None else [base])]
    given = len(args)
    args += more

    def body(place_ref, *refs):
        weights = refs[count : count + len(parts)]
        base_ref = None if base is None else refs[given - 1]

        def sums():
            for i, (source, r) in enumerate(flat_blocks(refs[:count])):
                yield i, weighted(place_ref, source, r, weights, parts, None if base is None else base_ref[i])

        kernel(place_ref, sums, *refs[given:])

    flops = 4 * SUB * rows * sum(weight.shape[0] for weight, _ in parts) * HDIM
    specs = [SMEM] + [VMEM] * len(args)
    outs = [VMEM] * len(out_shape) if isinstance(out_shape, list) else VMEM
    return call(body, name, out_shape, specs, outs, LIMIT, flops, 2 * MIB)(place, *args)


def begin(place, streams, parts, base=None):
    def kernel(place_ref, sums, out):
        for i, total in sums():
            out[i] = total

    shape = pltpu.VMEM((SUB, streams[0].shape[1], 2 * HDIM), F32)
    return run_blocks(kernel, "begin", place, streams, parts, base, shape)


def keys_values(place, streams, parts, base, total):
    rows = streams[0].shape[1]

    def kernel(place_ref, sums, given_ref, key_ref, value_ref, state_ref, total_ref):
        for i, both in sums():
            key_ref[i] = silu(both[:, :HDIM]).astype(BF16)
            value_ref[i] = both[:, HDIM:].astype(BF16)
        added = jnp.zeros((HDIM, HDIM), F32)
        for i in range(SUB):
            state = dot(key_ref[i], value_ref[i], ((0,), (0,)))
            state_ref[i] = state
            added = added + state
        total_ref[0] = given_ref[...]
        total_ref[1] = added

    shape = jax.ShapeDtypeStruct((SUB, rows, HDIM), BF16)
    shapes = [shape, shape] + [jax.ShapeDtypeStruct((n, HDIM, HDIM), F32) for n in (SUB, 2)]
    return run_blocks(kernel, "keys_values", place, streams, parts, base, shapes, [total])


def queries(place, streams, parts, base):
    def kernel(place_ref, sums, out):
        swap = place_ref[1] == 1
        for i, total in sums():
            both = silu(total).astype(BF16)
            out[i, :, :HDIM] = jnp.where(swap, both[:, HDIM:], both[:, :HDIM])
            out[i, :, HDIM:] = jnp.where(swap, both[:, :HDIM], both[:, HDIM:])

    shape = jax.ShapeDtypeStruct((SUB, streams[0].shape[1], 2 * HDIM), BF16)
    return run_blocks(kernel, "queries", place, streams, parts, base, shape)


def attend(place, blocks, query, heads, carried):
    rows = query.shape[1]
    count = len(blocks)
    flat, where = [], []
    for parts in heads:
        index = []
        for part in parts:
            index += [(len(flat), r) for r in range(part[0].shape[0])]
            flat += part
        where.append(index)
    flat.append(carried)

    def kernel(place_ref, query_ref, *refs):
        ins, outs = refs[: len(flat)], refs[len(flat) :]
        causal = lax.broadcasted_iota(jnp.int32, (rows, rows), 1) <= lax.broadcasted_iota(
            jnp.int32, (rows, rows), 0
        )
        block = place_ref[0]
        for i, r in enumerate(blocks):
            for h, index in enumerate(where):
                earlier = ins[-1][h]
                for other in range(SUB):
                    if other != r:
                        is_before = jnp.bitwise_xor(block, other) < jnp.bitwise_xor(block, r)
                        slot, j = index[other]
                        earlier = earlier + jnp.where(is_before, ins[slot + 2][j], 0.0)
                slot, j = index[r]
                key, value = ins[slot][j], ins[slot + 1][j]
                q = query_ref[r, :, h * HDIM : (h + 1) * HDIM]
                scores = dot(q, key, ((1,), (1,)))
                weights = jnp.where(causal, scores, 0.0).astype(BF16)
                mixed = dot(weights, value) + dot(q, earlier.astype(BF16))
                scale = lax.rsqrt(jnp.mean(mixed * mixed, axis=-1, keepdims=True) + 1e-06)
                target = pl.multiple_of(jnp.bitwise_xor(place_ref[1], h) * HDIM, HDIM)
                outs[i][:, pl.ds(target, HDIM)] = (mixed * scale).astype(BF16)

    shapes = [jax.ShapeDtypeStruct((rows, 2 * HDIM), BF16)] * count
    flops = count * 4 * rows * HDIM * (2 * rows + HDIM)
    specs = [SMEM] + [VMEM] * (1 + len(flat))
    return call(kernel, "attend", shapes, specs, [VMEM] * count, LIMIT, flops, 2 * MIB)(place, query, *flat)


def add_features(pieces, weight, partial=None):
    rows, depth = pieces[0].shape
    width = weight.shape[2]
    count = len(pieces)
    tile = min(512, width)

    def kernel(*refs):
        w_ref, out = refs[count], refs[-1]
        for start in range(0, width, tile):
            columns = slice(start, start + tile)
            total = refs[count + 1][:, columns] if partial is not None else jnp.zeros((rows, tile), F32)
            for i in range(count):
                total = total + dot(refs[i][...], w_ref[i, :, columns])
            out[:, columns] = total.astype(out.dtype)

    shape = pltpu.VMEM((rows, width), F32) if partial is None else jax.ShapeDtypeStruct((rows, width), BF16)
    args = [*pieces, weight] + ([] if partial is None else [partial])
    flops = 2 * count * depth * rows * width
    return call(kernel, "add_features", shape, [VMEM] * len(args), VMEM, LIMIT, flops, 8 * MIB)(*args)


def exclusive_prefix(value, groups):
    def shift(v, step):
        pairs = [(g * SUB + j, (g + step) * SUB + j) for g in range(groups - step) for j in range(SUB)]
        return lax.ppermute(v, "ctx", pairs)

    if groups == 1:
        return jnp.zeros_like(value)
    total = shift(value, 1)
    step = 1
    while step < groups - 1:
        total = total + shift(total, step)
        step *= 2
    return total


def local(tokens, w_query, w_key, w_value, w_out):
    n_ctx = lax.axis_size("ctx")
    groups = n_ctx // SUB
    rows, half = tokens.shape
    ctx = lax.axis_index("ctx")
    place = jnp.stack([ctx % SUB, lax.axis_index("groups"), lax.axis_index("head"), ctx]).astype(jnp.int32)

    def xor(value, step):
        return lax.ppermute(value, "ctx", [(i, i ^ step) for i in range(n_ctx)])

    def other_part(value):
        return lax.ppermute(value, "groups", [(0, 1), (1, 0)])

    def other_core(value):
        return lax.ppermute(value, "head", [(0, 1), (1, 0)])

    def spread(packed):
        return lax.all_to_all(packed, "ctx", 0, 0, tiled=True)

    def gather_queries(sent):
        ordered = [lax.dynamic_index_in_dim(jnp.stack(sent), (ctx % SUB) ^ j, keepdims=False) for j in range(SUB)]
        return spread(jnp.concatenate(ordered * groups, axis=0))

    cut = half * 11 // 16 // HDIM * HDIM
    pieced = n_ctx == 2 * SUB
    ob = lax.optimization_barrier

    across = xor(tokens, 2)
    beside = xor(tokens, 1)
    kv_mine = spread(pack_keys_values(place, w_key, w_value, n_ctx))
    far_tokens = other_core(tokens)
    w_far = other_core(w_out)
    beside, far_tokens, w_far, w_query = ob((beside, far_tokens, w_far, w_query))
    q_sent = pack_queries(place, w_query)
    far_beside = other_core(beside)

    def fetch(sent, *steps):
        if pieced:
            arrived.update({m: xor(sent[m % SUB], m) for m in steps})

    arrived = {0: q_sent[0]}
    fetch(q_sent, 1)
    beside_cut = beside[:, cut:]
    across, kv_mine, beside, far_beside, q_sent, arrived, beside_cut = ob(
        (across, kv_mine, beside, far_beside, q_sent, arrived, beside_cut)
    )
    middle = kv_mine.shape[0] // 2
    kv_upper = other_part(kv_mine[:middle])
    left = xor(across[:, :cut], 1)
    right = xor(beside_cut, 2)
    fetch(q_sent, 4, 6)
    near = [(tokens, 0, 0, 0), (far_tokens, 0, 0, 1), (beside, 1, 0, 0), (far_beside, 1, 0, 1)]
    near += [(across, 2, 0, 0), (other_core(across), 2, 0, 1)]
    near = stage(place, near, SUB - 1, rows, 2 * half)
    first = project(near, kv_mine)
    left, right, arrived, kv_upper, kv_mine, q_sent, first = ob(
        (left, right, arrived, kv_upper, kv_mine, q_sent, first)
    )
    kv_lower = other_part(kv_mine[middle:])
    fetch(q_sent, 5, 7)
    far_left, far_right = other_core(left), other_core(right)
    far_left, q_sent = ob((far_left, q_sent))
    fetch(q_sent, 3, 2)
    corner = [(left, 0, 0, 0), (far_left, 0, 0, 1), (right, 0, cut, 0), (far_right, 0, cut, 1)]
    corner = stage(place, corner, 1, rows, 2 * half)

    streams = [near, corner]
    last = project(corner, kv_mine, first[3])
    kv_base = begin(place, streams, [(kv_upper, 0)])
    if pieced:
        early = (0, 1, 4, 6)
        q_base = begin(place, streams, [(arrived[m], (m,)) for m in early])
        latest = {m: arrived.pop(m) for m in (3, 7)}
        q_base = begin(place, streams, [(arrived[m], (m,)) for m in sorted(arrived) if m not in early], q_base)
        arrived, kv_lower, kv_base, q_base = ob((arrived, kv_lower, kv_base, q_base))
        q_parts = [(piece, (m,)) for m, piece in latest.items()]
    else:
        q_base, q_parts = None, [(gather_queries(q_sent), 0)]
    *second, totals = keys_values(place, streams, [(kv_lower, middle)], kv_base, last[3])
    carried = exclusive_prefix(totals, groups)
    heads = [[first[:3], last[:3]], [second]]
    query = queries(place, streams, q_parts, q_base)
    normed = [attend(place, (r,), query, heads, carried)[0] for r in (3, 1, 2, 0)]
    normed = [normed[3], xor(normed[1], 1), xor(normed[2], 2), xor(normed[0], 3)]
    home_0, w_far = lax.optimization_barrier((normed[0], w_far))
    out_keep, out_far = stage_rows(place, w_out, w_far)
    out_keep, out_far, *normed = lax.optimization_barrier((out_keep, out_far, home_0, *normed[1:]))
    partial = add_features(normed, out_keep)
    return add_features([other_core(n) for n in normed], out_far, partial)


def solution(mesh):
    in_specs = (
        P(("groups", "ctx"), "head"),
        P("ctx", "head"),
        P("ctx", "head"),
        P("ctx", "head"),
        P("head", None),
    )
    out_specs = P(("groups", "ctx"), "head")
    return jax.shard_map(local, mesh=mesh, in_specs=in_specs, out_specs=out_specs, check_vma=False)
```

```python
import jax
import jax.numpy as jnp
from jax import lax
from jax.experimental import pallas as pl
from jax.experimental.pallas import tpu as pltpu
from jax.sharding import PartitionSpec as P

HDIM = 128
SUB = 4
F32 = jnp.float32
BF16 = jnp.bfloat16
MIB = 1 << 20
LIMIT = 8
ANY = pl.BlockSpec(memory_space=pl.ANY)
VMEM = pl.BlockSpec(memory_space=pltpu.VMEM)
SMEM = pl.BlockSpec(memory_space=pltpu.SMEM)


def dot(a, b, contract=((1,), (0,))):
    return lax.dot_general(a, b, (contract, ((), ())), preferred_element_type=F32)


def silu(u):
    return u / (1.0 + jnp.exp(-u))


def call(kernel, name, out_shape, in_specs, out_specs, limit, flops, moved, scratch=()):
    return pl.pallas_call(
        kernel,
        out_shape=out_shape,
        in_specs=in_specs,
        out_specs=out_specs,
        scratch_shapes=list(scratch),
        compiler_params=pltpu.CompilerParams(vmem_limit_bytes=limit * MIB),
        cost_estimate=pl.CostEstimate(flops=int(flops), bytes_accessed=int(moved), transcendentals=0),
        name=name,
    )


def pack_keys_values(place, w_key, w_value, count):
    depth = w_key.shape[0]

    def kernel(place_ref, key_ref, value_ref, out):
        for j in range(SUB):
            start = pl.multiple_of((2 * j + place_ref[1]) * HDIM, HDIM)
            key = key_ref[:, pl.ds(start, HDIM)]
            value = value_ref[:, pl.ds(start, HDIM)]
            for i in range(j, count, SUB):
                out[i * depth : (i + 1) * depth, :HDIM] = key
                out[i * depth : (i + 1) * depth, HDIM:] = value

    shape = jax.ShapeDtypeStruct((count * depth, 2 * HDIM), BF16)
    moved = count * depth * 2 * HDIM * 4
    return call(kernel, "pack_keys_values", shape, [SMEM, VMEM, VMEM], VMEM, LIMIT, 0, moved)(place, w_key, w_value)


def pack_queries(place, w_query):
    depth = w_query.shape[0]

    def kernel(place_ref, query_ref, *outs):
        for r, out in enumerate(outs):
            start = pl.multiple_of(jnp.bitwise_xor(place_ref[0], r) * 2 * HDIM, 2 * HDIM)
            out[...] = query_ref[:, pl.ds(start, 2 * HDIM)]

    shapes = [jax.ShapeDtypeStruct((depth, 2 * HDIM), BF16)] * SUB
    moved = SUB * depth * 2 * HDIM * 4
    return call(kernel, "pack_queries", shapes, [SMEM, VMEM], [VMEM] * SUB, LIMIT, 0, moved)(place, w_query)


def stage_rows(place, w_out, w_far):
    rows, width = w_out.shape
    depth, half = rows // SUB, width // 2

    def kernel(place_ref, out_ref, far_ref, keep, far, sems):
        column = pl.multiple_of(place_ref[2] * half, half)
        copies = []
        for r in range(SUB):
            row = pl.multiple_of(jnp.bitwise_xor(place_ref[0], r) * depth, depth)
            for i, (source, target) in enumerate(((out_ref, keep), (far_ref, far))):
                block = source.at[pl.ds(row, depth), pl.ds(column, half)]
                copies.append(pltpu.make_async_copy(block, target.at[r], sems.at[2 * r + i]))
        for copy in copies:
            copy.start()
        for copy in copies:
            copy.wait()

    shapes = [pltpu.VMEM((SUB, depth, half), BF16)] * 2
    sems = pltpu.SemaphoreType.DMA((2 * SUB,))
    return call(kernel, "stage_rows", shapes, [SMEM, ANY, ANY], [VMEM] * 2, 40, 0, rows * width * 4, [sems])(
        place, w_out, w_far
    )


def stage(place, pieces, blocks, rows, width):
    count = len(pieces)
    half = width // 2

    def kernel(place_ref, *refs):
        out, sems = refs[count], refs[count + 1]
        copies = []
        for i, ((array, r, column, far), ref) in enumerate(zip(pieces, refs)):
            if far is None:
                target = out.at[r]
            else:
                core = 1 - place_ref[2] if far else place_ref[2]
                start = pl.multiple_of(core * half + column, HDIM)
                target = out.at[r, :, pl.ds(start, array.shape[1])]
            copies.append(pltpu.make_async_copy(ref, target, sems.at[i]))
        for copy in copies:
            copy.start()
        for copy in copies:
            copy.wait()

    shape = pltpu.VMEM((blocks, rows, width), BF16)
    sems = pltpu.SemaphoreType.DMA((count,))
    moved = blocks * rows * width * 4
    return call(kernel, "stage", shape, [SMEM] + [ANY] * count, VMEM, 20 if blocks > 1 else LIMIT, 0, moved, [sems])(
        place, *[piece[0] for piece in pieces]
    )


def project(stream, kv, total=None):
    blocks, rows, width = stream.shape
    kv = kv if isinstance(kv, list) else [kv]
    cuts = [sum(w.shape[0] for w in kv[:i]) for i in range(len(kv) + 1)]

    def kernel(stream_ref, *refs):
        key_ref, value_ref, state_ref, total_ref = refs[-4:]
        for r in range(blocks):
            both = sum(dot(stream_ref[r, :, cuts[i] : cuts[i + 1]], refs[i][...]) for i in range(len(kv)))
            key_ref[r] = silu(both[:, :HDIM]).astype(BF16)
            value_ref[r] = both[:, HDIM:].astype(BF16)
        added = jnp.zeros((HDIM, HDIM), F32) if total is None else refs[len(kv)][...]
        for r in range(blocks):
            state = dot(key_ref[r], value_ref[r], ((0,), (0,)))
            state_ref[r] = state
            added = added + state
        total_ref[...] = added

    shape = jax.ShapeDtypeStruct((blocks, rows, HDIM), BF16)
    state = jax.ShapeDtypeStruct((blocks, HDIM, HDIM), F32)
    shapes = [shape, shape, state, jax.ShapeDtypeStruct((HDIM, HDIM), F32)]
    args = [stream, *kv] + ([] if total is None else [total])
    flops = 4 * blocks * rows * width * HDIM
    return call(kernel, "project", shapes, [VMEM] * len(args), [VMEM] * 4, LIMIT, flops, 2 * MIB)(*args)


def flat_blocks(streams):
    return [(stream, r) for stream in streams for r in range(stream.shape[0])]


def weighted(place_ref, source, r, refs, parts, base):
    total = base
    for ref, (weight, start) in zip(refs, parts):
        depth = weight.shape[0]
        if isinstance(start, tuple):
            lanes = pl.ds(pl.multiple_of(jnp.bitwise_xor(place_ref[3], start[0]) * depth, HDIM), depth)
        else:
            lanes = slice(start, start + depth)
        term = dot(source[r, :, lanes], ref[...])
        total = term if total is None else total + term
    return total


def run_blocks(kernel, name, place, streams, parts, base, out_shape, more=()):
    rows, width = streams[0].shape[1:]
    count = len(streams)
    args = [*streams, *[weight for weight, _ in parts], *([] if base is None else [base])]
    given = len(args)
    args += more

    def body(place_ref, *refs):
        weights = refs[count : count + len(parts)]
        base_ref = None if base is None else refs[given - 1]

        def sums():
            for i, (source, r) in enumerate(flat_blocks(refs[:count])):
                yield i, weighted(place_ref, source, r, weights, parts, None if base is None else base_ref[i])

        kernel(place_ref, sums, *refs[given:])

    flops = 4 * SUB * rows * sum(weight.shape[0] for weight, _ in parts) * HDIM
    specs = [SMEM] + [VMEM] * len(args)
    outs = [VMEM] * len(out_shape) if isinstance(out_shape, list) else VMEM
    return call(body, name, out_shape, specs, outs, LIMIT, flops, 2 * MIB)(place, *args)


def begin(place, streams, parts, base=None):
    def kernel(place_ref, sums, out):
        for i, total in sums():
            out[i] = total

    shape = pltpu.VMEM((SUB, streams[0].shape[1], 2 * HDIM), F32)
    return run_blocks(kernel, "begin", place, streams, parts, base, shape)


def keys_values(place, streams, parts, base, total):
    rows = streams[0].shape[1]

    def kernel(place_ref, sums, given_ref, key_ref, value_ref, state_ref, total_ref):
        for i, both in sums():
            key_ref[i] = silu(both[:, :HDIM]).astype(BF16)
            value_ref[i] = both[:, HDIM:].astype(BF16)
        added = jnp.zeros((HDIM, HDIM), F32)
        for i in range(SUB):
            state = dot(key_ref[i], value_ref[i], ((0,), (0,)))
            state_ref[i] = state
            added = added + state
        total_ref[0] = given_ref[...]
        total_ref[1] = added

    shape = jax.ShapeDtypeStruct((SUB, rows, HDIM), BF16)
    shapes = [shape, shape] + [jax.ShapeDtypeStruct((n, HDIM, HDIM), F32) for n in (SUB, 2)]
    return run_blocks(kernel, "keys_values", place, streams, parts, base, shapes, [total])


def queries(place, streams, parts, base):
    def kernel(place_ref, sums, out):
        swap = place_ref[1] == 1
        for i, total in sums():
            both = silu(total).astype(BF16)
            out[i, :, :HDIM] = jnp.where(swap, both[:, HDIM:], both[:, :HDIM])
            out[i, :, HDIM:] = jnp.where(swap, both[:, :HDIM], both[:, HDIM:])

    shape = jax.ShapeDtypeStruct((SUB, streams[0].shape[1], 2 * HDIM), BF16)
    return run_blocks(kernel, "queries", place, streams, parts, base, shape)


def attend(place, blocks, query, heads, carried):
    rows = query.shape[1]
    count = len(blocks)
    flat, where = [], []
    for parts in heads:
        index = []
        for part in parts:
            index += [(len(flat), r) for r in range(part[0].shape[0])]
            flat += part
        where.append(index)
    flat.append(carried)

    def kernel(place_ref, query_ref, *refs):
        ins, outs = refs[: len(flat)], refs[len(flat) :]
        causal = lax.broadcasted_iota(jnp.int32, (rows, rows), 1) <= lax.broadcasted_iota(
            jnp.int32, (rows, rows), 0
        )
        block = place_ref[0]
        for i, r in enumerate(blocks):
            for h, index in enumerate(where):
                earlier = ins[-1][h]
                for other in range(SUB):
                    if other != r:
                        is_before = jnp.bitwise_xor(block, other) < jnp.bitwise_xor(block, r)
                        slot, j = index[other]
                        earlier = earlier + jnp.where(is_before, ins[slot + 2][j], 0.0)
                slot, j = index[r]
                key, value = ins[slot][j], ins[slot + 1][j]
                q = query_ref[r, :, h * HDIM : (h + 1) * HDIM]
                scores = dot(q, key, ((1,), (1,)))
                weights = jnp.where(causal, scores, 0.0).astype(BF16)
                mixed = dot(weights, value) + dot(q, earlier.astype(BF16))
                scale = lax.rsqrt(jnp.mean(mixed * mixed, axis=-1, keepdims=True) + 1e-06)
                target = pl.multiple_of(jnp.bitwise_xor(place_ref[1], h) * HDIM, HDIM)
                outs[i][:, pl.ds(target, HDIM)] = (mixed * scale).astype(BF16)

    shapes = [jax.ShapeDtypeStruct((rows, 2 * HDIM), BF16)] * count
    flops = count * 4 * rows * HDIM * (2 * rows + HDIM)
    specs = [SMEM] + [VMEM] * (1 + len(flat))
    return call(kernel, "attend", shapes, specs, [VMEM] * count, LIMIT, flops, 2 * MIB)(place, query, *flat)


def add_features(pieces, weight, partial=None):
    rows, depth = pieces[0].shape
    width = weight.shape[2]
    count = len(pieces)
    tile = min(512, width)

    def kernel(*refs):
        w_ref, out = refs[count], refs[-1]
        for start in range(0, width, tile):
            columns = slice(start, start + tile)
            total = refs[count + 1][:, columns] if partial is not None else jnp.zeros((rows, tile), F32)
            for i in range(count):
                total = total + dot(refs[i][...], w_ref[i, :, columns])
            out[:, columns] = total.astype(out.dtype)

    shape = pltpu.VMEM((rows, width), F32) if partial is None else jax.ShapeDtypeStruct((rows, width), BF16)
    args = [*pieces, weight] + ([] if partial is None else [partial])
    flops = 2 * count * depth * rows * width
    return call(kernel, "add_features", shape, [VMEM] * len(args), VMEM, LIMIT, flops, 8 * MIB)(*args)


def exclusive_prefix(value, groups):
    def shift(v, step):
        pairs = [(g * SUB + j, (g + step) * SUB + j) for g in range(groups - step) for j in range(SUB)]
        return lax.ppermute(v, "ctx", pairs)

    if groups == 1:
        return jnp.zeros_like(value)
    total = shift(value, 1)
    step = 1
    while step < groups - 1:
        total = total + shift(total, step)
        step *= 2
    return total


def local(tokens, w_query, w_key, w_value, w_out):
    n_ctx = lax.axis_size("ctx")
    groups = n_ctx // SUB
    rows, half = tokens.shape
    ctx = lax.axis_index("ctx")
    place = jnp.stack([ctx % SUB, lax.axis_index("groups"), lax.axis_index("head"), ctx]).astype(jnp.int32)

    def xor(value, step):
        return lax.ppermute(value, "ctx", [(i, i ^ step) for i in range(n_ctx)])

    def other_part(value):
        return lax.ppermute(value, "groups", [(0, 1), (1, 0)])

    def other_core(value):
        return lax.ppermute(value, "head", [(0, 1), (1, 0)])

    def spread(packed):
        return lax.all_to_all(packed, "ctx", 0, 0, tiled=True)

    def gather_queries(sent):
        ordered = [lax.dynamic_index_in_dim(jnp.stack(sent), (ctx % SUB) ^ j, keepdims=False) for j in range(SUB)]
        return spread(jnp.concatenate(ordered * groups, axis=0))

    cut = half * 11 // 16 // HDIM * HDIM
    pieced = n_ctx == 2 * SUB
    ob = lax.optimization_barrier

    across = xor(tokens, 2)
    beside = xor(tokens, 1)
    kv_mine = spread(pack_keys_values(place, w_key, w_value, n_ctx))
    far_tokens = other_core(tokens)
    w_far = other_core(w_out)
    beside, far_tokens, w_far, w_query = ob((beside, far_tokens, w_far, w_query))
    q_sent = pack_queries(place, w_query)
    far_beside = other_core(beside)

    def fetch(sent, *steps):
        if pieced:
            arrived.update({m: xor(sent[m % SUB], m) for m in steps})

    arrived = {0: q_sent[0]}
    fetch(q_sent, 1)
    beside_cut = beside[:, cut:]
    across, kv_mine, beside, far_beside, q_sent, arrived, beside_cut = ob(
        (across, kv_mine, beside, far_beside, q_sent, arrived, beside_cut)
    )
    middle = kv_mine.shape[0] // 2
    kv_upper = other_part(kv_mine[:middle])
    left = xor(across[:, :cut], 1)
    right = xor(beside_cut, 2)
    fetch(q_sent, 4, 6)
    near = [(tokens, 0, 0, 0), (far_tokens, 0, 0, 1), (beside, 1, 0, 0), (far_beside, 1, 0, 1)]
    near += [(across, 2, 0, 0), (other_core(across), 2, 0, 1)]
    near = stage(place, near, SUB - 1, rows, 2 * half)
    first = project(near, kv_mine)
    left, right, arrived, kv_upper, kv_mine, q_sent, first = ob(
        (left, right, arrived, kv_upper, kv_mine, q_sent, first)
    )
    kv_lower = other_part(kv_mine[middle:])
    fetch(q_sent, 5, 7)
    far_left, far_right = other_core(left), other_core(right)
    far_left, q_sent = ob((far_left, q_sent))
    fetch(q_sent, 3, 2)
    corner = [(left, 0, 0, 0), (far_left, 0, 0, 1), (right, 0, cut, 0), (far_right, 0, cut, 1)]
    corner = stage(place, corner, 1, rows, 2 * half)

    streams = [near, corner]
    last = project(corner, kv_mine, first[3])
    kv_base = begin(place, streams, [(kv_upper, 0)])
    if pieced:
        early = (0, 1, 4, 6)
        q_base = begin(place, streams, [(arrived[m], (m,)) for m in early])
        latest = {m: arrived.pop(m) for m in (3, 7)}
        arrived, kv_lower, kv_base, q_base = ob((arrived, kv_lower, kv_base, q_base))
        q_base = begin(place, streams, [(arrived[m], (m,)) for m in sorted(arrived) if m not in early], q_base)
        q_parts = [(piece, (m,)) for m, piece in latest.items()]
    else:
        q_base, q_parts = None, [(gather_queries(q_sent), 0)]
    *second, totals = keys_values(place, streams, [(kv_lower, middle)], kv_base, last[3])
    carried = exclusive_prefix(totals, groups)
    heads = [[first[:3], last[:3]], [second]]
    query = queries(place, streams, q_parts, q_base)
    normed = [n for blocks in ((3,), (1, 2), (0,)) for n in attend(place, blocks, query, heads, carried)]
    normed = [normed[3], xor(normed[1], 1), xor(normed[2], 2), xor(normed[0], 3)]
    home_0, w_far = lax.optimization_barrier((normed[0], w_far))
    out_keep, out_far = stage_rows(place, w_out, w_far)
    out_keep, out_far, *normed = lax.optimization_barrier((out_keep, out_far, home_0, *normed[1:]))
    partial = add_features(normed, out_keep)
    return add_features([other_core(n) for n in normed], out_far, partial)


def solution(mesh):
    in_specs = (
        P(("groups", "ctx"), "head"),
        P("ctx", "head"),
        P("ctx", "head"),
        P("ctx", "head"),
        P("head", None),
    )
    out_specs = P(("groups", "ctx"), "head")
    return jax.shard_map(local, mesh=mesh, in_specs=in_specs, out_specs=out_specs, check_vma=False)
```

```python
import jax
import jax.numpy as jnp
from jax import lax
from jax.experimental import pallas as pl
from jax.experimental.pallas import tpu as pltpu
from jax.sharding import PartitionSpec as P

HDIM = 128
SUB = 4
F32 = jnp.float32
BF16 = jnp.bfloat16
MIB = 1 << 20
LIMIT = 8
ANY = pl.BlockSpec(memory_space=pl.ANY)
VMEM = pl.BlockSpec(memory_space=pltpu.VMEM)
SMEM = pl.BlockSpec(memory_space=pltpu.SMEM)


def dot(a, b, contract=((1,), (0,))):
    return lax.dot_general(a, b, (contract, ((), ())), preferred_element_type=F32)


def silu(u):
    return u / (1.0 + jnp.exp(-u))


def call(kernel, name, out_shape, in_specs, out_specs, limit, flops, moved, scratch=()):
    return pl.pallas_call(
        kernel,
        out_shape=out_shape,
        in_specs=in_specs,
        out_specs=out_specs,
        scratch_shapes=list(scratch),
        compiler_params=pltpu.CompilerParams(vmem_limit_bytes=limit * MIB),
        cost_estimate=pl.CostEstimate(flops=int(flops), bytes_accessed=int(moved), transcendentals=0),
        name=name,
    )


def pack_keys_values(place, w_key, w_value, count):
    depth = w_key.shape[0]

    def kernel(place_ref, key_ref, value_ref, out):
        for j in range(SUB):
            start = pl.multiple_of((2 * j + place_ref[1]) * HDIM, HDIM)
            key = key_ref[:, pl.ds(start, HDIM)]
            value = value_ref[:, pl.ds(start, HDIM)]
            for i in range(j, count, SUB):
                out[i * depth : (i + 1) * depth, :HDIM] = key
                out[i * depth : (i + 1) * depth, HDIM:] = value

    shape = jax.ShapeDtypeStruct((count * depth, 2 * HDIM), BF16)
    moved = count * depth * 2 * HDIM * 4
    return call(kernel, "pack_keys_values", shape, [SMEM, VMEM, VMEM], VMEM, LIMIT, 0, moved)(place, w_key, w_value)


def pack_queries(place, w_query):
    depth = w_query.shape[0]

    def kernel(place_ref, query_ref, *outs):
        for r, out in enumerate(outs):
            start = pl.multiple_of(jnp.bitwise_xor(place_ref[0], r) * 2 * HDIM, 2 * HDIM)
            out[...] = query_ref[:, pl.ds(start, 2 * HDIM)]

    shapes = [jax.ShapeDtypeStruct((depth, 2 * HDIM), BF16)] * SUB
    moved = SUB * depth * 2 * HDIM * 4
    return call(kernel, "pack_queries", shapes, [SMEM, VMEM], [VMEM] * SUB, LIMIT, 0, moved)(place, w_query)


def stage_rows(place, w_out, w_far):
    rows, width = w_out.shape
    depth, half = rows // SUB, width // 2

    def kernel(place_ref, out_ref, far_ref, keep, far, sems):
        column = pl.multiple_of(place_ref[2] * half, half)
        copies = []
        for r in range(SUB):
            row = pl.multiple_of(jnp.bitwise_xor(place_ref[0], r) * depth, depth)
            for i, (source, target) in enumerate(((out_ref, keep), (far_ref, far))):
                block = source.at[pl.ds(row, depth), pl.ds(column, half)]
                copies.append(pltpu.make_async_copy(block, target.at[r], sems.at[2 * r + i]))
        for copy in copies:
            copy.start()
        for copy in copies:
            copy.wait()

    shapes = [pltpu.VMEM((SUB, depth, half), BF16)] * 2
    sems = pltpu.SemaphoreType.DMA((2 * SUB,))
    return call(kernel, "stage_rows", shapes, [SMEM, ANY, ANY], [VMEM] * 2, 28, 0, rows * width * 4, [sems])(
        place, w_out, w_far
    )


def stage(place, pieces, blocks, rows, width):
    count = len(pieces)
    half = width // 2

    def kernel(place_ref, *refs):
        out, sems = refs[count], refs[count + 1]
        copies = []
        for i, ((array, r, column, far), ref) in enumerate(zip(pieces, refs)):
            if far is None:
                target = out.at[r]
            else:
                core = 1 - place_ref[2] if far else place_ref[2]
                start = pl.multiple_of(core * half + column, HDIM)
                target = out.at[r, :, pl.ds(start, array.shape[1])]
            copies.append(pltpu.make_async_copy(ref, target, sems.at[i]))
        for copy in copies:
            copy.start()
        for copy in copies:
            copy.wait()

    shape = pltpu.VMEM((blocks, rows, width), BF16)
    sems = pltpu.SemaphoreType.DMA((count,))
    moved = blocks * rows * width * 4
    return call(kernel, "stage", shape, [SMEM] + [ANY] * count, VMEM, 20 if blocks > 1 else LIMIT, 0, moved, [sems])(
        place, *[piece[0] for piece in pieces]
    )


def project(stream, kv, total=None):
    blocks, rows, width = stream.shape
    kv = kv if isinstance(kv, list) else [kv]
    cuts = [sum(w.shape[0] for w in kv[:i]) for i in range(len(kv) + 1)]

    def kernel(stream_ref, *refs):
        key_ref, value_ref, state_ref, total_ref = refs[-4:]
        for r in range(blocks):
            both = sum(dot(stream_ref[r, :, cuts[i] : cuts[i + 1]], refs[i][...]) for i in range(len(kv)))
            key_ref[r] = silu(both[:, :HDIM]).astype(BF16)
            value_ref[r] = both[:, HDIM:].astype(BF16)
        added = jnp.zeros((HDIM, HDIM), F32) if total is None else refs[len(kv)][...]
        for r in range(blocks):
            state = dot(key_ref[r], value_ref[r], ((0,), (0,)))
            state_ref[r] = state
            added = added + state
        total_ref[...] = added

    shape = jax.ShapeDtypeStruct((blocks, rows, HDIM), BF16)
    state = jax.ShapeDtypeStruct((blocks, HDIM, HDIM), F32)
    shapes = [shape, shape, state, jax.ShapeDtypeStruct((HDIM, HDIM), F32)]
    args = [stream, *kv] + ([] if total is None else [total])
    flops = 4 * blocks * rows * width * HDIM
    return call(kernel, "project", shapes, [VMEM] * len(args), [VMEM] * 4, LIMIT, flops, 2 * MIB)(*args)


def flat_blocks(streams):
    return [(stream, r) for stream in streams for r in range(stream.shape[0])]


def weighted(place_ref, source, r, refs, parts, base):
    total = base
    for ref, (weight, start) in zip(refs, parts):
        depth = weight.shape[0]
        if isinstance(start, tuple):
            lanes = pl.ds(pl.multiple_of(jnp.bitwise_xor(place_ref[3], start[0]) * depth, HDIM), depth)
        else:
            lanes = slice(start, start + depth)
        term = dot(source[r, :, lanes], ref[...])
        total = term if total is None else total + term
    return total


def run_blocks(kernel, name, place, streams, parts, base, out_shape, more=()):
    rows, width = streams[0].shape[1:]
    count = len(streams)
    args = [*streams, *[weight for weight, _ in parts], *([] if base is None else [base])]
    given = len(args)
    args += more

    def body(place_ref, *refs):
        weights = refs[count : count + len(parts)]
        base_ref = None if base is None else refs[given - 1]

        def sums():
            for i, (source, r) in enumerate(flat_blocks(refs[:count])):
                yield i, weighted(place_ref, source, r, weights, parts, None if base is None else base_ref[i])

        kernel(place_ref, sums, *refs[given:])

    flops = 4 * SUB * rows * sum(weight.shape[0] for weight, _ in parts) * HDIM
    specs = [SMEM] + [VMEM] * len(args)
    outs = [VMEM] * len(out_shape) if isinstance(out_shape, list) else VMEM
    return call(body, name, out_shape, specs, outs, LIMIT, flops, 2 * MIB)(place, *args)


def begin(place, streams, parts, base=None):
    def kernel(place_ref, sums, out):
        for i, total in sums():
            out[i] = total

    shape = pltpu.VMEM((SUB, streams[0].shape[1], 2 * HDIM), F32)
    return run_blocks(kernel, "begin", place, streams, parts, base, shape)


def keys_values(place, streams, parts, base, total):
    rows = streams[0].shape[1]

    def kernel(place_ref, sums, given_ref, key_ref, value_ref, state_ref, total_ref):
        for i, both in sums():
            key_ref[i] = silu(both[:, :HDIM]).astype(BF16)
            value_ref[i] = both[:, HDIM:].astype(BF16)
        added = jnp.zeros((HDIM, HDIM), F32)
        for i in range(SUB):
            state = dot(key_ref[i], value_ref[i], ((0,), (0,)))
            state_ref[i] = state
            added = added + state
        total_ref[0] = given_ref[...]
        total_ref[1] = added

    shape = jax.ShapeDtypeStruct((SUB, rows, HDIM), BF16)
    shapes = [shape, shape] + [jax.ShapeDtypeStruct((n, HDIM, HDIM), F32) for n in (SUB, 2)]
    return run_blocks(kernel, "keys_values", place, streams, parts, base, shapes, [total])


def queries(place, streams, parts, base):
    def kernel(place_ref, sums, out):
        swap = place_ref[1] == 1
        for i, total in sums():
            both = silu(total).astype(BF16)
            out[i, :, :HDIM] = jnp.where(swap, both[:, HDIM:], both[:, :HDIM])
            out[i, :, HDIM:] = jnp.where(swap, both[:, :HDIM], both[:, HDIM:])

    shape = jax.ShapeDtypeStruct((SUB, streams[0].shape[1], 2 * HDIM), BF16)
    return run_blocks(kernel, "queries", place, streams, parts, base, shape)


def attend(place, blocks, query, heads, carried):
    rows = query.shape[1]
    count = len(blocks)
    flat, where = [], []
    for parts in heads:
        index = []
        for part in parts:
            index += [(len(flat), r) for r in range(part[0].shape[0])]
            flat += part
        where.append(index)
    flat.append(carried)

    def kernel(place_ref, query_ref, *refs):
        ins, outs = refs[: len(flat)], refs[len(flat) :]
        causal = lax.broadcasted_iota(jnp.int32, (rows, rows), 1) <= lax.broadcasted_iota(
            jnp.int32, (rows, rows), 0
        )
        block = place_ref[0]
        for i, r in enumerate(blocks):
            for h, index in enumerate(where):
                earlier = ins[-1][h]
                for other in range(SUB):
                    if other != r:
                        is_before = jnp.bitwise_xor(block, other) < jnp.bitwise_xor(block, r)
                        slot, j = index[other]
                        earlier = earlier + jnp.where(is_before, ins[slot + 2][j], 0.0)
                slot, j = index[r]
                key, value = ins[slot][j], ins[slot + 1][j]
                q = query_ref[r, :, h * HDIM : (h + 1) * HDIM]
                scores = dot(q, key, ((1,), (1,)))
                weights = jnp.where(causal, scores, 0.0).astype(BF16)
                mixed = dot(weights, value) + dot(q, earlier.astype(BF16))
                scale = lax.rsqrt(jnp.mean(mixed * mixed, axis=-1, keepdims=True) + 1e-06)
                target = pl.multiple_of(jnp.bitwise_xor(place_ref[1], h) * HDIM, HDIM)
                outs[i][:, pl.ds(target, HDIM)] = (mixed * scale).astype(BF16)

    shapes = [jax.ShapeDtypeStruct((rows, 2 * HDIM), BF16)] * count
    flops = count * 4 * rows * HDIM * (2 * rows + HDIM)
    specs = [SMEM] + [VMEM] * (1 + len(flat))
    return call(kernel, "attend", shapes, specs, [VMEM] * count, LIMIT, flops, 2 * MIB)(place, query, *flat)


def add_features(pieces, weight, partial=None):
    rows, depth = pieces[0].shape
    width = weight.shape[2]
    count = len(pieces)
    tile = min(512, width)

    def kernel(*refs):
        w_ref, out = refs[count], refs[-1]
        for start in range(0, width, tile):
            columns = slice(start, start + tile)
            total = refs[count + 1][:, columns] if partial is not None else jnp.zeros((rows, tile), F32)
            for i in range(count):
                total = total + dot(refs[i][...], w_ref[i, :, columns])
            out[:, columns] = total.astype(out.dtype)

    shape = pltpu.VMEM((rows, width), F32) if partial is None else jax.ShapeDtypeStruct((rows, width), BF16)
    args = [*pieces, weight] + ([] if partial is None else [partial])
    flops = 2 * count * depth * rows * width
    return call(kernel, "add_features", shape, [VMEM] * len(args), VMEM, LIMIT, flops, 8 * MIB)(*args)


def exclusive_prefix(value, groups):
    def shift(v, step):
        pairs = [(g * SUB + j, (g + step) * SUB + j) for g in range(groups - step) for j in range(SUB)]
        return lax.ppermute(v, "ctx", pairs)

    if groups == 1:
        return jnp.zeros_like(value)
    total = shift(value, 1)
    step = 1
    while step < groups - 1:
        total = total + shift(total, step)
        step *= 2
    return total


def local(tokens, w_query, w_key, w_value, w_out):
    n_ctx = lax.axis_size("ctx")
    groups = n_ctx // SUB
    rows, half = tokens.shape
    ctx = lax.axis_index("ctx")
    place = jnp.stack([ctx % SUB, lax.axis_index("groups"), lax.axis_index("head"), ctx]).astype(jnp.int32)

    def xor(value, step):
        return lax.ppermute(value, "ctx", [(i, i ^ step) for i in range(n_ctx)])

    def other_part(value):
        return lax.ppermute(value, "groups", [(0, 1), (1, 0)])

    def other_core(value):
        return lax.ppermute(value, "head", [(0, 1), (1, 0)])

    def spread(packed):
        return lax.all_to_all(packed, "ctx", 0, 0, tiled=True)

    def gather_queries(sent):
        ordered = [lax.dynamic_index_in_dim(jnp.stack(sent), (ctx % SUB) ^ j, keepdims=False) for j in range(SUB)]
        return spread(jnp.concatenate(ordered * groups, axis=0))

    cut = half * 11 // 16 // HDIM * HDIM
    pieced = n_ctx == 2 * SUB
    ob = lax.optimization_barrier

    across = xor(tokens, 2)
    beside = xor(tokens, 1)
    kv_mine = spread(pack_keys_values(place, w_key, w_value, n_ctx))
    far_tokens = other_core(tokens)
    w_far = other_core(w_out)
    beside, far_tokens, w_far, w_query = ob((beside, far_tokens, w_far, w_query))
    q_sent = pack_queries(place, w_query)
    far_beside = other_core(beside)

    def fetch(sent, *steps):
        if pieced:
            arrived.update({m: xor(sent[m % SUB], m) for m in steps})

    arrived = {0: q_sent[0]}
    fetch(q_sent, 1)
    beside_cut = beside[:, cut:]
    across, kv_mine, beside, far_beside, q_sent, arrived, beside_cut = ob(
        (across, kv_mine, beside, far_beside, q_sent, arrived, beside_cut)
    )
    middle = kv_mine.shape[0] // 2
    kv_upper = other_part(kv_mine[:middle])
    left = xor(across[:, :cut], 1)
    right = xor(beside_cut, 2)
    fetch(q_sent, 4, 6)
    near = [(tokens, 0, 0, 0), (far_tokens, 0, 0, 1), (beside, 1, 0, 0), (far_beside, 1, 0, 1)]
    near += [(across, 2, 0, 0), (other_core(across), 2, 0, 1)]
    near = stage(place, near, SUB - 1, rows, 2 * half)
    first = project(near, kv_mine)
    left, right, arrived, kv_upper, kv_mine, q_sent, first = ob(
        (left, right, arrived, kv_upper, kv_mine, q_sent, first)
    )
    kv_lower = other_part(kv_mine[middle:])
    fetch(q_sent, 5, 7)
    far_left, far_right = other_core(left), other_core(right)
    far_left, q_sent = ob((far_left, q_sent))
    fetch(q_sent, 3, 2)
    corner = [(left, 0, 0, 0), (far_left, 0, 0, 1), (right, 0, cut, 0), (far_right, 0, cut, 1)]
    corner = stage(place, corner, 1, rows, 2 * half)

    streams = [near, corner]
    last = project(corner, kv_mine, first[3])
    last, w_far = ob((last, w_far))
    w_rows = stage_rows(place, w_out, w_far)
    kv_base = begin(place, streams, [(kv_upper, 0)])
    if pieced:
        early = (0, 1, 4, 6)
        q_base = begin(place, streams, [(arrived[m], (m,)) for m in early])
        latest = {m: arrived.pop(m) for m in (3, 7)}
        arrived, kv_lower, kv_base, q_base, w_rows = ob((arrived, kv_lower, kv_base, q_base, w_rows))
        q_base = begin(place, streams, [(arrived[m], (m,)) for m in sorted(arrived) if m not in early], q_base)
        q_parts = [(piece, (m,)) for m, piece in latest.items()]
    else:
        q_base, q_parts = None, [(gather_queries(q_sent), 0)]
    *second, totals = keys_values(place, streams, [(kv_lower, middle)], kv_base, last[3])
    carried = exclusive_prefix(totals, groups)
    heads = [[first[:3], last[:3]], [second]]
    query = queries(place, streams, q_parts, q_base)
    normed = [n for blocks in ((3,), (1, 2), (0,)) for n in attend(place, blocks, query, heads, carried)]
    normed = [normed[3], xor(normed[1], 1), xor(normed[2], 2), xor(normed[0], 3)]
    out_keep, out_far = w_rows
    partial = add_features(normed, out_keep)
    return add_features([other_core(n) for n in normed], out_far, partial)


def solution(mesh):
    in_specs = (
        P(("groups", "ctx"), "head"),
        P("ctx", "head"),
        P("ctx", "head"),
        P("ctx", "head"),
        P("head", None),
    )
    out_specs = P(("groups", "ctx"), "head")
    return jax.shard_map(local, mesh=mesh, in_specs=in_specs, out_specs=out_specs, check_vma=False)
```
